32 devices in a mesh: seq: 4 (over x, core), dp: 8 (over z, y).
Axes of the slice: x: 2, y: 2, z: 4, core: 2. Of those that a mesh axis runs over, the one named last changes fastest.
Arguments:
- tokens: bfloat16 [8, 2048, 768], P('dp', 'seq'), may hold values from -6 to 6
- qkv_weight: bfloat16 [768, 2304], P('dp'), may hold values from -0.21875 to 0.21875
- out_weight: bfloat16 [768, 768], P('dp'), may hold values from -0.625 to 0.625
- up_weight: bfloat16 [768, 3072], P('dp'), may hold values from -0.21875 to 0.21875
- down_weight: bfloat16 [3072, 768], P('dp'), may hold values from -0.109375 to 0.109375
- norm_gain: bfloat16 [768], P('dp'), may hold values from 0.5 to 1.5
- mlp_gain: bfloat16 [768], P('dp'), may hold values from 0.5 to 1.5
- pass_embed: bfloat16 [768], P('dp'), may hold values from -6 to 6
- cotangent: bfloat16 [8, 2048, 768], P('dp', 'seq'), may hold values from -6 to 6
Outputs:
- mixed_out: bfloat16 [8, 2048, 768], P('dp', 'seq')
- input_grad: float32 [8, 2048, 768], P('dp', 'seq')
- qkv_grad: float32 [768, 2304], P('dp')
- output_grad: float32 [768, 768], P('dp')
- up_weight_grad: float32 [768, 3072], P('dp')
- down_weight_grad: float32 [3072, 768], P('dp')
- norm_gain_grad: float32 [768], P('dp')
- mlp_gain_grad: float32 [768], P('dp')
- embed_grad: float32 [768], P('dp')
The draws below stay inside these ranges and needn't reach their ends.
All inputs are finite; a program needn't handle non-finite values.
Results may differ from the reference program's by a relative error of at most 0.019.
Values may be sent and summed in bfloat16 or wider, within the bound.
A program may use at most 256 MiB of HBM per device.

```python
from functools import partial
import jax
import jax.numpy as jnp
from jax import lax

D = 768
FF = 3072
HEADS = 12
HEAD_DIM = 64
LENGTH = 2048
SEQS = 8


def level_of(key, dims, shards, low, high):
    factor_of = 1.0
    for axis_at, blocks in shards:
        steps = jax.random.uniform(jax.random.fold_in(jax.random.fold_in(key, 6), axis_at), (blocks,), jnp.float32, low / len(shards), high / len(shards))
        factor_of = factor_of * jnp.repeat(jnp.exp(steps), dims[axis_at] // blocks).reshape((-1,) + (1,) * (len(dims) - 1 - axis_at))
    return factor_of


def normal_values(own_key, dims, scale, limit, pieces=(), dtype=jnp.bfloat16):
    values = scale * jax.random.normal(own_key, dims, jnp.float32)
    if pieces:
        values = values * level_of(own_key, dims, pieces, -0.22, 0.18)
    return jnp.clip(values, -limit, limit).astype(dtype)


def setup_inputs(seed: int = 0) -> dict:
    splits = jax.random.split(jax.random.key(seed), 10)
    tokens = normal_values(splits[0], (SEQS, LENGTH, D), 1.0, 6.0, ((0, 8), (1, 4)))
    qkv_weight = normal_values(splits[1], (D, 3 * D), D ** -0.5, 0.21875, ((0, 8),))
    out_weight = normal_values(splits[2], (D, D), (D // 8) ** -0.5, 0.625, ((0, 8),))
    up_weight = normal_values(splits[3], (D, FF), D ** -0.5, 0.21875, ((0, 8),))
    down_weight = normal_values(splits[4], (FF, D), FF ** -0.5, 0.109375, ((0, 8),))
    norm_gain = jnp.clip(1.0 + 0.1 * jax.random.normal(splits[5], (D,), jnp.float32), 0.5, 1.5).astype(jnp.bfloat16)
    mlp_gain = jnp.clip(1.0 + 0.1 * jax.random.normal(splits[6], (D,), jnp.float32), 0.5, 1.5).astype(jnp.bfloat16)
    pass_embed = normal_values(splits[7], (D,), 1.0, 6.0, ((0, 8),))
    cotangent = normal_values(splits[8], (SEQS, LENGTH, D), 1.0, 6.0, ((0, 8), (1, 4)))
    return {"tokens": tokens, "qkv_weight": qkv_weight, "out_weight": out_weight, "up_weight": up_weight, "down_weight": down_weight, "norm_gain": norm_gain, "mlp_gain": mlp_gain, "pass_embed": pass_embed, "cotangent": cotangent}


@jax.custom_vjp
def low(v):
    return lax.optimization_barrier(v.astype(jnp.bfloat16)).astype(jnp.float32)

@jax.custom_vjp
def low_back(v):
    return v

def low_keep(v):
    return (low(v), None)

def low_pass(kept, grad):
    return (grad,)

def back_keep(v):
    return (v, None)

def back_low(kept, grad):
    return (low(grad),)
low.defvjp(low_keep, low_pass)
low_back.defvjp(back_keep, back_low)
epsilon = 1e-05
highest = lax.Precision.HIGHEST

def layer_norm(vector, gain_vec):
    centre = vector - lax.optimization_barrier(jnp.mean(vector, axis=-1, keepdims=True))
    spread = lax.optimization_barrier(jnp.mean(centre * centre, axis=-1, keepdims=True))
    return centre * lax.rsqrt(spread + epsilon) * gain_vec

def head_attention(queries, key_rows, value_rows, allowed):
    scores = low_back(jnp.dot(queries, key_rows.T, precision=highest) * HEAD_DIM ** (-0.5))
    scores = jnp.where(allowed, scores, -1e+30)
    row_max = lax.optimization_barrier(jnp.max(scores, axis=-1, keepdims=True))
    weights = jnp.exp(scores - row_max)
    chances = weights / lax.optimization_barrier(jnp.sum(weights, axis=-1, keepdims=True))
    return jnp.dot(low(chances), value_rows, precision=highest)

def block(stream, params, earlier):
    qkv_w, out_w, up_w, down_w, gain_a, gain_b = params
    normed = low(layer_norm(stream, gain_a))
    packed = low(low_back(jnp.dot(normed, qkv_w, precision=highest)))
    packed = packed.reshape(LENGTH, HEADS, 3, HEAD_DIM).transpose(2, 1, 0, 3)
    queries, key_rows, value_rows = (packed[0], packed[1], packed[2])
    causal = jnp.arange(LENGTH)[None, :] <= jnp.arange(LENGTH)[:, None]
    if earlier is None:
        all_keys, all_values, allowed = (key_rows, value_rows, causal)
    else:
        all_keys = jnp.concatenate([earlier[0], key_rows], axis=1)
        all_values = jnp.concatenate([earlier[1], value_rows], axis=1)
        allowed = jnp.concatenate([causal, causal], axis=1)

    def one_head(head_item):
        return head_attention(head_item[0], head_item[1], head_item[2], allowed)
    attended = lax.map(jax.checkpoint(one_head), (queries, all_keys, all_values))
    mixed = low(low_back(attended.transpose(1, 0, 2).reshape(LENGTH, D)))
    middle = stream + low_back(jnp.dot(mixed, out_w, precision=highest))
    normed_b = low(layer_norm(middle, gain_b))
    hidden = low_back(jnp.dot(normed_b, up_w, precision=highest))
    active = low(jax.nn.gelu(hidden, approximate=True))
    result = middle + low_back(jnp.dot(active, down_w, precision=highest))
    return (result, key_rows, value_rows)

def one_sequence(stream, params):
    first_out, key_rows, value_rows = block(stream, params[:6], None)
    second_out, unused_keys, unused_values = block(first_out + params[6], params[:6], (key_rows, value_rows))
    return second_out

def reference(tokens, qkv_weight, out_weight, up_weight, down_weight, norm_gain, mlp_gain, pass_embed, cotangent):
    params = (qkv_weight.astype(jnp.float32), out_weight.astype(jnp.float32), up_weight.astype(jnp.float32), down_weight.astype(jnp.float32), norm_gain.astype(jnp.float32), mlp_gain.astype(jnp.float32), pass_embed.astype(jnp.float32))

    def forward(start, weights):
        return lax.map(jax.checkpoint(partial(one_sequence, params=weights)), start)
    result, pullback = jax.vjp(forward, tokens.astype(jnp.float32), params)
    start_grad, weight_grads = pullback(cotangent.astype(jnp.float32))
    return (result.astype(jnp.bfloat16), start_grad, weight_grads[0], weight_grads[1], weight_grads[2], weight_grads[3], weight_grads[4], weight_grads[5], weight_grads[6])
```

```python
import functools

import jax
import jax.numpy as jnp
from jax import lax
from jax.experimental import pallas as pl
from jax.experimental.pallas import tpu as pltpu
from jax.sharding import PartitionSpec as P

HEAD_DIM = 64


epsilon = 1e-05


def layer_norm(vector, gain_vec):
    centre = vector - jnp.mean(vector, axis=-1, keepdims=True)
    spread = jnp.mean(centre * centre, axis=-1, keepdims=True)
    return centre * lax.rsqrt(spread + epsilon) * gain_vec


def gelu_value(vector):
    return jax.nn.gelu(vector, approximate=True)


def contract_rows(left_side, right_side):
    return lax.dot_general(
        left_side, right_side, (((0,), (0,)), ((), ())), preferred_element_type=jnp.float32
    )


def contract_cols(left_side, right_side):
    return lax.dot_general(
        left_side, right_side, (((1,), (1,)), ((), ())), preferred_element_type=jnp.float32
    )


HD = 64
NEG = -1e30

def nt(a, b):
    return lax.dot_general(a, b, (((1,), (1,)), ((), ())), preferred_element_type=jnp.float32)

def nn(a, b):
    return lax.dot_general(a, b, (((1,), (0,)), ((), ())), preferred_element_type=jnp.float32)

def fwd_kernel(nsets, heads, bq, bk, *refs):
    qkv = refs[:nsets]
    o_ref, lse_ref = refs[nsets:nsets + 2]
    q_s, k_s, vt_s = refs[nsets + 2:]
    length = o_ref.shape[0]
    own = qkv[-1]
    for h in range(heads):
        c0 = 3 * HD * h
        q_s[...] = own[:, c0:c0 + HD] * jnp.bfloat16(HD ** -0.5)
        for s in range(nsets):
            k_s[s] = qkv[s][:, c0 + HD:c0 + 2 * HD]
            vt_s[s, :HD] = qkv[s][:, c0 + 2 * HD:c0 + 3 * HD].T
            vt_s[s, HD:] = jnp.ones((16, length), jnp.bfloat16)

        def q_block(i, _):
            q0 = pl.multiple_of(i * bq, bq)
            q = q_s[pl.ds(q0, bq), :]
            per = bq // bk

            def step(blocks, carry):
                m, acc = carry
                ss = []
                for (s, k0, mask) in blocks:
                    st = nt(k_s[s, pl.ds(k0, bk), :], q)
                    if mask is not None:
                        st = jnp.where(mask, st, NEG)
                    ss.append(st)
                m_new = m
                for st in ss:
                    m_new = jnp.maximum(m_new, jnp.max(st, axis=0, keepdims=True))
                acc = acc * jnp.exp(m - m_new)
                for (s, k0, _), st in zip(blocks, ss):
                    p = jnp.exp(st - m_new).astype(jnp.bfloat16)
                    acc = acc + nn(vt_s[s, :, pl.ds(k0, bk)], p)
                return m_new, acc

            carry = (jnp.full((1, bq), NEG, jnp.float32), jnp.zeros((HD + 16, bq), jnp.float32))
            for t in range(per):
                row = lax.broadcasted_iota(jnp.int32, (bk, bq), 0) + t * bk
                col = lax.broadcasted_iota(jnp.int32, (bk, bq), 1)
                mask = row <= col
                carry = step([(s, pl.multiple_of(q0 + t * bk, bk), mask) for s in range(nsets)], carry)

            def body(j, carry):
                return step([(s, pl.multiple_of(j * bk, bk), None) for s in range(nsets)], carry)
            m, acc = lax.fori_loop(0, i * per, body, carry)
            l = acc[HD:HD + 1]
            ot = acc[:HD] / l
            o_ref[pl.ds(q0, bq), HD * h:HD * h + HD] = ot.T.astype(jnp.bfloat16)
            lse_ref[h, :, pl.ds(q0, bq)] = m + jnp.log(l)
            return 0
        lax.fori_loop(0, length // bq, q_block, 0)

def attn_fwd(packs, bq=512, bk=512):
    nsets = len(packs)
    length, cols = packs[0].shape
    heads = cols // (3 * HD)
    return pl.pallas_call(
        functools.partial(fwd_kernel, nsets, heads, bq, bk),
        out_shape=(jax.ShapeDtypeStruct((length, heads * HD), jnp.bfloat16),
                   jax.ShapeDtypeStruct((heads, 1, length), jnp.float32)),
        in_specs=[pl.BlockSpec(memory_space=pltpu.VMEM)] * nsets,
        out_specs=(pl.BlockSpec(memory_space=pltpu.VMEM),) * 2,
        scratch_shapes=[pltpu.VMEM((length, HD), jnp.bfloat16),
                        pltpu.VMEM((nsets, length, HD), jnp.bfloat16),
                        pltpu.VMEM((nsets, HD + 16, length), jnp.bfloat16)],
        compiler_params=pltpu.CompilerParams(vmem_limit_bytes=56 << 20),
        name=f"attn_fwd{nsets}",
    )(*packs)

def bwd_kernel(nsets, heads, bq, bk, has_add, *refs):
    it = iter(refs)
    qkv = [next(it) for _ in range(nsets)]
    do_ref, o_ref, lse_ref = next(it), next(it), next(it)
    add_ref = next(it) if has_add else None
    dqkv_ref = next(it)
    dprev_ref = next(it) if nsets == 2 else None
    q_s, k_s, kt_s, v_s, doz_s, qz_s, do_s, delta_s, dqt_s, dkv_s = it
    own = qkv[-1]
    length = do_ref.shape[0]
    nq, nk = length // bq, length // bk
    scale = jnp.bfloat16(HD ** -0.5)
    for h in range(heads):
        c0 = 3 * HD * h
        q = own[:, c0:c0 + HD]
        q_s[...] = q * scale
        do = do_ref[:, HD * h:HD * h + HD]
        do_s[...] = do
        zero = jnp.zeros((length, HD), jnp.bfloat16)
        qz_s[:, :HD] = q * scale
        qz_s[:, HD:] = zero
        doz_s[:, :HD] = zero
        doz_s[:, HD:] = do
        prod = do.astype(jnp.float32) * o_ref[:, HD * h:HD * h + HD].astype(jnp.float32)
        delta_s[...] = jnp.sum(prod.T, axis=0, keepdims=True)
        for s in range(nsets):
            k = qkv[s][:, c0 + HD:c0 + 2 * HD]
            k_s[s] = k
            kt_s[s] = (k * scale).T
            v_s[s] = qkv[s][:, c0 + 2 * HD:c0 + 3 * HD]
        dqt_s[...] = jnp.zeros_like(dqt_s)
        if has_add:
            dkv_s[0] = add_ref[h]
        else:
            for s in range(nsets):
                dkv_s[s] = jnp.zeros_like(dkv_s[s])

        def block(i, j, mask):
            q0 = pl.multiple_of(i * bq, bq)
            k0 = pl.multiple_of(j * bk, bk)
            qb = q_s[pl.ds(q0, bq), :]
            dob = do_s[pl.ds(q0, bq), :]
            lse = lse_ref[h, :, pl.ds(q0, bq)]
            delta = delta_s[:, pl.ds(q0, bq)]
            dq = None
            for s in range(nsets):
                st = nt(k_s[s, pl.ds(k0, bk), :], qb)
                p = jnp.exp(st - lse)
                if mask is not None:
                    p = jnp.where(mask, p, 0.0)
                dpt = nt(v_s[s, pl.ds(k0, bk), :], dob)
                ds = (p * (dpt - delta)).astype(jnp.bfloat16)
                pb = p.astype(jnp.bfloat16)
                dkv_s[s, pl.ds(k0, bk), :] += nn(pb, doz_s[pl.ds(q0, bq), :]) + nn(ds, qz_s[pl.ds(q0, bq), :])
                t = nn(kt_s[s, :, pl.ds(k0, bk)], ds)
                dq = t if dq is None else dq + t
            dqt_s[:, pl.ds(q0, bq)] += dq

        per = bq // bk
        def q_loop(i, _):
            for t in range(per):
                row = lax.broadcasted_iota(jnp.int32, (bk, bq), 0) + t * bk
                col = lax.broadcasted_iota(jnp.int32, (bk, bq), 1)
                block(i, i * per + t, row <= col)
            def k_loop(j, _):
                block(i, j, None)
                return 0
            lax.fori_loop(0, i * per, k_loop, 0)
            return 0
        lax.fori_loop(0, nq, q_loop, 0)
        dqkv_ref[:, c0:c0 + HD] = dqt_s[...].T.astype(jnp.bfloat16)
        dqkv_ref[:, c0 + HD:c0 + 3 * HD] = dkv_s[nsets - 1].astype(jnp.bfloat16)
        if nsets == 2:
            dprev_ref[h] = dkv_s[0]

def attn_bwd(packs, do, o, lse, add=None, bq=512, bk=512):
    nsets = len(packs)
    length, cols = packs[0].shape
    heads = cols // (3 * HD)
    outs = [jax.ShapeDtypeStruct((length, cols), jnp.bfloat16)]
    if nsets == 2:
        outs.append(jax.ShapeDtypeStruct((heads, length, 2 * HD), jnp.float32))
    args = list(packs) + [do, o, lse] + ([add] if add is not None else [])
    b = jnp.bfloat16
    return pl.pallas_call(
        functools.partial(bwd_kernel, nsets, heads, bq, bk, add is not None),
        out_shape=tuple(outs),
        in_specs=[pl.BlockSpec(memory_space=pltpu.VMEM)] * len(args),
        out_specs=(pl.BlockSpec(memory_space=pltpu.VMEM),) * len(outs),
        scratch_shapes=[pltpu.VMEM((length, HD), b),
                        pltpu.VMEM((nsets, length, HD), b),
                        pltpu.VMEM((nsets, HD, length), b),
                        pltpu.VMEM((nsets, length, HD), b),
                        pltpu.VMEM((length, 2 * HD), b),
                        pltpu.VMEM((length, 2 * HD), b),
                        pltpu.VMEM((length, HD), b),
                        pltpu.VMEM((1, length), jnp.float32),
                        pltpu.VMEM((HD, length), jnp.float32),
                        pltpu.VMEM((nsets, length, 2 * HD), jnp.float32)],
        compiler_params=pltpu.CompilerParams(vmem_limit_bytes=56 << 20),
        name=f"attn_bwd{nsets}",
    )(*args)


def block_forward(stream, weights, earlier):
    qkv_w, out_w, up_w, down_w, gain_a, gain_b = weights
    normed = layer_norm(stream, gain_a).astype(jnp.bfloat16)
    packed = jnp.dot(normed, qkv_w, preferred_element_type=jnp.float32).astype(jnp.bfloat16)
    heads = lax.all_to_all(packed, "seq", split_axis=1, concat_axis=0, tiled=True)
    packs = [heads] if earlier is None else [earlier, heads]
    mixed, totals = attn_fwd(packs)
    mixed_rows = lax.all_to_all(mixed, "seq", split_axis=0, concat_axis=1, tiled=True)
    middle = stream + jnp.dot(mixed_rows, out_w, preferred_element_type=jnp.float32)
    normed_b = layer_norm(middle, gain_b).astype(jnp.bfloat16)
    hidden = jnp.dot(normed_b, up_w, preferred_element_type=jnp.float32)
    active = gelu_value(hidden).astype(jnp.bfloat16)
    result = middle + jnp.dot(active, down_w, preferred_element_type=jnp.float32)
    stored = (
        stream,
        normed,
        packs,
        mixed,
        totals,
        mixed_rows,
        middle,
        normed_b,
        hidden,
        active,
    )
    return (result, stored, heads)


def block_backward(upstream, stored, weights, carried):
    qkv_w, out_w, up_w, down_w, gain_a, gain_b = weights
    (
        stream,
        normed,
        packs,
        mixed,
        totals,
        mixed_rows,
        middle,
        normed_b,
        hidden,
        active,
    ) = stored
    out_bf = upstream.astype(jnp.bfloat16)
    down_grad = contract_rows(active, out_bf)
    d_active = contract_cols(out_bf, down_w)
    d_hidden = jax.vjp(gelu_value, hidden)[1](d_active)[0].astype(jnp.bfloat16)
    up_grad = contract_rows(normed_b, d_hidden)
    d_normed_b = contract_cols(d_hidden, up_w)
    d_middle_norm, gain_b_grad = jax.vjp(layer_norm, middle, gain_b)[1](d_normed_b)
    d_middle = upstream + d_middle_norm
    middle_bf = d_middle.astype(jnp.bfloat16)
    out_grad = contract_rows(mixed_rows, middle_bf)
    d_mixed = contract_cols(middle_bf, out_w).astype(jnp.bfloat16)
    d_heads = lax.all_to_all(d_mixed, "seq", split_axis=1, concat_axis=0, tiled=True)
    outs = attn_bwd(packs, d_heads, mixed, totals, carried)
    d_packed = outs[0]
    passed = outs[1] if len(outs) > 1 else None
    d_rows = lax.all_to_all(d_packed, "seq", split_axis=0, concat_axis=1, tiled=True)
    qkv_grad = contract_rows(normed, d_rows)
    d_normed = contract_cols(d_rows, qkv_w)
    d_stream_norm, gain_a_grad = jax.vjp(layer_norm, stream, gain_a)[1](d_normed)
    grads = (qkv_grad, out_grad, up_grad, down_grad, gain_a_grad, gain_b_grad)
    return (d_middle + d_stream_norm, grads, passed)


def local(
    tokens,
    qkv_weight,
    out_weight,
    up_weight,
    down_weight,
    norm_gain,
    mlp_gain,
    pass_embed,
    cotangent,
):
    gathered = (
        lax.all_gather(qkv_weight, "dp", axis=0, tiled=True),
        lax.all_gather(out_weight, "dp", axis=0, tiled=True),
        lax.all_gather(up_weight, "dp", axis=0, tiled=True),
        lax.all_gather(down_weight, "dp", axis=0, tiled=True),
        lax.all_gather(norm_gain, "dp", axis=0, tiled=True),
        lax.all_gather(mlp_gain, "dp", axis=0, tiled=True),
        lax.all_gather(pass_embed, "dp", axis=0, tiled=True),
    )
    weights = (
        gathered[0],
        gathered[1],
        gathered[2],
        gathered[3],
        gathered[4].astype(jnp.float32),
        gathered[5].astype(jnp.float32),
    )
    embedding = gathered[6].astype(jnp.float32)
    first_out, first_kept, first_keys = block_forward(tokens[0].astype(jnp.float32), weights, None)
    second_out, second_kept, unused_keys = block_forward(first_out + embedding, weights, first_keys)
    d_second, second_grads, passed = block_backward(
        cotangent[0].astype(jnp.float32), second_kept, weights, None
    )
    embed_grad = jnp.sum(d_second, axis=0)
    d_first, first_grads, unused = block_backward(d_second, first_kept, weights, passed)
    summed = jax.tree.map(jnp.add, first_grads, second_grads) + (embed_grad,)
    shards = (
        lax.psum_scatter(
            summed[0].astype(jnp.bfloat16), "dp", scatter_dimension=0, tiled=True
        ).astype(jnp.float32),
        lax.psum_scatter(
            summed[1].astype(jnp.bfloat16), "dp", scatter_dimension=0, tiled=True
        ).astype(jnp.float32),
        lax.psum_scatter(
            summed[2].astype(jnp.bfloat16), "dp", scatter_dimension=0, tiled=True
        ).astype(jnp.float32),
        lax.psum_scatter(
            summed[3].astype(jnp.bfloat16), "dp", scatter_dimension=0, tiled=True
        ).astype(jnp.float32),
        lax.psum_scatter(
            summed[4].astype(jnp.bfloat16), "dp", scatter_dimension=0, tiled=True
        ).astype(jnp.float32),
        lax.psum_scatter(
            summed[5].astype(jnp.bfloat16), "dp", scatter_dimension=0, tiled=True
        ).astype(jnp.float32),
        lax.psum_scatter(
            summed[6].astype(jnp.bfloat16), "dp", scatter_dimension=0, tiled=True
        ).astype(jnp.float32),
    )
    final = (
        lax.psum(shards[0].astype(jnp.bfloat16), "seq").astype(jnp.float32),
        lax.psum(shards[1].astype(jnp.bfloat16), "seq").astype(jnp.float32),
        lax.psum(shards[2].astype(jnp.bfloat16), "seq").astype(jnp.float32),
        lax.psum(shards[3].astype(jnp.bfloat16), "seq").astype(jnp.float32),
        lax.psum(shards[4].astype(jnp.bfloat16), "seq").astype(jnp.float32),
        lax.psum(shards[5].astype(jnp.bfloat16), "seq").astype(jnp.float32),
        lax.psum(shards[6].astype(jnp.bfloat16), "seq").astype(jnp.float32),
    )
    return (
        second_out.astype(jnp.bfloat16)[None],
        d_first[None],
        final[0],
        final[1],
        final[2],
        final[3],
        final[4],
        final[5],
        final[6],
    )


def solution(mesh):
    in_specs = (
        P("dp", "seq", None),
        P("dp", None),
        P("dp", None),
        P("dp", None),
        P("dp", None),
        P("dp"),
        P("dp"),
        P("dp"),
        P("dp", "seq", None),
    )
    out_specs = (
        P("dp", "seq", None),
        P("dp", "seq", None),
        P("dp", None),
        P("dp", None),
        P("dp", None),
        P("dp", None),
        P("dp"),
        P("dp"),
        P("dp"),
    )
    return jax.shard_map(local, mesh=mesh, in_specs=in_specs, out_specs=out_specs, check_vma=False)
```

```python
import functools

import jax
import jax.numpy as jnp
from jax import lax
from jax.experimental import pallas as pl
from jax.experimental.pallas import tpu as pltpu
from jax.sharding import PartitionSpec as P

HEAD_DIM = 64


epsilon = 1e-05


def layer_norm(vector, gain_vec):
    centre = vector - jnp.mean(vector, axis=-1, keepdims=True)
    spread = jnp.mean(centre * centre, axis=-1, keepdims=True)
    return centre * lax.rsqrt(spread + epsilon) * gain_vec


def gelu_value(vector):
    return jax.nn.gelu(vector, approximate=True)


def contract_rows(left_side, right_side):
    return lax.dot_general(
        left_side, right_side, (((0,), (0,)), ((), ())), preferred_element_type=jnp.float32
    )


def contract_cols(left_side, right_side):
    return lax.dot_general(
        left_side, right_side, (((1,), (1,)), ((), ())), preferred_element_type=jnp.float32
    )


def nt(left, right):
    return lax.dot_general(
        left, right, (((1,), (1,)), ((), ())), preferred_element_type=jnp.float32
    )


def nn(left, right):
    return lax.dot_general(
        left, right, (((1,), (0,)), ((), ())), preferred_element_type=jnp.float32
    )


def remote(src, dst, send_sem, recv_sem, device):
    return pltpu.make_async_remote_copy(
        src_ref=src,
        dst_ref=dst,
        send_sem=send_sem,
        recv_sem=recv_sem,
        device_id=device,
        device_id_type=pl.DeviceIdType.MESH,
    )


def greet(devices):
    barrier = pltpu.get_barrier_semaphore()
    for device in devices:
        pl.semaphore_signal(
            barrier, inc=1, device_id=device, device_id_type=pl.DeviceIdType.MESH
        )
    pl.semaphore_wait(barrier, len(devices))


def seq_peers(seq):
    me = lax.axis_index("seq")
    return [lax.rem(me + d, seq) for d in range(1, seq)]


class Gather:
    def __init__(self, seq, dp, shards, wholes, sems):
        self.line = dp // 2
        self.shards, self.wholes = shards, wholes
        self.z_send, self.z_recv, self.y_send, self.y_recv, self.c_send, self.c_recv, self.own = sems
        me = lax.axis_index("seq")
        self.core = lax.rem(me, 2)
        self.core_peer = {"seq": me + 1 - 2 * self.core}
        self.rank = lax.axis_index("dp")
        self.a, self.b = lax.div(self.rank, 2), lax.rem(self.rank, 2)
        self.y_peer = {"dp": self.a * 2 + 1 - self.b}
        self.sent = []

    @staticmethod
    def sems(units, dp):
        line = dp // 2
        dma = pltpu.SemaphoreType.DMA
        return [
            dma((units, line)),
            dma((units, line)),
            dma((units, line)),
            dma((units, line)),
            dma((units, 2 * line)),
            dma((units, 2 * line)),
            dma((units,)),
        ]

    def z_rank(self, offset):
        return lax.rem(self.a + offset, self.line) * 2 + self.b

    def peers(self):
        z = [{"dp": self.z_rank(d)} for d in range(1, self.line)]
        return z + [self.y_peer]

    def place(self, unit, rank):
        rows, columns = self.shards[unit].shape
        half = columns // 2
        return (
            pl.ds(pl.multiple_of(rank * rows, 8), rows),
            pl.ds(pl.multiple_of(self.core * half, 128), half),
        )

    def send(self, src, dst, send_sem, recv_sem, device):
        copy = remote(src, dst, send_sem, recv_sem, device)
        copy.start()
        self.sent.append(copy)
        return copy

    def start(self, unit):
        shard, whole = self.shards[unit], self.wholes[unit]
        where = self.place(unit, self.rank)
        mine = shard.at[:, where[1]]
        self.z_copies = getattr(self, "z_copies", {})
        self.y_copies = getattr(self, "y_copies", {})
        self.c_copies = getattr(self, "c_copies", {})
        for d in range(1, self.line):
            self.z_copies[unit, d] = self.send(
                mine,
                whole.at[where],
                self.z_send.at[unit, d],
                self.z_recv.at[unit, d],
                {"dp": self.z_rank(d)},
            )
        self.y_copies[unit, 0] = self.send(
            mine, whole.at[where], self.y_send.at[unit, 0], self.y_recv.at[unit, 0], self.y_peer
        )
        local_copy = pltpu.make_async_copy(
            shard, whole.at[where[0]], self.own.at[unit]
        )
        local_copy.start()
        self.c_copies[unit, 0] = local_copy

    def to_core(self, unit, slot, rank):
        block = self.wholes[unit].at[self.place(unit, rank)]
        self.c_copies[unit, slot] = self.send(
            block, block, self.c_send.at[unit, slot], self.c_recv.at[unit, slot], self.core_peer
        )

    def forward_z(self, unit):
        for d in range(1, self.line):
            self.z_copies[unit, d].wait_recv()
            rank = self.z_rank(self.line - d)
            block = self.wholes[unit].at[self.place(unit, rank)]
            self.y_copies[unit, d] = self.send(
                block, block, self.y_send.at[unit, d], self.y_recv.at[unit, d], self.y_peer
            )
            self.to_core(unit, d, rank)

    def forward_y(self, unit):
        for d in range(self.line):
            self.y_copies[unit, d].wait_recv()
            rank = lax.rem(self.a + self.line - d, self.line) * 2 + 1 - self.b
            self.to_core(unit, self.line + d, rank)

    def finish(self, unit):
        for slot in range(1, 2 * self.line):
            self.c_copies[unit, slot].wait_recv()
        self.c_copies[unit, 0].wait()

    def drain(self):
        for copy in self.sent:
            copy.wait_send()


def gather_kernel(seq, dp, units, *refs):
    shards, wholes, sems = refs[:units], refs[units : 2 * units], refs[2 * units :]
    gather = Gather(seq, dp, shards, wholes, sems)
    greet(gather.peers() + [gather.core_peer])
    for unit in range(units):
        gather.start(unit)
    for unit in range(units):
        gather.forward_z(unit)
    for unit in range(units):
        gather.forward_y(unit)
    for unit in range(units):
        gather.finish(unit)
    gather.drain()


def whole_shape(shard, dp):
    return jax.ShapeDtypeStruct((shard.shape[0] * dp, shard.shape[1]), shard.dtype)


def gather_now(seq, dp, shards):
    units = len(shards)
    hbm = pl.BlockSpec(memory_space=pl.ANY)
    return pl.pallas_call(
        functools.partial(gather_kernel, seq, dp, units),
        out_shape=tuple(whole_shape(shard, dp) for shard in shards),
        in_specs=[hbm] * units,
        out_specs=(hbm,) * units,
        scratch_shapes=Gather.sems(units, dp),
        compiler_params=pltpu.CompilerParams(
            collective_id=0, has_side_effects=True, vmem_limit_bytes=4 << 20
        ),
        name="gather_first",
    )(*shards)


def causal_mask(size):
    rows = lax.broadcasted_iota(jnp.int32, (size, size), 0)
    columns = lax.broadcasted_iota(jnp.int32, (size, size), 1)
    return rows <= columns


def forward_kernel(seq, dp, sets, units, heads, *refs):
    refs = list(refs)

    def take(count):
        taken = refs[:count]
        del refs[:count]
        return taken

    (packed,) = take(1)
    earlier = take(sets - 1)
    shards = take(units)
    heads_out, mixed_out, own_out, totals_out = take(4)
    wholes = take(units)
    arrived, mixed_in, q_s, k_s, v_s, in_send, in_recv, out_send, out_recv = take(9)
    gather = Gather(seq, dp, shards, wholes, refs) if units else None

    tokens = packed.shape[1]
    length = tokens * seq
    group = 3 * HEAD_DIM
    me = lax.axis_index("seq")
    peers = seq_peers(seq)
    greet([{"seq": peer} for peer in peers] + (gather.peers() if units else []))

    own_lanes = pl.ds(pl.multiple_of(me * tokens, tokens), tokens)
    copies = {}
    for h in range(heads):
        for d, peer in enumerate(peers):
            copy = remote(
                packed.at[pl.ds(pl.multiple_of((peer * heads + h) * group, group), group)],
                arrived.at[pl.ds(h * group, group), own_lanes],
                in_send.at[h, d],
                in_recv.at[h, d],
                {"seq": peer},
            )
            copy.start()
            copies[h, d] = copy
    for unit in range(units):
        gather.start(unit)
    for h in range(heads):
        arrived[h * group : (h + 1) * group, own_lanes] = packed[
            pl.ds(pl.multiple_of((me * heads + h) * group, group), group), :
        ]

    mask = causal_mask(tokens)
    for s in range(sets):
        v_s[s, HEAD_DIM:] = jnp.ones((16, length), jnp.bfloat16)
    results = []
    for h in range(heads):
        c0 = h * group
        for s in range(sets):
            source = earlier[s] if s < sets - 1 else arrived
            if s == sets - 1:
                for d in range(seq - 1):
                    copies[h, d].wait_recv()
                heads_out[c0 : c0 + group, :] = arrived[c0 : c0 + group, :]
                q_s[...] = arrived[c0 : c0 + HEAD_DIM, :] * jnp.bfloat16(HEAD_DIM**-0.5)
            k_s[s] = source[c0 + HEAD_DIM : c0 + 2 * HEAD_DIM, :].T
            v_s[s, :HEAD_DIM] = source[c0 + 2 * HEAD_DIM : c0 + 3 * HEAD_DIM, :]

        for i in range(seq):
            queries = q_s[:, i * tokens : (i + 1) * tokens]
            peak = total = None
            for j in [i] + list(range(i)):
                keys = slice(j * tokens, (j + 1) * tokens)
                scores = []
                for s in range(sets):
                    block = nn(k_s[s, keys, :], queries)
                    if j == i:
                        block = jnp.where(mask, block, -1e30)
                    scores.append(block)
                peak_now = peak
                for block in scores:
                    top = jnp.max(block, axis=0, keepdims=True)
                    peak_now = top if peak_now is None else jnp.maximum(peak_now, top)
                if total is not None:
                    total = total * jnp.exp(peak - peak_now)
                for s, block in enumerate(scores):
                    weights = jnp.exp(block - peak_now).astype(jnp.bfloat16)
                    part = nn(v_s[s, :, keys], weights)
                    total = part if total is None else total + part
                peak = peak_now
            row_sum = total[HEAD_DIM : HEAD_DIM + 1]
            own_out[h * HEAD_DIM : (h + 1) * HEAD_DIM, i * tokens : (i + 1) * tokens] = (
                total[:HEAD_DIM] / row_sum
            ).astype(jnp.bfloat16)
            totals_out[h, :, i * tokens : (i + 1) * tokens] = peak + jnp.log(row_sum)

        mine = pl.ds(pl.multiple_of((me * heads + h) * HEAD_DIM, HEAD_DIM), HEAD_DIM)
        for d, peer in enumerate(peers):
            copy = remote(
                own_out.at[
                    pl.ds(h * HEAD_DIM, HEAD_DIM),
                    pl.ds(pl.multiple_of(peer * tokens, tokens), tokens),
                ],
                mixed_in.at[mine],
                out_send.at[h, d],
                out_recv.at[h, d],
                {"seq": peer},
            )
            copy.start()
            results.append(copy)
        mixed_in[mine] = own_out[h * HEAD_DIM : (h + 1) * HEAD_DIM, own_lanes]
        if units:
            if h == 0:
                gather.forward_z(0)
            elif h == 1:
                gather.forward_y(0)
                gather.forward_z(1)
    if units:
        gather.forward_z(2)
        gather.forward_y(1)
        gather.forward_y(2)
        for unit in range(units):
            gather.finish(unit)
        gather.drain()
    for copy in copies.values():
        copy.wait_send()
    for copy in results:
        copy.wait()
    mixed_out[...] = mixed_in[...]


def attend_forward(seq, dp, heads, packed, earlier, shards, call_id):
    width, tokens = packed.shape
    length = tokens * seq
    sets, units = 1 + len(earlier), len(shards)
    rows = heads * 3 * HEAD_DIM
    vmem = pl.BlockSpec(memory_space=pltpu.VMEM)
    hbm = pl.BlockSpec(memory_space=pl.ANY)
    dma = pltpu.SemaphoreType.DMA
    outs = pl.pallas_call(
        functools.partial(forward_kernel, seq, dp, sets, units, heads),
        out_shape=(
            jax.ShapeDtypeStruct((rows, length), jnp.bfloat16),
            jax.ShapeDtypeStruct((width // 3, tokens), jnp.bfloat16),
            jax.ShapeDtypeStruct((heads * HEAD_DIM, length), jnp.bfloat16),
            jax.ShapeDtypeStruct((heads, 1, length), jnp.float32),
        )
        + tuple(whole_shape(shard, dp) for shard in shards),
        in_specs=[vmem] * sets + [hbm] * units,
        out_specs=(vmem,) * 4 + (hbm,) * units,
        scratch_shapes=[
            pltpu.VMEM((rows, length), jnp.bfloat16),
            pltpu.VMEM((width // 3, tokens), jnp.bfloat16),
            pltpu.VMEM((HEAD_DIM, length), jnp.bfloat16),
            pltpu.VMEM((sets, length, HEAD_DIM), jnp.bfloat16),
            pltpu.VMEM((sets, HEAD_DIM + 16, length), jnp.bfloat16),
            dma((heads, seq)),
            dma((heads, seq)),
            dma((heads, seq)),
            dma((heads, seq)),
        ]
        + (Gather.sems(units, dp) if units else []),
        compiler_params=pltpu.CompilerParams(
            collective_id=call_id, has_side_effects=True, vmem_limit_bytes=40 << 20
        ),
        name=f"attend_forward_{sets}",
    )(packed, *earlier, *shards)
    return outs[:4], outs[4:]


def backward_kernel(seq, sets, carried, heads, *refs):
    refs = list(refs)

    def take(count):
        taken = refs[:count]
        del refs[:count]
        return taken

    (d_mixed,) = take(1)
    packs = take(sets)
    own_in, totals_in = take(2)
    carry_in = take(1)[0] if carried else None
    (d_packed_out,) = take(1)
    carry_out = take(1)[0] if sets == 2 else None
    arrived, local_grad, d_packed_in, q_s, k_s, kt_s, v_s, delta_s, dq_s, dkv_s = take(10)
    in_send, in_recv, out_send, out_recv = refs

    tokens = d_mixed.shape[1]
    length = tokens * seq
    group = 3 * HEAD_DIM
    me = lax.axis_index("seq")
    peers = seq_peers(seq)
    greet([{"seq": peer} for peer in peers])
    own_lanes = pl.ds(pl.multiple_of(me * tokens, tokens), tokens)
    scale = jnp.bfloat16(HEAD_DIM**-0.5)

    copies = {}
    for h in range(heads):
        for d, peer in enumerate(peers):
            copy = remote(
                d_mixed.at[pl.ds(pl.multiple_of((peer * heads + h) * HEAD_DIM, HEAD_DIM), HEAD_DIM)],
                arrived.at[pl.ds(h * HEAD_DIM, HEAD_DIM), own_lanes],
                in_send.at[h, d],
                in_recv.at[h, d],
                {"seq": peer},
            )
            copy.start()
            copies[h, d] = copy
    for h in range(heads):
        arrived[h * HEAD_DIM : (h + 1) * HEAD_DIM, own_lanes] = d_mixed[
            pl.ds(pl.multiple_of((me * heads + h) * HEAD_DIM, HEAD_DIM), HEAD_DIM), :
        ]

    mask = causal_mask(tokens)
    results = []
    for h in range(heads):
        c0 = h * group
        r0 = h * HEAD_DIM
        q_s[...] = packs[-1][c0 : c0 + HEAD_DIM, :] * scale
        for s in range(sets):
            keys = packs[s][c0 + HEAD_DIM : c0 + 2 * HEAD_DIM, :]
            k_s[s] = keys.T
            kt_s[s] = keys * scale
            v_s[s] = packs[s][c0 + 2 * HEAD_DIM : c0 + 3 * HEAD_DIM, :].T
        for d in range(seq - 1):
            copies[h, d].wait_recv()
        delta_s[...] = jnp.sum(
            arrived[r0 : r0 + HEAD_DIM, :].astype(jnp.float32)
            * own_in[r0 : r0 + HEAD_DIM, :].astype(jnp.float32),
            axis=0,
            keepdims=True,
        )
        for j in range(seq):
            keys = slice(j * tokens, (j + 1) * tokens)
            for i in range(j, seq):
                span = slice(i * tokens, (i + 1) * tokens)
                queries = q_s[:, span]
                grads = arrived[r0 : r0 + HEAD_DIM, span]
                d_query = dq_s[:, span] if j > 0 else None
                for s in range(sets):
                    chances = jnp.exp(nn(k_s[s, keys, :], queries) - totals_in[h, :, span])
                    if i == j:
                        chances = jnp.where(mask, chances, 0.0)
                    d_chance = nn(v_s[s, keys, :], grads)
                    d_score = (chances * (d_chance - delta_s[:, span])).astype(jnp.bfloat16)
                    d_key = nt(queries, d_score)
                    d_value = nt(grads, chances.astype(jnp.bfloat16))
                    if i == j:
                        if carried:
                            d_key = d_key + carry_in[h, :HEAD_DIM, keys]
                            d_value = d_value + carry_in[h, HEAD_DIM:, keys]
                        dkv_s[s, :HEAD_DIM, keys] = d_key
                        dkv_s[s, HEAD_DIM:, keys] = d_value
                    else:
                        dkv_s[s, :HEAD_DIM, keys] += d_key
                        dkv_s[s, HEAD_DIM:, keys] += d_value
                    part = nn(kt_s[s, :, keys], d_score)
                    d_query = part if d_query is None else d_query + part
                dq_s[:, span] = d_query
            local_grad[c0 : c0 + HEAD_DIM, keys] = dq_s[:, keys].astype(jnp.bfloat16)
            local_grad[c0 + HEAD_DIM : c0 + group, keys] = dkv_s[sets - 1, :, keys].astype(
                jnp.bfloat16
            )
        if sets == 2:
            carry_out[h] = dkv_s[0]
        mine = pl.ds(pl.multiple_of((me * heads + h) * group, group), group)
        for d, peer in enumerate(peers):
            copy = remote(
                local_grad.at[
                    pl.ds(c0, group), pl.ds(pl.multiple_of(peer * tokens, tokens), tokens)
                ],
                d_packed_in.at[mine],
                out_send.at[h, d],
                out_recv.at[h, d],
                {"seq": peer},
            )
            copy.start()
            results.append(copy)
        d_packed_in[mine] = local_grad[c0 : c0 + group, own_lanes]
    for copy in copies.values():
        copy.wait_send()
    for copy in results:
        copy.wait()
    d_packed_out[...] = d_packed_in[...]


def attend_backward(seq, heads, d_mixed, packs, own, totals, carried, call_id):
    width, tokens = d_mixed.shape
    length = tokens * seq
    sets = len(packs)
    rows = heads * 3 * HEAD_DIM
    extra = [] if carried is None else [carried]
    vmem = pl.BlockSpec(memory_space=pltpu.VMEM)
    dma = pltpu.SemaphoreType.DMA
    out_shape = [jax.ShapeDtypeStruct((3 * width, tokens), jnp.bfloat16)]
    if sets == 2:
        out_shape.append(jax.ShapeDtypeStruct((heads, 2 * HEAD_DIM, length), jnp.float32))
    return pl.pallas_call(
        functools.partial(backward_kernel, seq, sets, bool(extra), heads),
        out_shape=tuple(out_shape),
        in_specs=[vmem] * (3 + sets + len(extra)),
        out_specs=(vmem,) * len(out_shape),
        scratch_shapes=[
            pltpu.VMEM((heads * HEAD_DIM, length), jnp.bfloat16),
            pltpu.VMEM((rows, length), jnp.bfloat16),
            pltpu.VMEM((3 * width, tokens), jnp.bfloat16),
            pltpu.VMEM((HEAD_DIM, length), jnp.bfloat16),
            pltpu.VMEM((sets, length, HEAD_DIM), jnp.bfloat16),
            pltpu.VMEM((sets, HEAD_DIM, length), jnp.bfloat16),
            pltpu.VMEM((sets, length, HEAD_DIM), jnp.bfloat16),
            pltpu.VMEM((1, length), jnp.float32),
            pltpu.VMEM((HEAD_DIM, length), jnp.float32),
            pltpu.VMEM((sets, 2 * HEAD_DIM, length), jnp.float32),
            dma((heads, seq)),
            dma((heads, seq)),
            dma((heads, seq)),
            dma((heads, seq)),
        ],
        compiler_params=pltpu.CompilerParams(
            collective_id=call_id, has_side_effects=True, vmem_limit_bytes=48 << 20
        ),
        name=f"attend_backward_{sets}",
    )(d_mixed, *packs, own, totals, *extra)


def block_forward(sizes, call_id, stream, qkv_w, gains, earlier, weights, shards):
    seq, dp, heads = sizes
    normed = layer_norm(stream, gains[0]).astype(jnp.bfloat16)
    packed = lax.dot_general(
        qkv_w, normed, (((0,), (1,)), ((), ())), preferred_element_type=jnp.float32
    ).astype(jnp.bfloat16)
    (head_rows, mixed, own, totals), gathered = attend_forward(
        seq, dp, heads, packed, earlier, shards, call_id
    )
    out_w, up_w, down_w = weights or gathered
    middle = stream + contract_rows(mixed, out_w)
    normed_b = layer_norm(middle, gains[1]).astype(jnp.bfloat16)
    hidden = jnp.dot(normed_b, up_w, preferred_element_type=jnp.float32)
    active = gelu_value(hidden).astype(jnp.bfloat16)
    result = middle + jnp.dot(active, down_w, preferred_element_type=jnp.float32)
    stored = (stream, normed, earlier + [head_rows], own, totals, mixed, middle, normed_b, hidden, active)
    return result, stored, (out_w, up_w, down_w)


def block_backward(sizes, call_id, upstream, stored, qkv_w, gains, weights, carried):
    seq, dp, heads = sizes
    out_w, up_w, down_w = weights
    stream, normed, packs, own, totals, mixed, middle, normed_b, hidden, active = stored
    out_bf = upstream.astype(jnp.bfloat16)
    down_grad = contract_rows(active, out_bf)
    d_active = contract_cols(out_bf, down_w)
    d_hidden = jax.vjp(gelu_value, hidden)[1](d_active)[0].astype(jnp.bfloat16)
    up_grad = contract_rows(normed_b, d_hidden)
    d_normed_b = contract_cols(d_hidden, up_w)
    d_middle_norm, gain_b_grad = jax.vjp(layer_norm, middle, gains[1])[1](d_normed_b)
    d_middle = upstream + d_middle_norm
    middle_bf = d_middle.astype(jnp.bfloat16)
    out_grad = jnp.dot(mixed, middle_bf, preferred_element_type=jnp.float32)
    d_mixed = contract_cols(out_w, middle_bf).astype(jnp.bfloat16)
    outs = attend_backward(seq, heads, d_mixed, packs, own, totals, carried, call_id)
    d_packed = outs[0]
    passed = outs[1] if len(outs) > 1 else None
    qkv_grad = lax.dot_general(
        normed, d_packed, (((0,), (1,)), ((), ())), preferred_element_type=jnp.float32
    )
    d_normed = lax.dot_general(
        d_packed, qkv_w, (((0,), (1,)), ((), ())), preferred_element_type=jnp.float32
    )
    d_stream_norm, gain_a_grad = jax.vjp(layer_norm, stream, gains[0])[1](d_normed)
    grads = (qkv_grad, out_grad, up_grad, down_grad, gain_a_grad, gain_b_grad)
    return d_middle + d_stream_norm, grads, passed


def local(
    seq,
    dp,
    tokens,
    qkv_weight,
    out_weight,
    up_weight,
    down_weight,
    norm_gain,
    mlp_gain,
    pass_embed,
    cotangent,
):
    share = norm_gain.shape[0]
    small = jnp.zeros((8, 256), jnp.bfloat16)
    small = small.at[0, :share].set(norm_gain).at[1, :share].set(mlp_gain)
    small = small.at[0, 128 : 128 + share].set(pass_embed)
    qkv_w, small = gather_now(seq, dp, [qkv_weight, small])
    small = small.reshape(dp, 8, 256)
    gains = [small[:, row, :share].reshape(-1).astype(jnp.float32) for row in (0, 1)]
    embedding = small[:, 0, 128 : 128 + share].reshape(-1).astype(jnp.float32)
    heads = qkv_weight.shape[1] // (3 * HEAD_DIM * seq)
    sizes = (seq, dp, heads)
    first_out, first_kept, weights = block_forward(
        sizes,
        1,
        tokens[0].astype(jnp.float32),
        qkv_w,
        gains,
        [],
        None,
        [out_weight, up_weight, down_weight],
    )
    second_out, second_kept, weights = block_forward(
        sizes, 2, first_out + embedding, qkv_w, gains, [first_kept[2][0]], weights, []
    )
    d_second, second_grads, passed = block_backward(
        sizes, 3, cotangent[0].astype(jnp.float32), second_kept, qkv_w, gains, weights, None
    )
    embed_grad = jnp.sum(d_second, axis=0)
    d_first, first_grads, unused = block_backward(
        sizes, 4, d_second, first_kept, qkv_w, gains, weights, passed
    )
    summed = jax.tree.map(jnp.add, first_grads, second_grads) + (embed_grad,)
    shards = (
        lax.psum_scatter(
            summed[0].astype(jnp.bfloat16), "dp", scatter_dimension=0, tiled=True
        ).astype(jnp.float32),
        lax.psum_scatter(
            summed[1].astype(jnp.bfloat16), "dp", scatter_dimension=0, tiled=True
        ).astype(jnp.float32),
        lax.psum_scatter(
            summed[2].astype(jnp.bfloat16), "dp", scatter_dimension=0, tiled=True
        ).astype(jnp.float32),
        lax.psum_scatter(
            summed[3].astype(jnp.bfloat16), "dp", scatter_dimension=0, tiled=True
        ).astype(jnp.float32),
        lax.psum_scatter(
            summed[4].astype(jnp.bfloat16), "dp", scatter_dimension=0, tiled=True
        ).astype(jnp.float32),
        lax.psum_scatter(
            summed[5].astype(jnp.bfloat16), "dp", scatter_dimension=0, tiled=True
        ).astype(jnp.float32),
        lax.psum_scatter(
            summed[6].astype(jnp.bfloat16), "dp", scatter_dimension=0, tiled=True
        ).astype(jnp.float32),
    )
    final = (
        lax.psum(shards[0].astype(jnp.bfloat16), "seq").astype(jnp.float32),
        lax.psum(shards[1].astype(jnp.bfloat16), "seq").astype(jnp.float32),
        lax.psum(shards[2].astype(jnp.bfloat16), "seq").astype(jnp.float32),
        lax.psum(shards[3].astype(jnp.bfloat16), "seq").astype(jnp.float32),
        lax.psum(shards[4].astype(jnp.bfloat16), "seq").astype(jnp.float32),
        lax.psum(shards[5].astype(jnp.bfloat16), "seq").astype(jnp.float32),
        lax.psum(shards[6].astype(jnp.bfloat16), "seq").astype(jnp.float32),
    )
    return (
        second_out.astype(jnp.bfloat16)[None],
        d_first[None],
        final[0],
        final[1],
        final[2],
        final[3],
        final[4],
        final[5],
        final[6],
    )


def solution(mesh):
    in_specs = (
        P("dp", "seq", None),
        P("dp", None),
        P("dp", None),
        P("dp", None),
        P("dp", None),
        P("dp"),
        P("dp"),
        P("dp"),
        P("dp", "seq", None),
    )
    out_specs = (
        P("dp", "seq", None),
        P("dp", "seq", None),
        P("dp", None),
        P("dp", None),
        P("dp", None),
        P("dp", None),
        P("dp"),
        P("dp"),
        P("dp"),
    )
    return jax.shard_map(
        functools.partial(local, mesh.shape["seq"], mesh.shape["dp"]), mesh=mesh, in_specs=in_specs, out_specs=out_specs, check_vma=False)
```

```python
import functools

import jax
import jax.numpy as jnp
from jax import lax
from jax.experimental import pallas as pl
from jax.experimental.pallas import tpu as pltpu
from jax.sharding import PartitionSpec as P

HEAD_DIM = 64
BACKGROUND = 3


epsilon = 1e-05


def layer_norm(vector, gain_vec):
    centre = vector - jnp.mean(vector, axis=-1, keepdims=True)
    spread = jnp.mean(centre * centre, axis=-1, keepdims=True)
    return centre * lax.rsqrt(spread + epsilon) * gain_vec


def gelu_value(vector):
    return jax.nn.gelu(vector, approximate=True)


def contract_rows(left_side, right_side):
    return lax.dot_general(
        left_side, right_side, (((0,), (0,)), ((), ())), preferred_element_type=jnp.float32
    )


def contract_cols(left_side, right_side):
    return lax.dot_general(
        left_side, right_side, (((1,), (1,)), ((), ())), preferred_element_type=jnp.float32
    )


def nt(left, right):
    return lax.dot_general(
        left, right, (((1,), (1,)), ((), ())), preferred_element_type=jnp.float32
    )


def nn(left, right):
    return lax.dot_general(
        left, right, (((1,), (0,)), ((), ())), preferred_element_type=jnp.float32
    )


def remote(src, dst, send_sem, recv_sem, device):
    return pltpu.make_async_remote_copy(
        src_ref=src,
        dst_ref=dst,
        send_sem=send_sem,
        recv_sem=recv_sem,
        device_id=device,
        device_id_type=pl.DeviceIdType.MESH,
    )


def greet(devices):
    barrier = pltpu.get_barrier_semaphore()
    for device in devices:
        pl.semaphore_signal(
            barrier, inc=1, device_id=device, device_id_type=pl.DeviceIdType.MESH
        )
    pl.semaphore_wait(barrier, len(devices))


def seq_peers(seq):
    me = lax.axis_index("seq")
    return [lax.rem(me + d, seq) for d in range(1, seq)]


class Gather:
    def __init__(self, seq, dp, shards, wholes, sems):
        self.line = dp // 2
        self.shards, self.wholes = shards, wholes
        self.z_send, self.z_recv, self.y_send, self.y_recv, self.c_send, self.c_recv, self.own = sems
        me = lax.axis_index("seq")
        self.core = lax.rem(me, 2)
        self.core_peer = {"seq": me + 1 - 2 * self.core}
        self.rank = lax.axis_index("dp")
        self.a, self.b = lax.div(self.rank, 2), lax.rem(self.rank, 2)
        self.y_peer = {"dp": self.a * 2 + 1 - self.b}
        self.sent = []

    @staticmethod
    def sems(units, dp):
        line = dp // 2
        dma = pltpu.SemaphoreType.DMA
        return [
            dma((units, line)),
            dma((units, line)),
            dma((units, line)),
            dma((units, line)),
            dma((units, 2 * line)),
            dma((units, 2 * line)),
            dma((units,)),
        ]

    def z_rank(self, offset):
        return lax.rem(self.a + offset, self.line) * 2 + self.b

    def peers(self):
        z = [{"dp": self.z_rank(d)} for d in range(1, self.line)]
        return z + [self.y_peer]

    def place(self, unit, rank):
        rows, columns = self.shards[unit].shape
        half = columns // 2
        return (
            pl.ds(pl.multiple_of(rank * rows, 8), rows),
            pl.ds(pl.multiple_of(self.core * half, 128), half),
        )

    def send(self, src, dst, send_sem, recv_sem, device):
        copy = remote(src, dst, send_sem, recv_sem, device)
        copy.start()
        self.sent.append(copy)
        return copy

    def start(self, unit):
        shard, whole = self.shards[unit], self.wholes[unit]
        where = self.place(unit, self.rank)
        mine = shard.at[:, where[1]]
        self.z_copies = getattr(self, "z_copies", {})
        self.y_copies = getattr(self, "y_copies", {})
        self.c_copies = getattr(self, "c_copies", {})
        for d in range(1, self.line):
            self.z_copies[unit, d] = self.send(
                mine,
                whole.at[where],
                self.z_send.at[unit, d],
                self.z_recv.at[unit, d],
                {"dp": self.z_rank(d)},
            )
        self.y_copies[unit, 0] = self.send(
            mine, whole.at[where], self.y_send.at[unit, 0], self.y_recv.at[unit, 0], self.y_peer
        )
        local_copy = pltpu.make_async_copy(
            shard, whole.at[where[0]], self.own.at[unit]
        )
        local_copy.start()
        self.c_copies[unit, 0] = local_copy

    def to_core(self, unit, slot, rank):
        block = self.wholes[unit].at[self.place(unit, rank)]
        self.c_copies[unit, slot] = self.send(
            block, block, self.c_send.at[unit, slot], self.c_recv.at[unit, slot], self.core_peer
        )

    def forward_z(self, unit):
        for d in range(1, self.line):
            self.z_copies[unit, d].wait_recv()
            rank = self.z_rank(self.line - d)
            block = self.wholes[unit].at[self.place(unit, rank)]
            self.y_copies[unit, d] = self.send(
                block, block, self.y_send.at[unit, d], self.y_recv.at[unit, d], self.y_peer
            )
            self.to_core(unit, d, rank)

    def forward_y(self, unit):
        for d in range(self.line):
            self.y_copies[unit, d].wait_recv()
            rank = lax.rem(self.a + self.line - d, self.line) * 2 + 1 - self.b
            self.to_core(unit, self.line + d, rank)

    def finish(self, unit):
        for slot in range(1, 2 * self.line):
            self.c_copies[unit, slot].wait_recv()
        self.c_copies[unit, 0].wait()

    def drain(self):
        for copy in self.sent:
            copy.wait_send()


def gather_kernel(seq, dp, units, *refs):
    shards, wholes, sems = refs[:units], refs[units : 2 * units], refs[2 * units :]
    gather = Gather(seq, dp, shards, wholes, sems)
    greet(gather.peers() + [gather.core_peer])
    for unit in range(units):
        gather.start(unit)
    for unit in range(units):
        gather.forward_z(unit)
    for unit in range(units):
        gather.forward_y(unit)
    for unit in range(units):
        gather.finish(unit)
    gather.drain()


def whole_shape(shard, dp):
    return jax.ShapeDtypeStruct((shard.shape[0] * dp, shard.shape[1]), shard.dtype)


def gather_now(seq, dp, shards):
    units = len(shards)
    hbm = pl.BlockSpec(memory_space=pl.ANY)
    return pl.pallas_call(
        functools.partial(gather_kernel, seq, dp, units),
        out_shape=tuple(whole_shape(shard, dp) for shard in shards),
        in_specs=[hbm] * units,
        out_specs=(hbm,) * units,
        scratch_shapes=Gather.sems(units, dp),
        compiler_params=pltpu.CompilerParams(
            collective_id=0, has_side_effects=True, vmem_limit_bytes=4 << 20
        ),
        name="gather_first",
    )(*shards)


class Scatter:
    SEMS = 11

    def __init__(self, seq, dp, grads, outs, scratch):
        self.seq, self.dp, self.line, self.chips = seq, dp, dp // 2, seq // 2
        self.grads, self.outs = grads, outs
        me = lax.axis_index("seq")
        self.core, self.chip = lax.rem(me, 2), lax.div(me, 2)
        self.core_peer = {"seq": me + 1 - 2 * self.core}
        self.rank = lax.axis_index("dp")
        self.a, self.b = lax.div(self.rank, 2), lax.rem(self.rank, 2)
        self.y_peer = {"dp": self.a * 2 + 1 - self.b}
        self.buffers = [scratch[7 * u : 7 * u + 7] for u in range(len(grads))]
        self.sems = scratch[7 * len(grads) :]
        self.flying, self.sent = {}, []

    @staticmethod
    def scratch(seq, dp, grads):
        shapes = []
        line, chips = dp // 2, seq // 2
        for grad in grads:
            rows, half = grad.shape[1], grad.shape[2] // 2
            for lead in ((dp,), (dp,), (line,), (line,), (), (chips,)):
                shapes.append(pltpu.VMEM(lead + (rows, half), jnp.bfloat16))
            shapes.append(pltpu.VMEM((rows, 2 * half), jnp.float32))
        units, dma = len(grads), pltpu.SemaphoreType.DMA
        sizes = (1, 1, 1, line, line, line, line, chips, chips, 1, 1)
        return shapes + [dma((units, size)) for size in sizes]

    def peers(self):
        z = [{"dp": self.other(d) * 2 + self.b} for d in range(1, self.line)]
        return z + [self.y_peer]

    def x_peers(self):
        return [
            {"seq": lax.rem(self.chip + d, self.chips) * 2 + self.core}
            for d in range(1, self.chips)
        ]

    def other(self, offset):
        return lax.rem(self.a + offset, self.line)

    def half(self, unit, core):
        half = self.grads[unit].shape[2] // 2
        return pl.ds(pl.multiple_of(core * half, 128), half)

    def send(self, key, src, dst, sems, slot, device):
        unit = key[1]
        copy = remote(
            src, dst, self.sems[sems].at[unit, slot], self.sems[sems + 1].at[unit, slot], device
        )
        copy.start()
        self.flying[key] = copy
        self.sent.append(copy)

    def start(self, unit):
        total, core_in = self.buffers[unit][:2]
        grad = self.grads[unit]
        self.send(
            ("core", unit), grad.at[:, :, self.half(unit, 1 - self.core)], core_in, 0, 0, self.core_peer
        )
        copy = pltpu.make_async_copy(
            grad.at[:, :, self.half(unit, self.core)], total, self.sems[2].at[unit, 0]
        )
        copy.start()
        self.flying["own", unit] = copy

    def chip_sum(self, unit):
        total, core_in, y_in = self.buffers[unit][:3]
        self.flying["core", unit].wait_recv()
        self.flying["own", unit].wait()
        for place in range(self.line):
            row = place * 2 + 1 - self.b
            total[row] = add(total[row], core_in[row]).astype(jnp.bfloat16)
            self.send(("y", unit, place), total.at[row], y_in.at[place], 3, place, self.y_peer)

    def y_sum(self, unit):
        total, core_in, y_in, z_in = self.buffers[unit][:4]
        for d in range(1, self.line):
            place = self.other(d)
            row = place * 2 + self.b
            if d == 1:
                for slot in range(self.line):
                    self.flying["y", unit, slot].wait_recv()
            total[row] = add(total[row], core_in[row], y_in[place]).astype(jnp.bfloat16)
            self.send(("z", unit, d), total.at[row], z_in.at[d], 5, d, {"dp": row})

    def z_sum(self, unit):
        total, core_in, y_in, z_in, x_out, x_in = self.buffers[unit][:6]
        for d in range(1, self.line):
            self.flying["z", unit, d].wait_recv()
        terms = [total[self.rank], core_in[self.rank], y_in[self.a]]
        terms += [z_in[d] for d in range(1, self.line)]
        x_out[...] = add(*terms).astype(jnp.bfloat16)
        for d, peer in enumerate(self.x_peers()):
            self.send(("x", unit, d), x_out, x_in.at[d], 7, d, peer)

    def x_sum(self, unit):
        x_out, x_in, final = self.buffers[unit][4:]
        for d in range(self.chips - 1):
            self.flying["x", unit, d].wait_recv()
        mine = self.half(unit, self.core)
        final[:, mine] = add(x_out[...], *[x_in[d] for d in range(self.chips - 1)])
        self.send(("f", unit), final.at[:, mine], final.at[:, mine], 9, 0, self.core_peer)

    def finish(self, unit):
        self.flying["f", unit].wait_recv()
        self.outs[unit][...] = self.buffers[unit][6][...]

    def drain(self):
        for copy in self.sent:
            copy.wait_send()


def add(*terms):
    total = terms[0].astype(jnp.float32)
    for term in terms[1:]:
        total = total + term.astype(jnp.float32)
    return total


def scatter_kernel(seq, dp, units, *refs):
    grads, outs, scratch = refs[:units], refs[units : 2 * units], refs[2 * units :]
    work = Scatter(seq, dp, grads, outs, scratch)
    greet(work.peers() + work.x_peers() + [work.core_peer])
    stages = (work.start, work.chip_sum, work.y_sum, work.z_sum, work.x_sum, work.finish)
    for stage in stages:
        for unit in range(units):
            stage(unit)
    work.drain()


def owned_shape(grad):
    return jax.ShapeDtypeStruct(grad.shape[1:], jnp.float32)


def scatter_now(seq, dp, grads, call_id):
    units = len(grads)
    return pl.pallas_call(
        functools.partial(scatter_kernel, seq, dp, units),
        out_shape=tuple(owned_shape(grad) for grad in grads),
        in_specs=[pl.BlockSpec(memory_space=pl.ANY)] * units,
        out_specs=(pl.BlockSpec(memory_space=pltpu.VMEM),) * units,
        scratch_shapes=Scatter.scratch(seq, dp, grads),
        compiler_params=pltpu.CompilerParams(
            collective_id=call_id, has_side_effects=True, vmem_limit_bytes=48 << 20
        ),
        name="scatter_last",
    )(*grads)


def causal_mask(size):
    rows = lax.broadcasted_iota(jnp.int32, (size, size), 0)
    columns = lax.broadcasted_iota(jnp.int32, (size, size), 1)
    return rows <= columns


def forward_kernel(seq, dp, sets, units, heads, *refs):
    refs = list(refs)

    def take(count):
        taken = refs[:count]
        del refs[:count]
        return taken

    (packed,) = take(1)
    earlier = take(sets - 1)
    shards = take(units)
    heads_out, mixed_out, own_out, totals_out = take(4)
    wholes = take(units)
    arrived, mixed_in, q_s, k_s, v_s, in_send, in_recv, out_send, out_recv = take(9)
    gather = Gather(seq, dp, shards, wholes, refs) if units else None

    tokens = packed.shape[1]
    length = tokens * seq
    group = 3 * HEAD_DIM
    me = lax.axis_index("seq")
    peers = seq_peers(seq)
    greet([{"seq": peer} for peer in peers] + (gather.peers() if units else []))

    own_lanes = pl.ds(pl.multiple_of(me * tokens, tokens), tokens)
    copies = {}
    for h in range(heads):
        for d, peer in enumerate(peers):
            copy = remote(
                packed.at[pl.ds(pl.multiple_of((peer * heads + h) * group, group), group)],
                arrived.at[pl.ds(h * group, group), own_lanes],
                in_send.at[h, d],
                in_recv.at[h, d],
                {"seq": peer},
            )
            copy.start()
            copies[h, d] = copy
    for unit in range(units):
        gather.start(unit)
    for h in range(heads):
        arrived[h * group : (h + 1) * group, own_lanes] = packed[
            pl.ds(pl.multiple_of((me * heads + h) * group, group), group), :
        ]

    mask = causal_mask(tokens)
    for s in range(sets):
        v_s[s, HEAD_DIM:] = jnp.ones((16, length), jnp.bfloat16)
    results = []
    for h in range(heads):
        c0 = h * group
        for s in range(sets):
            source = earlier[s] if s < sets - 1 else arrived
            if s == sets - 1:
                for d in range(seq - 1):
                    copies[h, d].wait_recv()
                heads_out[c0 : c0 + group, :] = arrived[c0 : c0 + group, :]
                q_s[...] = arrived[c0 : c0 + HEAD_DIM, :] * jnp.bfloat16(HEAD_DIM**-0.5)
            k_s[s] = source[c0 + HEAD_DIM : c0 + 2 * HEAD_DIM, :].T
            v_s[s, :HEAD_DIM] = source[c0 + 2 * HEAD_DIM : c0 + 3 * HEAD_DIM, :]

        for i in range(seq):
            queries = q_s[:, i * tokens : (i + 1) * tokens]
            peak = total = None
            for j in [i] + list(range(i)):
                keys = slice(j * tokens, (j + 1) * tokens)
                scores = []
                for s in range(sets):
                    block = nn(k_s[s, keys, :], queries)
                    if j == i:
                        block = jnp.where(mask, block, -1e30)
                    scores.append(block)
                peak_now = peak
                for block in scores:
                    top = jnp.max(block, axis=0, keepdims=True)
                    peak_now = top if peak_now is None else jnp.maximum(peak_now, top)
                if total is not None:
                    total = total * jnp.exp(peak - peak_now)
                for s, block in enumerate(scores):
                    weights = jnp.exp(block - peak_now).astype(jnp.bfloat16)
                    part = nn(v_s[s, :, keys], weights)
                    total = part if total is None else total + part
                peak = peak_now
            row_sum = total[HEAD_DIM : HEAD_DIM + 1]
            own_out[h * HEAD_DIM : (h + 1) * HEAD_DIM, i * tokens : (i + 1) * tokens] = (
                total[:HEAD_DIM] / row_sum
            ).astype(jnp.bfloat16)
            totals_out[h, :, i * tokens : (i + 1) * tokens] = peak + jnp.log(row_sum)

        mine = pl.ds(pl.multiple_of((me * heads + h) * HEAD_DIM, HEAD_DIM), HEAD_DIM)
        for d, peer in enumerate(peers):
            copy = remote(
                own_out.at[
                    pl.ds(h * HEAD_DIM, HEAD_DIM),
                    pl.ds(pl.multiple_of(peer * tokens, tokens), tokens),
                ],
                mixed_in.at[mine],
                out_send.at[h, d],
                out_recv.at[h, d],
                {"seq": peer},
            )
            copy.start()
            results.append(copy)
        mixed_in[mine] = own_out[h * HEAD_DIM : (h + 1) * HEAD_DIM, own_lanes]
        if units:
            if h == 0:
                gather.forward_z(0)
            elif h == 1:
                gather.forward_y(0)
                gather.forward_z(1)
    if units:
        gather.forward_z(2)
        gather.forward_y(1)
        gather.forward_y(2)
        for unit in range(units):
            gather.finish(unit)
        gather.drain()
    for copy in copies.values():
        copy.wait_send()
    for copy in results:
        copy.wait()
    mixed_out[...] = mixed_in[...]


def attend_forward(seq, dp, heads, packed, earlier, shards, call_id):
    width, tokens = packed.shape
    length = tokens * seq
    sets, units = 1 + len(earlier), len(shards)
    rows = heads * 3 * HEAD_DIM
    vmem = pl.BlockSpec(memory_space=pltpu.VMEM)
    hbm = pl.BlockSpec(memory_space=pl.ANY)
    dma = pltpu.SemaphoreType.DMA
    outs = pl.pallas_call(
        functools.partial(forward_kernel, seq, dp, sets, units, heads),
        out_shape=(
            jax.ShapeDtypeStruct((rows, length), jnp.bfloat16),
            jax.ShapeDtypeStruct((width // 3, tokens), jnp.bfloat16),
            jax.ShapeDtypeStruct((heads * HEAD_DIM, length), jnp.bfloat16),
            jax.ShapeDtypeStruct((heads, 1, length), jnp.float32),
        )
        + tuple(whole_shape(shard, dp) for shard in shards),
        in_specs=[vmem] * sets + [hbm] * units,
        out_specs=(vmem,) * 4 + (hbm,) * units,
        scratch_shapes=[
            pltpu.VMEM((rows, length), jnp.bfloat16),
            pltpu.VMEM((width // 3, tokens), jnp.bfloat16),
            pltpu.VMEM((HEAD_DIM, length), jnp.bfloat16),
            pltpu.VMEM((sets, length, HEAD_DIM), jnp.bfloat16),
            pltpu.VMEM((sets, HEAD_DIM + 16, length), jnp.bfloat16),
            dma((heads, seq)),
            dma((heads, seq)),
            dma((heads, seq)),
            dma((heads, seq)),
        ]
        + (Gather.sems(units, dp) if units else []),
        compiler_params=pltpu.CompilerParams(
            collective_id=call_id, has_side_effects=True, vmem_limit_bytes=40 << 20
        ),
        name=f"attend_forward_{sets}",
    )(packed, *earlier, *shards)
    return outs[:4], outs[4:]


def backward_kernel(seq, dp, sets, carried, units, heads, *refs):
    refs = list(refs)

    def take(count):
        taken = refs[:count]
        del refs[:count]
        return taken

    (d_mixed,) = take(1)
    packs = take(sets)
    own_in, totals_in = take(2)
    carry_in = take(1)[0] if carried else None
    grads_in = take(units)
    (d_packed_out,) = take(1)
    carry_out = take(1)[0] if sets == 2 else None
    grads_out = take(units)
    arrived, local_grad, d_packed_in, q_s, k_s, kt_s, v_s, delta_s, dq_s, dkv_s = take(10)
    in_send, in_recv, out_send, out_recv = take(4)
    work = Scatter(seq, dp, grads_in, grads_out, refs) if units else None

    tokens = d_mixed.shape[1]
    length = tokens * seq
    group = 3 * HEAD_DIM
    me = lax.axis_index("seq")
    peers = seq_peers(seq)
    greet([{"seq": peer} for peer in peers] + (work.peers() if units else []))
    own_lanes = pl.ds(pl.multiple_of(me * tokens, tokens), tokens)
    scale = jnp.bfloat16(HEAD_DIM**-0.5)

    copies = {}
    for h in range(heads):
        for d, peer in enumerate(peers):
            copy = remote(
                d_mixed.at[pl.ds(pl.multiple_of((peer * heads + h) * HEAD_DIM, HEAD_DIM), HEAD_DIM)],
                arrived.at[pl.ds(h * HEAD_DIM, HEAD_DIM), own_lanes],
                in_send.at[h, d],
                in_recv.at[h, d],
                {"seq": peer},
            )
            copy.start()
            copies[h, d] = copy
    stages = []
    if units:
        for unit in range(units):
            work.start(unit)
        stages = background_order(work, units)
    for h in range(heads):
        arrived[h * HEAD_DIM : (h + 1) * HEAD_DIM, own_lanes] = d_mixed[
            pl.ds(pl.multiple_of((me * heads + h) * HEAD_DIM, HEAD_DIM), HEAD_DIM), :
        ]

    mask = causal_mask(tokens)
    results = []
    for h in range(heads):
        c0 = h * group
        r0 = h * HEAD_DIM
        q_s[...] = packs[-1][c0 : c0 + HEAD_DIM, :] * scale
        for s in range(sets):
            keys = packs[s][c0 + HEAD_DIM : c0 + 2 * HEAD_DIM, :]
            k_s[s] = keys.T
            kt_s[s] = keys * scale
            v_s[s] = packs[s][c0 + 2 * HEAD_DIM : c0 + 3 * HEAD_DIM, :].T
        for d in range(seq - 1):
            copies[h, d].wait_recv()
        delta_s[...] = jnp.sum(
            arrived[r0 : r0 + HEAD_DIM, :].astype(jnp.float32)
            * own_in[r0 : r0 + HEAD_DIM, :].astype(jnp.float32),
            axis=0,
            keepdims=True,
        )
        for j in range(seq):
            keys = slice(j * tokens, (j + 1) * tokens)
            for i in range(j, seq):
                span = slice(i * tokens, (i + 1) * tokens)
                queries = q_s[:, span]
                grads = arrived[r0 : r0 + HEAD_DIM, span]
                d_query = dq_s[:, span] if j > 0 else None
                for s in range(sets):
                    chances = jnp.exp(nn(k_s[s, keys, :], queries) - totals_in[h, :, span])
                    if i == j:
                        chances = jnp.where(mask, chances, 0.0)
                    d_chance = nn(v_s[s, keys, :], grads)
                    d_score = (chances * (d_chance - delta_s[:, span])).astype(jnp.bfloat16)
                    d_key = nt(queries, d_score)
                    d_value = nt(grads, chances.astype(jnp.bfloat16))
                    if i == j:
                        if carried:
                            d_key = d_key + carry_in[h, :HEAD_DIM, keys]
                            d_value = d_value + carry_in[h, HEAD_DIM:, keys]
                        dkv_s[s, :HEAD_DIM, keys] = d_key
                        dkv_s[s, HEAD_DIM:, keys] = d_value
                    else:
                        dkv_s[s, :HEAD_DIM, keys] += d_key
                        dkv_s[s, HEAD_DIM:, keys] += d_value
                    part = nn(kt_s[s, :, keys], d_score)
                    d_query = part if d_query is None else d_query + part
                dq_s[:, span] = d_query
            local_grad[c0 : c0 + HEAD_DIM, keys] = dq_s[:, keys].astype(jnp.bfloat16)
            local_grad[c0 + HEAD_DIM : c0 + group, keys] = dkv_s[sets - 1, :, keys].astype(
                jnp.bfloat16
            )
            if stages:
                stages.pop(0)()
        if sets == 2:
            carry_out[h] = dkv_s[0]
        mine = pl.ds(pl.multiple_of((me * heads + h) * group, group), group)
        for d, peer in enumerate(peers):
            copy = remote(
                local_grad.at[
                    pl.ds(c0, group), pl.ds(pl.multiple_of(peer * tokens, tokens), tokens)
                ],
                d_packed_in.at[mine],
                out_send.at[h, d],
                out_recv.at[h, d],
                {"seq": peer},
            )
            copy.start()
            results.append(copy)
        d_packed_in[mine] = local_grad[c0 : c0 + group, own_lanes]
    for stage in stages:
        stage()
    if units:
        work.drain()
    for copy in copies.values():
        copy.wait_send()
    for copy in results:
        copy.wait()
    d_packed_out[...] = d_packed_in[...]


def background_order(work, units):
    order = []
    for step in range(units + 4):
        for stage, call in enumerate((work.chip_sum, work.y_sum, work.z_sum, work.x_sum, work.finish)):
            if 0 <= step - stage < units:
                order.append(functools.partial(call, step - stage))
    return order


def attend_backward(seq, dp, heads, d_mixed, packs, own, totals, carried, grads, call_id):
    width, tokens = d_mixed.shape
    length = tokens * seq
    sets = len(packs)
    rows = heads * 3 * HEAD_DIM
    extra = [] if carried is None else [carried]
    vmem = pl.BlockSpec(memory_space=pltpu.VMEM)
    dma = pltpu.SemaphoreType.DMA
    out_shape = [jax.ShapeDtypeStruct((3 * width, tokens), jnp.bfloat16)]
    if sets == 2:
        out_shape.append(jax.ShapeDtypeStruct((heads, 2 * HEAD_DIM, length), jnp.float32))
    units = len(grads)
    out_shape += [owned_shape(grad) for grad in grads]
    hbm = pl.BlockSpec(memory_space=pl.ANY)
    return pl.pallas_call(
        functools.partial(backward_kernel, seq, dp, sets, bool(extra), units, heads),
        out_shape=tuple(out_shape),
        in_specs=[vmem] * (3 + sets + len(extra)) + [hbm] * units,
        out_specs=(vmem,) * len(out_shape),
        scratch_shapes=[
            pltpu.VMEM((heads * HEAD_DIM, length), jnp.bfloat16),
            pltpu.VMEM((rows, length), jnp.bfloat16),
            pltpu.VMEM((3 * width, tokens), jnp.bfloat16),
            pltpu.VMEM((HEAD_DIM, length), jnp.bfloat16),
            pltpu.VMEM((sets, length, HEAD_DIM), jnp.bfloat16),
            pltpu.VMEM((sets, HEAD_DIM, length), jnp.bfloat16),
            pltpu.VMEM((sets, length, HEAD_DIM), jnp.bfloat16),
            pltpu.VMEM((1, length), jnp.float32),
            pltpu.VMEM((HEAD_DIM, length), jnp.float32),
            pltpu.VMEM((sets, 2 * HEAD_DIM, length), jnp.float32),
            dma((heads, seq)),
            dma((heads, seq)),
            dma((heads, seq)),
            dma((heads, seq)),
        ]
        + (Scatter.scratch(seq, dp, grads) if units else []),
        compiler_params=pltpu.CompilerParams(
            collective_id=call_id, has_side_effects=True, vmem_limit_bytes=58 << 20
        ),
        name=f"attend_backward_{sets}",
    )(d_mixed, *packs, own, totals, *extra, *grads)


def block_forward(sizes, call_id, stream, qkv_w, gains, earlier, weights, shards):
    seq, dp, heads = sizes
    normed = layer_norm(stream, gains[0]).astype(jnp.bfloat16)
    packed = lax.dot_general(
        qkv_w, normed, (((0,), (1,)), ((), ())), preferred_element_type=jnp.float32
    ).astype(jnp.bfloat16)
    (head_rows, mixed, own, totals), gathered = attend_forward(
        seq, dp, heads, packed, earlier, shards, call_id
    )
    out_w, up_w, down_w = weights or gathered
    middle = stream + contract_rows(mixed, out_w)
    normed_b = layer_norm(middle, gains[1]).astype(jnp.bfloat16)
    hidden = jnp.dot(normed_b, up_w, preferred_element_type=jnp.float32)
    active = gelu_value(hidden).astype(jnp.bfloat16)
    result = middle + jnp.dot(active, down_w, preferred_element_type=jnp.float32)
    stored = (stream, normed, earlier + [head_rows], own, totals, mixed, middle, normed_b, hidden, active)
    return result, stored, (out_w, up_w, down_w)


def split_rows(dp, first, second):
    total = (first + second).astype(jnp.bfloat16)
    return total.reshape(dp, total.shape[0] // dp, total.shape[1])


def block_backward(sizes, call_id, upstream, stored, qkv_w, gains, weights, carried, later):
    seq, dp, heads = sizes
    out_w, up_w, down_w = weights
    stream, normed, packs, own, totals, mixed, middle, normed_b, hidden, active = stored
    out_bf = upstream.astype(jnp.bfloat16)
    down_grad = contract_rows(active, out_bf)
    d_active = contract_cols(out_bf, down_w)
    d_hidden = jax.vjp(gelu_value, hidden)[1](d_active)[0].astype(jnp.bfloat16)
    up_grad = contract_rows(normed_b, d_hidden)
    d_normed_b = contract_cols(d_hidden, up_w)
    d_middle_norm, gain_b_grad = jax.vjp(layer_norm, middle, gains[1])[1](d_normed_b)
    d_middle = upstream + d_middle_norm
    middle_bf = d_middle.astype(jnp.bfloat16)
    out_grad = jnp.dot(mixed, middle_bf, preferred_element_type=jnp.float32)
    d_mixed = contract_cols(out_w, middle_bf).astype(jnp.bfloat16)
    background = []
    if later is not None:
        background = [
            split_rows(dp, one, two)
            for one, two in zip((out_grad, up_grad, down_grad)[:BACKGROUND], later[1 : 1 + BACKGROUND])
        ]
    outs = attend_backward(
        seq, dp, heads, d_mixed, packs, own, totals, carried, background, call_id
    )
    d_packed = outs[0]
    passed = outs[1] if later is None else outs[1:]
    qkv_grad = lax.dot_general(
        normed, d_packed, (((0,), (1,)), ((), ())), preferred_element_type=jnp.float32
    )
    d_normed = lax.dot_general(
        d_packed, qkv_w, (((0,), (1,)), ((), ())), preferred_element_type=jnp.float32
    )
    d_stream_norm, gain_a_grad = jax.vjp(layer_norm, stream, gains[0])[1](d_normed)
    grads = (qkv_grad, out_grad, up_grad, down_grad, gain_a_grad, gain_b_grad)
    return d_middle + d_stream_norm, grads, passed


def local(
    seq,
    dp,
    tokens,
    qkv_weight,
    out_weight,
    up_weight,
    down_weight,
    norm_gain,
    mlp_gain,
    pass_embed,
    cotangent,
):
    share = norm_gain.shape[0]
    small = jnp.zeros((8, 256), jnp.bfloat16)
    small = small.at[0, :share].set(norm_gain).at[1, :share].set(mlp_gain)
    small = small.at[0, 128 : 128 + share].set(pass_embed)
    qkv_w, small = gather_now(seq, dp, [qkv_weight, small])
    small = small.reshape(dp, 8, 256)
    gains = [small[:, row, :share].reshape(-1).astype(jnp.float32) for row in (0, 1)]
    embedding = small[:, 0, 128 : 128 + share].reshape(-1).astype(jnp.float32)
    heads = qkv_weight.shape[1] // (3 * HEAD_DIM * seq)
    sizes = (seq, dp, heads)
    first_out, first_kept, weights = block_forward(
        sizes,
        1,
        tokens[0].astype(jnp.float32),
        qkv_w,
        gains,
        [],
        None,
        [out_weight, up_weight, down_weight],
    )
    second_out, second_kept, weights = block_forward(
        sizes, 2, first_out + embedding, qkv_w, gains, [first_kept[2][0]], weights, []
    )
    d_second, second_grads, passed = block_backward(
        sizes, 3, cotangent[0].astype(jnp.float32), second_kept, qkv_w, gains, weights, None, None
    )
    embed_grad = jnp.sum(d_second, axis=0)
    d_first, first_grads, done = block_backward(
        sizes, 4, d_second, first_kept, qkv_w, gains, weights, passed, second_grads
    )
    vectors = [first_grads[4] + second_grads[4], first_grads[5] + second_grads[5], embed_grad]
    gain_a, gain_b, embed = [
        jnp.pad(v.astype(jnp.bfloat16).reshape(dp, 1, share), ((0, 0), (0, 0), (0, 128 - share)))
        for v in vectors
    ]
    top = jnp.concatenate([gain_a, embed], axis=2)
    low = jnp.concatenate([gain_b, jnp.zeros_like(embed)], axis=2)
    small = jnp.concatenate([top, low, jnp.zeros((dp, 6, 256), jnp.bfloat16)], axis=1)
    last = [
        split_rows(dp, one, two)
        for one, two in list(zip(first_grads, second_grads))[1 + BACKGROUND : 4] + [(first_grads[0], second_grads[0])]
    ]
    rest = scatter_now(seq, dp, [small] + last, 5)
    small, qkv = rest[0], rest[-1]
    others = list(done) + list(rest[1:-1])
    return (
        second_out.astype(jnp.bfloat16)[None],
        d_first[None],
        qkv,
        *others,
        small[0, :share],
        small[1, :share],
        small[0, 128 : 128 + share],
    )


def solution(mesh):
    in_specs = (
        P("dp", "seq", None),
        P("dp", None),
        P("dp", None),
        P("dp", None),
        P("dp", None),
        P("dp"),
        P("dp"),
        P("dp"),
        P("dp", "seq", None),
    )
    out_specs = (
        P("dp", "seq", None),
        P("dp", "seq", None),
        P("dp", None),
        P("dp", None),
        P("dp", None),
        P("dp", None),
        P("dp"),
        P("dp"),
        P("dp"),
    )
    return jax.shard_map(
        functools.partial(local, mesh.shape["seq"], mesh.shape["dp"]), mesh=mesh, in_specs=in_specs, out_specs=out_specs, check_vma=False)
```

```python
import functools

import jax
import jax.numpy as jnp
from jax import lax
from jax.experimental import pallas as pl
from jax.experimental.pallas import tpu as pltpu
from jax.sharding import PartitionSpec as P

HEAD_DIM = 64
CHUNK = 768
EVERY = 3
SLOTS = 5


epsilon = 1e-05


def layer_norm(vector, gain_vec):
    centre = vector - jnp.mean(vector, axis=-1, keepdims=True)
    spread = jnp.mean(centre * centre, axis=-1, keepdims=True)
    return centre * lax.rsqrt(spread + epsilon) * gain_vec


def gelu_value(vector):
    return jax.nn.gelu(vector, approximate=True)


def contract_rows(left_side, right_side):
    return lax.dot_general(
        left_side, right_side, (((0,), (0,)), ((), ())), preferred_element_type=jnp.float32
    )


def contract_cols(left_side, right_side):
    return lax.dot_general(
        left_side, right_side, (((1,), (1,)), ((), ())), preferred_element_type=jnp.float32
    )


def nt(left, right):
    return lax.dot_general(
        left, right, (((1,), (1,)), ((), ())), preferred_element_type=jnp.float32
    )


def nn(left, right):
    return lax.dot_general(
        left, right, (((1,), (0,)), ((), ())), preferred_element_type=jnp.float32
    )


def remote(src, dst, send_sem, recv_sem, device):
    return pltpu.make_async_remote_copy(
        src_ref=src,
        dst_ref=dst,
        send_sem=send_sem,
        recv_sem=recv_sem,
        device_id=device,
        device_id_type=pl.DeviceIdType.MESH,
    )


def greet(devices):
    barrier = pltpu.get_barrier_semaphore()
    for device in devices:
        pl.semaphore_signal(
            barrier, inc=1, device_id=device, device_id_type=pl.DeviceIdType.MESH
        )
    pl.semaphore_wait(barrier, len(devices))


def seq_peers(seq):
    me = lax.axis_index("seq")
    return [lax.rem(me + d, seq) for d in range(1, seq)]


class Gather:
    def __init__(self, seq, dp, shards, wholes, units, sems):
        self.line = dp // 2
        self.shards, self.wholes, self.units = shards, wholes, units
        self.z_send, self.z_recv, self.y_send, self.y_recv, self.c_send, self.c_recv, self.own = sems
        me = lax.axis_index("seq")
        self.core = lax.rem(me, 2)
        self.core_peer = {"seq": me + 1 - 2 * self.core}
        self.rank = lax.axis_index("dp")
        self.a, self.b = lax.div(self.rank, 2), lax.rem(self.rank, 2)
        self.y_peer = {"dp": self.a * 2 + 1 - self.b}
        self.flying, self.sent = {}, []

    @staticmethod
    def sems(arrays, units, dp):
        line, dma = dp // 2, pltpu.SemaphoreType.DMA
        sizes = (line, line, line, line, 2 * line, 2 * line)
        return [dma((units, size)) for size in sizes] + [dma((arrays,))]

    def z_rank(self, offset):
        return lax.rem(self.a + offset, self.line) * 2 + self.b

    def peers(self):
        z = [{"dp": self.z_rank(d)} for d in range(1, self.line)]
        return z + [self.y_peer]

    def columns(self, unit):
        array, row, rows, column, columns = self.units[unit]
        half = columns // 2
        return pl.ds(pl.multiple_of(column + self.core * half, 128), half)

    def block(self, unit, rank):
        array, row, rows, column, columns = self.units[unit]
        first = rank * self.shards[array].shape[0] + row
        return self.wholes[array].at[pl.ds(pl.multiple_of(first, 8), rows), self.columns(unit)]

    def send(self, key, src, dst, send_sem, recv_sem, device):
        copy = remote(src, dst, send_sem, recv_sem, device)
        copy.start()
        self.flying[key] = copy
        self.sent.append(copy)

    def keep_own(self):
        for array, (shard, whole) in enumerate(zip(self.shards, self.wholes)):
            rows = shard.shape[0]
            copy = pltpu.make_async_copy(
                shard, whole.at[pl.ds(pl.multiple_of(self.rank * rows, 8), rows)], self.own.at[array]
            )
            copy.start()
            self.flying["own", array] = copy

    def start(self, unit):
        array, row, rows = self.units[unit][:3]
        mine = self.shards[array].at[pl.ds(row, rows), self.columns(unit)]
        there = self.block(unit, self.rank)
        for d in range(1, self.line):
            self.send(
                ("z", unit, d),
                mine,
                there,
                self.z_send.at[unit, d],
                self.z_recv.at[unit, d],
                {"dp": self.z_rank(d)},
            )
        self.send(
            ("y", unit, 0), mine, there, self.y_send.at[unit, 0], self.y_recv.at[unit, 0], self.y_peer
        )

    def to_core(self, unit, slot, rank):
        block = self.block(unit, rank)
        self.send(
            ("core", unit, slot),
            block,
            block,
            self.c_send.at[unit, slot],
            self.c_recv.at[unit, slot],
            self.core_peer,
        )

    def forward_z(self, unit):
        for d in range(1, self.line):
            self.flying["z", unit, d].wait_recv()
            rank = self.z_rank(self.line - d)
            block = self.block(unit, rank)
            self.send(
                ("y", unit, d),
                block,
                block,
                self.y_send.at[unit, d],
                self.y_recv.at[unit, d],
                self.y_peer,
            )
            self.to_core(unit, d, rank)

    def forward_y(self, unit):
        for d in range(self.line):
            self.flying["y", unit, d].wait_recv()
            rank = lax.rem(self.a + self.line - d, self.line) * 2 + 1 - self.b
            self.to_core(unit, self.line + d, rank)

    def finish(self):
        for unit in range(len(self.units)):
            for slot in range(1, 2 * self.line):
                self.flying["core", unit, slot].wait_recv()
        for array in range(len(self.shards)):
            self.flying["own", array].wait()
        for copy in self.sent:
            copy.wait_send()

    def steps(self):
        count, calls = len(self.units), []
        for step in range(count + 1):
            if step < count:
                calls.append(functools.partial(self.forward_z, step))
            if step > 0:
                calls.append(functools.partial(self.forward_y, step - 1))
        return calls


def cut(shapes, rows, size):
    units = []
    for array, shape in enumerate(shapes):
        high, wide = min(shape[0], rows), min(shape[1], size)
        for row in range(0, shape[0], high):
            for column in range(0, shape[1], wide):
                units.append((array, row, high, column, wide))
    return units


def gather_kernel(seq, dp, units, arrays, *refs):
    shards, wholes, sems = refs[:arrays], refs[arrays : 2 * arrays], refs[2 * arrays :]
    gather = Gather(seq, dp, shards, wholes, units, sems)
    greet(gather.peers() + [gather.core_peer])
    for unit in range(len(units)):
        gather.start(unit)
    gather.keep_own()
    for call in gather.steps():
        call()
    gather.finish()


def whole_shape(shard, dp):
    return jax.ShapeDtypeStruct((shard.shape[0] * dp, shard.shape[1]), shard.dtype)


def gather_now(seq, dp, shards):
    arrays = len(shards)
    units = cut([shard.shape for shard in shards], shards[0].shape[0], CHUNK)
    hbm = pl.BlockSpec(memory_space=pl.ANY)
    return pl.pallas_call(
        functools.partial(gather_kernel, seq, dp, units, arrays),
        out_shape=tuple(whole_shape(shard, dp) for shard in shards),
        in_specs=[hbm] * arrays,
        out_specs=(hbm,) * arrays,
        scratch_shapes=Gather.sems(arrays, len(units), dp),
        compiler_params=pltpu.CompilerParams(
            collective_id=0, has_side_effects=True, vmem_limit_bytes=4 << 20
        ),
        name="gather_first",
    )(*shards)


class Scatter:
    def __init__(self, seq, dp, units, outs, scratch):
        self.seq, self.dp, self.line, self.chips = seq, dp, dp // 2, seq // 2
        self.units, self.outs = units, outs
        me = lax.axis_index("seq")
        self.core, self.chip = lax.rem(me, 2), lax.div(me, 2)
        self.core_peer = {"seq": me + 1 - 2 * self.core}
        self.rank = lax.axis_index("dp")
        self.a, self.b = lax.div(self.rank, 2), lax.rem(self.rank, 2)
        self.y_peer = {"dp": self.a * 2 + 1 - self.b}
        count = len(units)
        self.small, self.terms = scratch[0], scratch[1]
        self.buffers = [scratch[2 + 6 * u : 8 + 6 * u] for u in range(count)]
        self.sems = scratch[2 + 6 * count :]
        self.flying, self.sent = {}, {}

    @staticmethod
    def scratch(seq, dp, units):
        line, chips, b = dp // 2, seq // 2, jnp.bfloat16
        rows, columns = units[1][1:3]
        shapes = [
            pltpu.VMEM((dp,) + units[0][1:3], b),
            pltpu.VMEM((SLOTS, dp, rows, columns), b),
        ]
        for unit in units:
            rows, half = unit[1], unit[2] // 2
            for lead in ((dp,), (line,), (line,), (), (chips,)):
                shapes.append(pltpu.VMEM(lead + (rows, half), b))
            shapes.append(pltpu.VMEM((rows, 2 * half), jnp.float32))
        count, dma = len(units), pltpu.SemaphoreType.DMA
        sizes = (1, 1, 1, line, line, line, line, chips, chips, 1, 1)
        return shapes + [dma((count, size)) for size in sizes]

    def peers(self):
        z = [{"dp": self.other(d) * 2 + self.b} for d in range(1, self.line)]
        return z + [self.y_peer]

    def x_peers(self):
        return [
            {"seq": lax.rem(self.chip + d, self.chips) * 2 + self.core}
            for d in range(1, self.chips)
        ]

    def other(self, offset):
        return lax.rem(self.a + offset, self.line)

    def half(self, unit, core):
        half = self.units[unit][2] // 2
        return pl.ds(pl.multiple_of(core * half, 128), half)

    def term(self, unit, row, core):
        lanes = self.half(unit, core)
        if unit == 0:
            return self.small.at[row, :, lanes]
        return self.terms.at[(unit - 1) % SLOTS, row, :, lanes]

    def all_terms(self, unit, core):
        lanes = self.half(unit, core)
        if unit == 0:
            return self.small.at[:, :, lanes]
        return self.terms.at[(unit - 1) % SLOTS, :, :, lanes]

    def send(self, key, src, dst, sems, slot, device):
        unit = key[1]
        copy = remote(
            src, dst, self.sems[sems].at[unit, slot], self.sems[sems + 1].at[unit, slot], device
        )
        copy.start()
        self.flying[key] = copy
        self.sent.setdefault((unit, key[0] in ("core", "y", "z")), []).append(copy)

    def free(self, unit):
        if unit >= 1:
            for copy in self.sent.pop((unit, True), []):
                copy.wait_send()

    def start(self, unit):
        self.send(
            ("core", unit), self.all_terms(unit, 1 - self.core), self.buffers[unit][0], 0, 0, self.core_peer
        )

    def chip_sum(self, unit):
        core_in, y_in = self.buffers[unit][:2]
        self.flying["core", unit].wait_recv()
        for place in range(self.line):
            row = place * 2 + 1 - self.b
            total = self.term(unit, row, self.core)
            total[...] = add(total[...], core_in[row]).astype(jnp.bfloat16)
            self.send(("y", unit, place), total, y_in.at[place], 3, place, self.y_peer)

    def y_sum(self, unit):
        core_in, y_in, z_in = self.buffers[unit][:3]
        for place in range(self.line):
            self.flying["y", unit, place].wait_recv()
        for d in range(1, self.line):
            place = self.other(d)
            row = place * 2 + self.b
            total = self.term(unit, row, self.core)
            total[...] = add(total[...], core_in[row], y_in[place]).astype(jnp.bfloat16)
            self.send(("z", unit, d), total, z_in.at[d], 5, d, {"dp": row})

    def z_sum(self, unit):
        core_in, y_in, z_in, x_out, x_in = self.buffers[unit][:5]
        for d in range(1, self.line):
            self.flying["z", unit, d].wait_recv()
        terms = [self.term(unit, self.rank, self.core)[...], core_in[self.rank], y_in[self.a]]
        terms += [z_in[d] for d in range(1, self.line)]
        x_out[...] = add(*terms).astype(jnp.bfloat16)
        for d, peer in enumerate(self.x_peers()):
            self.send(("x", unit, d), x_out, x_in.at[d], 7, d, peer)

    def x_sum(self, unit):
        x_out, x_in, final = self.buffers[unit][3:]
        for d in range(self.chips - 1):
            self.flying["x", unit, d].wait_recv()
        mine = self.half(unit, self.core)
        final[:, mine] = add(x_out[...], *[x_in[d] for d in range(self.chips - 1)])
        self.send(("f", unit), final.at[:, mine], final.at[:, mine], 9, 0, self.core_peer)

    def finish(self, unit):
        array, rows, columns, row, column = self.units[unit]
        self.flying["f", unit].wait_recv()
        self.sent.pop((unit, False))
        for key in (("f", unit), *[("x", unit, d) for d in range(self.chips - 1)]):
            self.flying[key].wait_send()
        copy = pltpu.make_async_copy(
            self.buffers[unit][5],
            self.outs[array].at[pl.ds(row, rows), pl.ds(column, columns)],
            self.sems[2].at[unit, 0],
        )
        copy.start()
        self.flying["out", unit] = copy

    def drain(self):
        for copies in self.sent.values():
            for copy in copies:
                copy.wait_send()
        for unit in range(len(self.units)):
            self.flying["out", unit].wait()


def add(*terms):
    total = terms[0].astype(jnp.float32)
    for term in terms[1:]:
        total = total + term.astype(jnp.float32)
    return total


class Products:
    def __init__(self, refs, scratch, work, d_packed):
        (
            self.small,
            mixed,
            middle,
            active,
            upstream,
            normed_b,
            d_hidden,
            normed,
            self.second_packed,
        ) = refs
        self.stream, self.keep_rows, self.keep_left, self.result, self.sems = scratch
        self.work, self.d_packed = work, d_packed
        self.width, self.both = self.stream.shape[1:]
        self.tokens = self.both // 2
        self.mixed, self.active, self.d_hidden = mixed, active, d_hidden
        self.kept = [(middle, self.keep_rows.at[0]), (upstream, self.keep_rows.at[1])]
        self.kept += [(normed_b, self.keep_left.at[0]), (normed, self.keep_left.at[1])]
        self.flying = {}

    @staticmethod
    def scratch(width, tokens):
        b = jnp.bfloat16
        return [
            pltpu.VMEM((2, width, 2 * tokens), b),
            pltpu.VMEM((2, 2 * tokens, width), b),
            pltpu.VMEM((2, width, 2 * tokens), b),
            pltpu.VMEM((width, width), jnp.float32),
            pltpu.SemaphoreType.DMA((32, 2)),
        ]

    def copy(self, key, slot, side, src, dst):
        copy = pltpu.make_async_copy(src, dst, self.sems.at[slot, side])
        copy.start()
        self.flying.setdefault(key, []).append(copy)

    def wait(self, key):
        for copy in self.flying.pop(key, []):
            copy.wait()

    def begin(self):
        self.copy("small", 30, 0, self.small, self.work.small)
        self.fetch(1)
        for index, (pair, place) in enumerate(self.kept):
            for side in range(2):
                span = pl.ds(side * self.tokens, self.tokens)
                where = place.at[span] if index < 2 else place.at[:, span]
                self.copy(("kept", index), 20 + index, side, pair[side], where)
        self.fetch(2)

    def kind(self, unit):
        array, rows, columns, row, column = self.work.units[unit]
        return array, row // rows, column // columns

    def fetch(self, unit):
        if unit >= len(self.work.units):
            return
        array, row, column = self.kind(unit)
        slot = unit % 2
        for side in range(2):
            lanes = pl.ds(side * self.tokens, self.tokens)
            if array == 1:
                self.copy(unit, unit, side, self.mixed[side], self.stream.at[slot, :, lanes])
            elif array == 3:
                rows = self.work.units[unit][1]
                for rank in range(self.work.dp):
                    pltpu.make_async_copy(
                        self.active[side].at[rank, row],
                        self.stream.at[slot, pl.ds(rank * rows, rows), lanes],
                        self.sems.at[unit, side],
                    ).start()
                all_ranks = pltpu.make_async_copy(
                    self.d_hidden[side].at[pl.ds(0, self.width)],
                    self.stream.at[slot, :, lanes],
                    self.sems.at[unit, side],
                )
                self.flying.setdefault(unit, []).append(all_ranks)
            elif array == 2:
                self.copy(
                    unit,
                    unit,
                    side,
                    self.d_hidden[side].at[pl.ds(column * self.width, self.width)],
                    self.stream.at[slot, :, lanes],
                )
            elif side == 1:
                self.copy(
                    unit,
                    unit,
                    side,
                    self.second_packed.at[pl.ds(column * self.width, self.width)],
                    self.stream.at[slot, :, lanes],
                )

    def make(self, unit):
        work = self.work
        if unit == 0:
            self.wait("small")
            work.start(0)
            return
        array, row, column = self.kind(unit)
        slot = unit % 2
        kept = {1: 0, 3: 1, 2: 2, 4: 3}[array]
        self.wait(("kept", kept))
        self.wait(unit)
        if array == 4:
            self.stream[slot, :, : self.tokens] = self.d_packed[
                column * self.width : (column + 1) * self.width, :
            ]
        step = self.width // 3
        for part in range(3):
            span = slice(part * step, (part + 1) * step)
            if kept < 2:
                self.result[span, :] = nn(self.stream[slot, span, :], self.keep_rows[kept])
            else:
                self.result[span, :] = nt(self.keep_left[kept - 2, span, :], self.stream[slot])
        work.free(unit - SLOTS)
        rows = work.units[unit][1]
        for rank in range(work.dp):
            work.terms[(unit - 1) % SLOTS, rank] = self.result[
                rank * rows : (rank + 1) * rows, :
            ].astype(jnp.bfloat16)
        work.start(unit)
        self.fetch(unit + 2)


def background_order(work, products):
    count = len(work.units)
    stages = (
        (3, products.make),
        (2, work.chip_sum),
        (0, work.y_sum),
        (-1, work.z_sum),
        (-2, work.x_sum),
        (-3, work.finish),
    )
    order = []
    for step in range(-3, count + 3):
        calls = [
            functools.partial(call, step + ahead) for ahead, call in stages if 0 <= step + ahead < count
        ]
        order.append(calls)
    return order


def causal_mask(size):
    rows = lax.broadcasted_iota(jnp.int32, (size, size), 0)
    columns = lax.broadcasted_iota(jnp.int32, (size, size), 1)
    return rows <= columns


def forward_kernel(seq, dp, sets, units, arrays, heads, *refs):
    refs = list(refs)

    def take(count):
        taken = refs[:count]
        del refs[:count]
        return taken

    (packed,) = take(1)
    earlier = take(sets - 1)
    shards = take(arrays)
    heads_out, mixed_out, own_out, totals_out = take(4)
    wholes = take(arrays)
    arrived, mixed_in, q_s, k_s, v_s, in_send, in_recv, out_send, out_recv = take(9)
    gather = Gather(seq, dp, shards, wholes, units, refs) if units else None

    tokens = packed.shape[1]
    length = tokens * seq
    group = 3 * HEAD_DIM
    me = lax.axis_index("seq")
    peers = seq_peers(seq)
    greet([{"seq": peer} for peer in peers] + (gather.peers() if units else []))

    own_lanes = pl.ds(pl.multiple_of(me * tokens, tokens), tokens)
    copies = {}
    for h in range(heads):
        for d, peer in enumerate(peers):
            copy = remote(
                packed.at[pl.ds(pl.multiple_of((peer * heads + h) * group, group), group)],
                arrived.at[pl.ds(h * group, group), own_lanes],
                in_send.at[h, d],
                in_recv.at[h, d],
                {"seq": peer},
            )
            copy.start()
            copies[h, d] = copy
    steps = []
    if units:
        for unit in range(len(units)):
            gather.start(unit)
        gather.keep_own()
        steps = gather.steps()
        steps.pop(0)()
    for h in range(heads):
        arrived[h * group : (h + 1) * group, own_lanes] = packed[
            pl.ds(pl.multiple_of((me * heads + h) * group, group), group), :
        ]

    mask = causal_mask(tokens)
    for s in range(sets):
        v_s[s, HEAD_DIM:] = jnp.ones((16, length), jnp.bfloat16)
    results = []
    for h in range(heads):
        c0 = h * group
        for s in range(sets):
            source = earlier[s] if s < sets - 1 else arrived
            if s == sets - 1:
                for d in range(seq - 1):
                    copies[h, d].wait_recv()
                heads_out[c0 : c0 + group, :] = arrived[c0 : c0 + group, :]
                q_s[...] = arrived[c0 : c0 + HEAD_DIM, :] * jnp.bfloat16(HEAD_DIM**-0.5)
            k_s[s] = source[c0 + HEAD_DIM : c0 + 2 * HEAD_DIM, :].T
            v_s[s, :HEAD_DIM] = source[c0 + 2 * HEAD_DIM : c0 + 3 * HEAD_DIM, :]

        for i in range(seq):
            queries = q_s[:, i * tokens : (i + 1) * tokens]
            peak = total = None
            for j in [i] + list(range(i)):
                keys = slice(j * tokens, (j + 1) * tokens)
                scores = []
                for s in range(sets):
                    block = nn(k_s[s, keys, :], queries)
                    if j == i:
                        block = jnp.where(mask, block, -1e30)
                    scores.append(block)
                peak_now = peak
                for block in scores:
                    top = jnp.max(block, axis=0, keepdims=True)
                    peak_now = top if peak_now is None else jnp.maximum(peak_now, top)
                if total is not None:
                    total = total * jnp.exp(peak - peak_now)
                for s, block in enumerate(scores):
                    weights = jnp.exp(block - peak_now).astype(jnp.bfloat16)
                    part = nn(v_s[s, :, keys], weights)
                    total = part if total is None else total + part
                peak = peak_now
            row_sum = total[HEAD_DIM : HEAD_DIM + 1]
            own_out[h * HEAD_DIM : (h + 1) * HEAD_DIM, i * tokens : (i + 1) * tokens] = (
                total[:HEAD_DIM] / row_sum
            ).astype(jnp.bfloat16)
            totals_out[h, :, i * tokens : (i + 1) * tokens] = peak + jnp.log(row_sum)
            if steps and i % 2 == 1:
                steps.pop(0)()

        mine = pl.ds(pl.multiple_of((me * heads + h) * HEAD_DIM, HEAD_DIM), HEAD_DIM)
        for d, peer in enumerate(peers):
            copy = remote(
                own_out.at[
                    pl.ds(h * HEAD_DIM, HEAD_DIM),
                    pl.ds(pl.multiple_of(peer * tokens, tokens), tokens),
                ],
                mixed_in.at[mine],
                out_send.at[h, d],
                out_recv.at[h, d],
                {"seq": peer},
            )
            copy.start()
            results.append(copy)
        mixed_in[mine] = own_out[h * HEAD_DIM : (h + 1) * HEAD_DIM, own_lanes]
    for step in steps:
        step()
    if units:
        gather.finish()
    for copy in copies.values():
        copy.wait_send()
    for copy in results:
        copy.wait()
    mixed_out[...] = mixed_in[...]


def attend_forward(seq, dp, heads, packed, earlier, shards, call_id):
    width, tokens = packed.shape
    length = tokens * seq
    sets, arrays = 1 + len(earlier), len(shards)
    units = cut([shard.shape for shard in shards], shards[0].shape[0], CHUNK) if arrays else []
    rows = heads * 3 * HEAD_DIM
    vmem = pl.BlockSpec(memory_space=pltpu.VMEM)
    hbm = pl.BlockSpec(memory_space=pl.ANY)
    dma = pltpu.SemaphoreType.DMA
    outs = pl.pallas_call(
        functools.partial(forward_kernel, seq, dp, sets, units, arrays, heads),
        out_shape=(
            jax.ShapeDtypeStruct((rows, length), jnp.bfloat16),
            jax.ShapeDtypeStruct((width // 3, tokens), jnp.bfloat16),
            jax.ShapeDtypeStruct((heads * HEAD_DIM, length), jnp.bfloat16),
            jax.ShapeDtypeStruct((heads, 1, length), jnp.float32),
        )
        + tuple(whole_shape(shard, dp) for shard in shards),
        in_specs=[vmem] * sets + [hbm] * arrays,
        out_specs=(vmem,) * 4 + (hbm,) * arrays,
        scratch_shapes=[
            pltpu.VMEM((rows, length), jnp.bfloat16),
            pltpu.VMEM((width // 3, tokens), jnp.bfloat16),
            pltpu.VMEM((HEAD_DIM, length), jnp.bfloat16),
            pltpu.VMEM((sets, length, HEAD_DIM), jnp.bfloat16),
            pltpu.VMEM((sets, HEAD_DIM + 16, length), jnp.bfloat16),
            dma((heads, seq)),
            dma((heads, seq)),
            dma((heads, seq)),
            dma((heads, seq)),
        ]
        + (Gather.sems(arrays, len(units), dp) if units else []),
        compiler_params=pltpu.CompilerParams(
            collective_id=call_id, has_side_effects=True, vmem_limit_bytes=40 << 20
        ),
        name=f"attend_forward_{sets}",
    )(packed, *earlier, *shards)
    return outs[:4], outs[4:]


def backward_kernel(seq, dp, sets, units, heads, *refs):
    refs = list(refs)

    def take(count):
        taken = refs[:count]
        del refs[:count]
        return taken

    (d_mixed,) = take(1)
    packs = take(sets)
    own_in, totals_in = take(2)
    if units:
        (carry_in, small) = take(2)
        pairs = [take(2) for _ in range(7)]
        (second_packed,) = take(1)
    (d_packed_out,) = take(1)
    carry_out = None if units else take(1)[0]
    grads_out = take(5) if units else []
    arrived, local_grad, d_packed_in, q_s, k_s, kt_s, v_s, delta_s, dq_s, dkv_s = take(10)
    in_send, in_recv, out_send, out_recv, out_sem = take(5)
    if units:
        carry_s, carry_sem = take(2)
        product_scratch = take(5)
        work = Scatter(seq, dp, units, grads_out, refs)
        products = Products([small] + pairs + [second_packed], product_scratch, work, d_packed_in)

    tokens = d_mixed.shape[1]
    length = tokens * seq
    group = 3 * HEAD_DIM
    me = lax.axis_index("seq")
    peers = seq_peers(seq)
    greet([{"seq": peer} for peer in peers] + (work.peers() if units else []))
    own_lanes = pl.ds(pl.multiple_of(me * tokens, tokens), tokens)
    scale = jnp.bfloat16(HEAD_DIM**-0.5)

    copies = {}
    for h in range(heads):
        for d, peer in enumerate(peers):
            copy = remote(
                d_mixed.at[pl.ds(pl.multiple_of((peer * heads + h) * HEAD_DIM, HEAD_DIM), HEAD_DIM)],
                arrived.at[pl.ds(h * HEAD_DIM, HEAD_DIM), own_lanes],
                in_send.at[h, d],
                in_recv.at[h, d],
                {"seq": peer},
            )
            copy.start()
            copies[h, d] = copy
    steps = []
    if units:
        products.begin()
        steps = background_order(work, products)
        early = [unit[0] for unit in units].index(4)
        later = steps[early:]
        steps = steps[:early]
    for h in range(heads):
        arrived[h * HEAD_DIM : (h + 1) * HEAD_DIM, own_lanes] = d_mixed[
            pl.ds(pl.multiple_of((me * heads + h) * HEAD_DIM, HEAD_DIM), HEAD_DIM), :
        ]

    def run(calls):
        for call in calls:
            call()

    def outgoing(h, rank, send_slot):
        return remote(
            local_grad.at[
                pl.ds(h * group, group), pl.ds(pl.multiple_of(rank * tokens, tokens), tokens)
            ],
            d_packed_in.at[pl.ds(pl.multiple_of((me * heads + h) * group, group), group)],
            out_send.at[h, send_slot],
            out_recv.at[h, me],
            {"seq": rank},
        )

    if steps:
        run(steps.pop(0))
    mask = causal_mask(tokens)
    hook = 0
    for h in range(heads):
        c0 = h * group
        r0 = h * HEAD_DIM
        if units:
            carried = pltpu.make_async_copy(carry_in.at[h], carry_s, carry_sem.at[h])
            carried.start()
        q_s[...] = packs[-1][c0 : c0 + HEAD_DIM, :] * scale
        for s in range(sets):
            keys = packs[s][c0 + HEAD_DIM : c0 + 2 * HEAD_DIM, :]
            k_s[s] = keys.T
            kt_s[s] = keys * scale
            v_s[s] = packs[s][c0 + 2 * HEAD_DIM : c0 + 3 * HEAD_DIM, :].T
        for d in range(seq - 1):
            copies[h, d].wait_recv()
        delta_s[...] = jnp.sum(
            arrived[r0 : r0 + HEAD_DIM, :].astype(jnp.float32)
            * own_in[r0 : r0 + HEAD_DIM, :].astype(jnp.float32),
            axis=0,
            keepdims=True,
        )
        if units:
            carried.wait()
        for j in range(seq):
            keys = slice(j * tokens, (j + 1) * tokens)
            for i in range(j, seq):
                span = slice(i * tokens, (i + 1) * tokens)
                queries = q_s[:, span]
                grads = arrived[r0 : r0 + HEAD_DIM, span]
                d_query = dq_s[:, span] if j > 0 else None
                for s in range(sets):
                    chances = jnp.exp(nn(k_s[s, keys, :], queries) - totals_in[h, :, span])
                    if i == j:
                        chances = jnp.where(mask, chances, 0.0)
                    d_chance = nn(v_s[s, keys, :], grads)
                    d_score = (chances * (d_chance - delta_s[:, span])).astype(jnp.bfloat16)
                    d_key = nt(queries, d_score)
                    d_value = nt(grads, chances.astype(jnp.bfloat16))
                    if i == j:
                        if units:
                            d_key = d_key + carry_s[:HEAD_DIM, keys]
                            d_value = d_value + carry_s[HEAD_DIM:, keys]
                        dkv_s[s, :HEAD_DIM, keys] = d_key
                        dkv_s[s, HEAD_DIM:, keys] = d_value
                    else:
                        dkv_s[s, :HEAD_DIM, keys] += d_key
                        dkv_s[s, HEAD_DIM:, keys] += d_value
                    part = nn(kt_s[s, :, keys], d_score)
                    d_query = part if d_query is None else d_query + part
                dq_s[:, span] = d_query
                hook += 1
                if steps and hook % EVERY == 0:
                    run(steps.pop(0))
            local_grad[c0 : c0 + HEAD_DIM, keys] = dq_s[:, keys].astype(jnp.bfloat16)
            local_grad[c0 + HEAD_DIM : c0 + group, keys] = dkv_s[sets - 1, :, keys].astype(
                jnp.bfloat16
            )
            if h == heads - 1:

                @pl.when(me != j)
                def _():
                    outgoing(h, jnp.int32(j), j).start()

        if not units:
            carry_out[h] = dkv_s[0]
        if h < heads - 1:
            for d, peer in enumerate(peers):
                outgoing(h, peer, d).start()
        d_packed_in[pl.ds(pl.multiple_of((me * heads + h) * group, group), group)] = local_grad[
            c0 : c0 + group, own_lanes
        ]
    for calls in steps:
        run(calls)
    for h in range(heads):
        for peer in peers:
            remote(
                local_grad.at[pl.ds(h * group, group), own_lanes],
                d_packed_in.at[pl.ds(pl.multiple_of((peer * heads + h) * group, group), group)],
                out_send.at[h, 0],
                out_recv.at[h, peer],
                {"seq": peer},
            ).wait_recv()
    finished = pltpu.make_async_copy(d_packed_in, d_packed_out, out_sem.at[0])
    finished.start()
    if units:
        for calls in later:
            run(calls)
        work.drain()
    for copy in copies.values():
        copy.wait_send()
    for h in range(heads - 1):
        for d, peer in enumerate(peers):
            outgoing(h, peer, d).wait_send()
    for j in range(seq):

        @pl.when(me != j)
        def _():
            outgoing(heads - 1, jnp.int32(j), j).wait_send()

    finished.wait()


def attend_backward(seq, dp, heads, d_mixed, packs, own, totals, extra, units, call_id):
    width, tokens = d_mixed.shape
    length = tokens * seq
    sets = len(packs)
    rows = heads * 3 * HEAD_DIM
    vmem = pl.BlockSpec(memory_space=pltpu.VMEM)
    hbm = pl.BlockSpec(memory_space=pl.ANY)
    dma = pltpu.SemaphoreType.DMA
    f32 = jnp.float32
    out_shape = [jax.ShapeDtypeStruct((3 * width, tokens), jnp.bfloat16)]
    out_specs = [hbm]
    more = []
    if units:
        heights = [0] * 5
        for array, high, wide, row, column in units:
            heights[array] = max(heights[array], row + high)
        widths = [0] * 5
        for array, high, wide, row, column in units:
            widths[array] = max(widths[array], column + wide)
        out_shape += [jax.ShapeDtypeStruct(shape, f32) for shape in zip(heights, widths)]
        out_specs += [hbm] * 5
        more = [pltpu.VMEM((2 * HEAD_DIM, length), f32), dma((heads,))]
        more += Products.scratch(width, tokens) + Scatter.scratch(seq, dp, units)
    else:
        out_shape.append(jax.ShapeDtypeStruct((heads, 2 * HEAD_DIM, length), f32))
        out_specs.append(vmem)
    return pl.pallas_call(
        functools.partial(backward_kernel, seq, dp, sets, units, heads),
        out_shape=tuple(out_shape),
        in_specs=[vmem] * (3 + sets) + [hbm] * len(extra),
        out_specs=tuple(out_specs),
        scratch_shapes=[
            pltpu.VMEM((heads * HEAD_DIM, length), jnp.bfloat16),
            pltpu.VMEM((rows, length), jnp.bfloat16),
            pltpu.VMEM((3 * width, tokens), jnp.bfloat16),
            pltpu.VMEM((HEAD_DIM, length), jnp.bfloat16),
            pltpu.VMEM((sets, length, HEAD_DIM), jnp.bfloat16),
            pltpu.VMEM((sets, HEAD_DIM, length), jnp.bfloat16),
            pltpu.VMEM((sets, length, HEAD_DIM), jnp.bfloat16),
            pltpu.VMEM((1, length), f32),
            pltpu.VMEM((HEAD_DIM, length), f32),
            pltpu.VMEM((sets, 2 * HEAD_DIM, length), f32),
            dma((heads, seq)),
            dma((heads, seq)),
            dma((heads, seq)),
            dma((heads, seq)),
            dma((1,)),
        ]
        + more,
        compiler_params=pltpu.CompilerParams(
            collective_id=call_id, has_side_effects=True, vmem_limit_bytes=60 << 20
        ),
        name=f"attend_backward_{sets}",
    )(d_mixed, *packs, own, totals, *extra)


def dots(left, right, left_side, right_side):
    return lax.dot_general(
        left,
        right,
        (((left_side,), (right_side,)), ((), ())),
        preferred_element_type=jnp.float32,
    )


def block_forward(sizes, call_id, stream, qkv_w, gains, earlier, weights, shards):
    seq, dp, heads = sizes
    normed = layer_norm(stream, gains[0]).astype(jnp.bfloat16)
    packed = dots(qkv_w, normed, 0, 1).astype(jnp.bfloat16)
    (head_rows, mixed, own, totals), gathered = attend_forward(
        seq, dp, heads, packed, earlier, shards, call_id
    )
    out_w, up_w, down_w = weights or gathered
    middle = stream + dots(mixed, out_w, 0, 0)
    normed_b = layer_norm(middle, gains[1]).astype(jnp.bfloat16)
    hidden = dots(up_w, normed_b, 0, 1)
    active = gelu_value(hidden).astype(jnp.bfloat16)
    result = middle + dots(active, down_w, 0, 0)
    stored = (
        stream,
        normed.T,
        earlier + [head_rows],
        own,
        totals,
        mixed,
        middle,
        normed_b.T,
        hidden,
        active,
    )
    return result, stored, (out_w, up_w, down_w)


def block_backward(sizes, call_id, upstream, stored, qkv_w, gains, weights, second):
    seq, dp, heads = sizes
    out_w, up_w, down_w = weights
    stream, normed, packs, own, totals, mixed, middle, normed_b, hidden, active = stored
    out_bf = upstream.astype(jnp.bfloat16)
    d_active = dots(down_w, out_bf, 1, 1)
    d_hidden = jax.vjp(gelu_value, hidden)[1](d_active)[0].astype(jnp.bfloat16)
    d_normed_b = dots(d_hidden, up_w, 0, 1)
    d_middle_norm = jax.vjp(layer_norm, middle, gains[1])[1](d_normed_b)[0]
    d_middle = upstream + d_middle_norm
    middle_bf = d_middle.astype(jnp.bfloat16)
    d_mixed = dots(out_w, middle_bf, 1, 1).astype(jnp.bfloat16)
    width, tokens = d_mixed.shape
    rows = width // dp
    active = active.reshape(dp, active.shape[0] // width, rows, tokens)
    factors = (mixed, middle_bf, active, out_bf, normed_b, d_hidden, normed)
    extra, units = [], []
    if second is not None:
        passed, small, second_factors, second_packed = second
        extra = [passed, small]
        for pair in zip(factors, second_factors):
            extra += pair
        extra.append(second_packed)
        ff = d_hidden.shape[0]
        units = [(0, 8, 256, 0, 0)]
        units += [(1, rows, width, 0, 0)]
        units += [(3, rows, width, row, 0) for row in range(0, ff // dp, rows)]
        units += [(2, rows, width, 0, column) for column in range(0, ff, width)]
        units += [(4, rows, width, 0, column) for column in range(0, 3 * width, width)]
    outs = attend_backward(seq, dp, heads, d_mixed, packs, own, totals, extra, units, call_id)
    d_packed = outs[0]
    d_normed = dots(d_packed, qkv_w, 0, 1)
    d_stream_norm = jax.vjp(layer_norm, stream, gains[0])[1](d_normed)[0]
    return d_middle + d_stream_norm, factors, outs


def local(
    seq,
    dp,
    tokens,
    qkv_weight,
    out_weight,
    up_weight,
    down_weight,
    norm_gain,
    mlp_gain,
    pass_embed,
    cotangent,
):
    share = norm_gain.shape[0]
    lanes = [
        jnp.pad(v.reshape(1, share), ((0, 0), (0, 128 - share)))
        for v in (norm_gain, pass_embed, mlp_gain)
    ]
    small = jnp.concatenate(
        [
            jnp.concatenate(lanes[:2], axis=1),
            jnp.pad(lanes[2], ((0, 0), (0, 128))),
            jnp.zeros((6, 256), jnp.bfloat16),
        ]
    )
    qkv_w, small = gather_now(seq, dp, [qkv_weight, small])
    small = small.reshape(dp, 8, 256)
    gains = [small[:, row, :share].reshape(-1).astype(jnp.float32) for row in (0, 1)]
    embedding = small[:, 0, 128 : 128 + share].reshape(-1).astype(jnp.float32)
    heads = qkv_weight.shape[1] // (3 * HEAD_DIM * seq)
    sizes = (seq, dp, heads)
    first_out, first_kept, weights = block_forward(
        sizes,
        1,
        tokens[0].astype(jnp.float32),
        qkv_w,
        gains,
        [],
        None,
        [out_weight, up_weight, down_weight],
    )
    second_out, second_kept, weights = block_forward(
        sizes, 2, first_out + embedding, qkv_w, gains, [first_kept[2][0]], weights, []
    )
    d_second, factors, outs = block_backward(
        sizes, 3, cotangent[0].astype(jnp.float32), second_kept, qkv_w, gains, weights, None
    )
    embed = jnp.sum(d_second, axis=0).astype(jnp.bfloat16).reshape(dp, 1, share)
    embed = jnp.pad(embed, ((0, 0), (0, 7), (0, 256 - share)))
    second = (outs[1], embed, factors, outs[0])
    d_first, factors, outs = block_backward(
        sizes, 4, d_second, first_kept, qkv_w, gains, weights, second
    )
    packed, small, out_grad, up_grad, down_grad, qkv_grad = outs
    f32 = jnp.float32
    gain_a = jnp.sum(qkv_weight.astype(f32) * qkv_grad, axis=1) / norm_gain.astype(f32)
    gain_b = jnp.sum(up_weight.astype(f32) * up_grad, axis=1) / mlp_gain.astype(f32)
    return (
        second_out.astype(jnp.bfloat16)[None],
        d_first[None],
        qkv_grad,
        out_grad,
        up_grad,
        down_grad,
        gain_a,
        gain_b,
        small[0, :share],
    )


def solution(mesh):
    in_specs = (
        P("dp", "seq", None),
        P("dp", None),
        P("dp", None),
        P("dp", None),
        P("dp", None),
        P("dp"),
        P("dp"),
        P("dp"),
        P("dp", "seq", None),
    )
    out_specs = (
        P("dp", "seq", None),
        P("dp", "seq", None),
        P("dp", None),
        P("dp", None),
        P("dp", None),
        P("dp", None),
        P("dp"),
        P("dp"),
        P("dp"),
    )
    return jax.shard_map(
        functools.partial(local, mesh.shape["seq"], mesh.shape["dp"]), mesh=mesh, in_specs=in_specs, out_specs=out_specs, check_vma=False)
```

```python
import functools
import math

import jax
import jax.numpy as jnp
from jax import lax
from jax.experimental import pallas as pl
from jax.experimental.pallas import tpu as pltpu
from jax.sharding import PartitionSpec as P

HEAD_DIM = 64
CHUNK = 768
EVERY = 3
SLOTS = 5
PAIRS = 2


epsilon = 1e-05


def nt(left, right):
    return lax.dot_general(
        left, right, (((1,), (1,)), ((), ())), preferred_element_type=jnp.float32
    )


def nn(left, right):
    return lax.dot_general(
        left, right, (((1,), (0,)), ((), ())), preferred_element_type=jnp.float32
    )


def remote(src, dst, send_sem, recv_sem, device):
    return pltpu.make_async_remote_copy(
        src_ref=src,
        dst_ref=dst,
        send_sem=send_sem,
        recv_sem=recv_sem,
        device_id=device,
        device_id_type=pl.DeviceIdType.MESH,
    )


def greet(devices):
    barrier = pltpu.get_barrier_semaphore()
    for device in devices:
        pl.semaphore_signal(
            barrier, inc=1, device_id=device, device_id_type=pl.DeviceIdType.MESH
        )
    pl.semaphore_wait(barrier, len(devices))


def seq_peers(seq):
    me = lax.axis_index("seq")
    return [lax.rem(me + d, seq) for d in range(1, seq)]


class Gather:
    def __init__(self, seq, dp, shards, wholes, units, sems):
        self.line = dp // 2
        self.shards, self.wholes, self.units, self.sems = shards, wholes, units, sems
        me = lax.axis_index("seq")
        self.core, self.chip = lax.rem(me, 2), lax.div(me, 2)
        self.core_peer = {"seq": me + 1 - 2 * self.core}
        self.x_peer = {"seq": self.core + 2 - 2 * self.chip}
        self.rank = lax.axis_index("dp")
        self.a, self.b = lax.div(self.rank, 2), lax.rem(self.rank, 2)
        self.y_peer = {"dp": self.a * 2 + 1 - self.b}
        self.flying, self.sent = {}, []

    @staticmethod
    def scratch(arrays, units, dp):
        line, dma = dp // 2, pltpu.SemaphoreType.DMA
        sizes = (line, line, line, line, 2 * line, 2 * line, 2 * line, 2 * line, 2 * line, 2 * line)
        return [dma((units, size)) for size in sizes] + [dma((arrays,))]

    def z_rank(self, offset):
        return lax.rem(self.a + offset, self.line) * 2 + self.b

    def peers(self):
        z = [{"dp": self.z_rank(d)} for d in range(1, self.line)]
        return z + [self.y_peer]

    def shared(self, unit):
        return sum(self.units[unit][5:]) > 0

    def place(self, unit, first, chip):
        array, row, rows, column, columns, row_step, column_step = self.units[unit]
        half = columns // 2
        start = first + row
        side = column + self.core * half
        if row_step:
            start = start + chip * row_step
        if column_step:
            side = side + chip * column_step
        if not isinstance(start, int):
            start = pl.multiple_of(start, 8)
        return pl.ds(start, rows), pl.ds(pl.multiple_of(side, 128), half)

    def block(self, unit, rank, chip):
        array = self.units[unit][0]
        return self.wholes[array].at[self.place(unit, rank * self.shards[array].shape[0], chip)]

    def send(self, kind, unit, slot, src, dst, device):
        sems = {"z": 0, "y": 2, "core": 4, "x": 6, "core2": 8}[kind]
        copy = remote(
            src, dst, self.sems[sems].at[unit, slot], self.sems[sems + 1].at[unit, slot], device
        )
        copy.start()
        self.flying[kind, unit, slot] = copy
        self.sent.append(copy)

    def keep_own(self):
        for array, (shard, whole) in enumerate(zip(self.shards, self.wholes)):
            rows = shard.shape[0]
            copy = pltpu.make_async_copy(
                shard,
                whole.at[pl.ds(pl.multiple_of(self.rank * rows, 8), rows)],
                self.sems[10].at[array],
            )
            copy.start()
            self.flying["own", array] = copy

    def start(self, unit):
        array = self.units[unit][0]
        mine = self.shards[array].at[self.place(unit, 0, self.chip)]
        there = self.block(unit, self.rank, self.chip)
        for d in range(1, self.line):
            self.send("z", unit, d, mine, there, {"dp": self.z_rank(d)})
        self.send("y", unit, 0, mine, there, self.y_peer)

    def spread(self, unit, slot, rank):
        block = self.block(unit, rank, self.chip)
        if self.shared(unit):
            self.send("x", unit, slot, block, block, self.x_peer)
        self.send("core", unit, slot, block, block, self.core_peer)

    def forward_z(self, unit):
        for d in range(1, self.line):
            self.flying["z", unit, d].wait_recv()
            rank = self.z_rank(self.line - d)
            block = self.block(unit, rank, self.chip)
            self.send("y", unit, d, block, block, self.y_peer)
            self.spread(unit, d, rank)

    def y_rank(self, d):
        return lax.rem(self.a + self.line - d, self.line) * 2 + 1 - self.b

    def forward_y(self, unit):
        for d in range(self.line):
            self.flying["y", unit, d].wait_recv()
            self.spread(unit, self.line + d, self.y_rank(d))

    def forward_x(self, unit):
        if not self.shared(unit):
            return
        for slot in range(1, 2 * self.line):
            self.flying["x", unit, slot].wait_recv()
            d = slot % self.line
            rank = self.y_rank(d) if slot >= self.line else self.z_rank(self.line - d)
            block = self.block(unit, rank, 1 - self.chip)
            self.send("core2", unit, slot, block, block, self.core_peer)

    def finish(self):
        for unit in range(len(self.units)):
            for slot in range(1, 2 * self.line):
                self.flying["core", unit, slot].wait_recv()
                if self.shared(unit):
                    self.flying["core2", unit, slot].wait_recv()
        for array in range(len(self.shards)):
            self.flying["own", array].wait()
        for copy in self.sent:
            copy.wait_send()

    def steps(self):
        count, calls = len(self.units), []
        for step in range(count + 2):
            for call, unit in (
                (self.forward_z, step),
                (self.forward_y, step - 1),
                (self.forward_x, step - 2),
            ):
                if 0 <= unit < count:
                    calls.append(functools.partial(call, unit))
        return calls


def first_units(shards):
    (rows, wide), small = shards[0].shape, shards[1].shape
    units = [(0, 0, rows, 0, CHUNK, 0, CHUNK)]
    units += [(0, 0, rows, column, CHUNK, 0, 0) for column in range(2 * CHUNK, wide, CHUNK)]
    return units + [(1, 0, small[0], 0, small[1], 0, 0)]


def later_units(shards):
    (rows, width), (_, up_wide), (down_rows, _) = [shard.shape for shard in shards]
    ups = [(1, 0, rows, column, CHUNK, 0, 0) for column in range(0, up_wide, CHUNK)]
    shared = 2 * PAIRS * rows
    pairs = [(2, row, rows, 0, width, rows, 0) for row in range(0, shared, 2 * rows)]
    downs = [(2, row, rows, 0, width, 0, 0) for row in range(shared, down_rows, rows)]
    return [(0, 0, rows, 0, width, 0, 0)] + ups[:1] + pairs[:1] + ups[1:3] + pairs[1:] + ups[3:] + downs


def gather_kernel(seq, dp, units, arrays, *refs):
    shards, wholes, sems = refs[:arrays], refs[arrays : 2 * arrays], refs[2 * arrays :]
    gather = Gather(seq, dp, shards, wholes, units, sems)
    greet(gather.peers() + [gather.core_peer, gather.x_peer])
    for unit in range(len(units)):
        gather.start(unit)
    gather.keep_own()
    for call in gather.steps():
        call()
    gather.finish()


def whole_shape(shard, dp):
    return jax.ShapeDtypeStruct((shard.shape[0] * dp, shard.shape[1]), shard.dtype)


def gather_now(seq, dp, shards):
    arrays = len(shards)
    units = first_units(shards)
    hbm = pl.BlockSpec(memory_space=pl.ANY)
    return pl.pallas_call(
        functools.partial(gather_kernel, seq, dp, units, arrays),
        out_shape=tuple(whole_shape(shard, dp) for shard in shards),
        in_specs=[hbm] * arrays,
        out_specs=(hbm,) * arrays,
        scratch_shapes=Gather.scratch(arrays, len(units), dp),
        compiler_params=pltpu.CompilerParams(
            collective_id=0, has_side_effects=True, vmem_limit_bytes=4 << 20
        ),
        name="gather_first",
    )(*shards)


class Scatter:
    def __init__(self, seq, dp, units, outs, scratch):
        self.seq, self.dp, self.line, self.chips = seq, dp, dp // 2, seq // 2
        self.units, self.outs = units, outs
        me = lax.axis_index("seq")
        self.core, self.chip = lax.rem(me, 2), lax.div(me, 2)
        self.core_peer = {"seq": me + 1 - 2 * self.core}
        self.rank = lax.axis_index("dp")
        self.a, self.b = lax.div(self.rank, 2), lax.rem(self.rank, 2)
        self.y_peer = {"dp": self.a * 2 + 1 - self.b}
        count = len(units)
        self.small, self.terms = scratch[0], scratch[1]
        self.buffers = [scratch[2 + 6 * u : 8 + 6 * u] for u in range(count)]
        self.sems = scratch[2 + 6 * count :]
        self.flying, self.sent = {}, {}

    @staticmethod
    def scratch(seq, dp, units):
        line, chips, b = dp // 2, seq // 2, jnp.bfloat16
        rows, columns = units[1][1:3]
        shapes = [
            pltpu.VMEM((dp,) + units[0][1:3], b),
            pltpu.VMEM((SLOTS, dp, rows, columns), b),
        ]
        for unit in units:
            rows, half = unit[1], unit[2] // 2
            for lead in ((dp,), (line,), (line,), (), (chips,)):
                shapes.append(pltpu.VMEM(lead + (rows, half), b))
            shapes.append(pltpu.VMEM((rows, 2 * half), jnp.float32))
        count, dma = len(units), pltpu.SemaphoreType.DMA
        sizes = (1, 1, 1, line, line, line, line, chips, chips, 1, 1)
        return shapes + [dma((count, size)) for size in sizes]

    def peers(self):
        z = [{"dp": self.other(d) * 2 + self.b} for d in range(1, self.line)]
        return z + [self.y_peer]

    def x_peers(self):
        return [
            {"seq": lax.rem(self.chip + d, self.chips) * 2 + self.core}
            for d in range(1, self.chips)
        ]

    def other(self, offset):
        return lax.rem(self.a + offset, self.line)

    def half(self, unit, core):
        half = self.units[unit][2] // 2
        return pl.ds(pl.multiple_of(core * half, 128), half)

    def term(self, unit, row, core):
        lanes = self.half(unit, core)
        if unit == 0:
            return self.small.at[row, :, lanes]
        return self.terms.at[(unit - 1) % SLOTS, row, :, lanes]

    def all_terms(self, unit, core):
        lanes = self.half(unit, core)
        if unit == 0:
            return self.small.at[:, :, lanes]
        return self.terms.at[(unit - 1) % SLOTS, :, :, lanes]

    def send(self, key, src, dst, sems, slot, device):
        unit = key[1]
        copy = remote(
            src, dst, self.sems[sems].at[unit, slot], self.sems[sems + 1].at[unit, slot], device
        )
        copy.start()
        self.flying[key] = copy
        self.sent.setdefault((unit, key[0] in ("core", "y", "z")), []).append(copy)

    def free(self, unit):
        if unit >= 1:
            for copy in self.sent.pop((unit, True), []):
                copy.wait_send()

    def start(self, unit):
        self.send(
            ("core", unit), self.all_terms(unit, 1 - self.core), self.buffers[unit][0], 0, 0, self.core_peer
        )

    def chip_sum(self, unit):
        core_in, y_in = self.buffers[unit][:2]
        self.flying["core", unit].wait_recv()
        for place in range(self.line):
            row = place * 2 + 1 - self.b
            total = self.term(unit, row, self.core)
            total[...] = add(total[...], core_in[row]).astype(jnp.bfloat16)
            self.send(("y", unit, place), total, y_in.at[place], 3, place, self.y_peer)

    def y_sum(self, unit):
        core_in, y_in, z_in = self.buffers[unit][:3]
        for place in range(self.line):
            self.flying["y", unit, place].wait_recv()
        for d in range(1, self.line):
            place = self.other(d)
            row = place * 2 + self.b
            total = self.term(unit, row, self.core)
            total[...] = add(total[...], core_in[row], y_in[place]).astype(jnp.bfloat16)
            self.send(("z", unit, d), total, z_in.at[d], 5, d, {"dp": row})

    def z_sum(self, unit):
        core_in, y_in, z_in, x_out, x_in = self.buffers[unit][:5]
        for d in range(1, self.line):
            self.flying["z", unit, d].wait_recv()
        terms = [self.term(unit, self.rank, self.core)[...], core_in[self.rank], y_in[self.a]]
        terms += [z_in[d] for d in range(1, self.line)]
        x_out[...] = add(*terms).astype(jnp.bfloat16)
        for d, peer in enumerate(self.x_peers()):
            self.send(("x", unit, d), x_out, x_in.at[d], 7, d, peer)

    def x_sum(self, unit):
        x_out, x_in, final = self.buffers[unit][3:]
        for d in range(self.chips - 1):
            self.flying["x", unit, d].wait_recv()
        mine = self.half(unit, self.core)
        final[:, mine] = add(x_out[...], *[x_in[d] for d in range(self.chips - 1)])
        self.send(("f", unit), final.at[:, mine], final.at[:, mine], 9, 0, self.core_peer)

    def finish(self, unit):
        array, rows, columns, row, column = self.units[unit]
        self.flying["f", unit].wait_recv()
        self.sent.pop((unit, False))
        for key in (("f", unit), *[("x", unit, d) for d in range(self.chips - 1)]):
            self.flying[key].wait_send()
        copy = pltpu.make_async_copy(
            self.buffers[unit][5],
            self.outs[array].at[pl.ds(row, rows), pl.ds(column, columns)],
            self.sems[2].at[unit, 0],
        )
        copy.start()
        self.flying["out", unit] = copy

    def drain(self):
        for copies in self.sent.values():
            for copy in copies:
                copy.wait_send()
        for unit in range(len(self.units)):
            self.flying["out", unit].wait()


def add(*terms):
    total = terms[0].astype(jnp.float32)
    for term in terms[1:]:
        total = total + term.astype(jnp.float32)
    return total


class Products:
    def __init__(self, refs, scratch, work, d_packed):
        (
            self.small,
            mixed,
            middle,
            active,
            upstream,
            normed_b,
            d_hidden,
            normed,
            self.second_packed,
        ) = refs
        self.stream, self.keep, self.sems = scratch
        self.work, self.d_packed = work, d_packed
        self.width, self.both = self.stream.shape[1:]
        self.tokens = self.both // 2
        self.mixed, self.active, self.d_hidden = mixed, active, d_hidden
        self.kept = (middle, normed_b, upstream, normed)
        self.flying = {}

    @staticmethod
    def scratch(width, tokens):
        b = jnp.bfloat16
        return [
            pltpu.VMEM((2, width, 2 * tokens), b),
            pltpu.VMEM((4, width, 2 * tokens), b),
            pltpu.SemaphoreType.DMA((32, 2)),
        ]

    def copy(self, key, slot, side, src, dst):
        copy = pltpu.make_async_copy(src, dst, self.sems.at[slot, side])
        copy.start()
        self.flying.setdefault(key, []).append(copy)

    def wait(self, key):
        for copy in self.flying.pop(key, []):
            copy.wait()

    def begin(self):
        self.copy("small", 30, 0, self.small, self.work.small)
        self.fetch(1)
        for index in (0, 2, 1, 3):
            for side in range(2):
                lanes = pl.ds(side * self.tokens, self.tokens)
                self.copy(
                    ("kept", index),
                    20 + index,
                    side,
                    self.kept[index][side],
                    self.keep.at[index, :, lanes],
                )
        self.fetch(2)

    def kind(self, unit):
        array, rows, columns, row, column = self.work.units[unit]
        return array, row // rows, column // columns

    def fetch(self, unit):
        if unit >= len(self.work.units):
            return
        array, row, column = self.kind(unit)
        slot = unit % 2
        for side in range(2):
            lanes = pl.ds(side * self.tokens, self.tokens)
            if array == 1:
                self.copy(unit, unit, side, self.mixed[side], self.stream.at[slot, :, lanes])
            elif array == 3:
                rows = self.work.units[unit][1]
                for rank in range(self.work.dp):
                    pltpu.make_async_copy(
                        self.active[side].at[rank, row],
                        self.stream.at[slot, pl.ds(rank * rows, rows), lanes],
                        self.sems.at[unit, side],
                    ).start()
                all_ranks = pltpu.make_async_copy(
                    self.d_hidden[side].at[pl.ds(0, self.width)],
                    self.stream.at[slot, :, lanes],
                    self.sems.at[unit, side],
                )
                self.flying.setdefault(unit, []).append(all_ranks)
            elif array == 2:
                self.copy(
                    unit,
                    unit,
                    side,
                    self.d_hidden[side].at[pl.ds(column * self.width, self.width)],
                    self.stream.at[slot, :, lanes],
                )
            elif side == 1:
                self.copy(
                    unit,
                    unit,
                    side,
                    self.second_packed.at[pl.ds(column * self.width, self.width)],
                    self.stream.at[slot, :, lanes],
                )

    def make(self, unit):
        work = self.work
        if unit == 0:
            self.wait("small")
            work.start(0)
            return
        array, row, column = self.kind(unit)
        slot = unit % 2
        kept = array - 1
        self.wait(("kept", kept))
        self.wait(unit)
        if array == 4:
            self.stream[slot, :, : self.tokens] = self.d_packed[
                column * self.width : (column + 1) * self.width, :
            ]
        work.free(unit - SLOTS)
        rows = work.units[unit][1]
        ranks = work.dp // 2
        for part in range(2):
            span = slice(part * ranks * rows, (part + 1) * ranks * rows)
            if array in (1, 3):
                product = nt(self.stream[slot, span, :], self.keep[kept])
            else:
                product = nt(self.keep[kept, span, :], self.stream[slot])
            for rank in range(ranks):
                work.terms[(unit - 1) % SLOTS, part * ranks + rank] = product[
                    rank * rows : (rank + 1) * rows, :
                ].astype(jnp.bfloat16)
        work.start(unit)
        self.fetch(unit + 2)


class Pipeline:
    def __init__(self, work, products):
        self.calls = (
            products.make,
            work.chip_sum,
            work.y_sum,
            work.z_sum,
            work.x_sum,
            work.finish,
        )
        self.lags = (0, 1, 2, 1, 1, 1)
        self.done = [0] * len(self.calls)

    def tick(self, limit):
        made = self.done[0]
        if made < limit and made - self.done[3] < SLOTS:
            self.calls[0](made)
            self.done[0] += 1
        full = self.done[0] == limit
        for stage in range(1, len(self.calls)):
            now, ahead = self.done[stage], self.done[stage - 1]
            ready = ahead - now > (0 if full else self.lags[stage])
            full = full and ahead == limit
            if ready:
                self.calls[stage](now)
                self.done[stage] += 1

    def run_out(self, limit):
        while self.done[-1] < limit:
            self.tick(limit)


def causal_mask(size):
    rows = lax.broadcasted_iota(jnp.int32, (size, size), 0)
    columns = lax.broadcasted_iota(jnp.int32, (size, size), 1)
    return rows <= columns


def forward_kernel(seq, dp, sets, units, arrays, heads, *refs):
    refs = list(refs)

    def take(count):
        taken = refs[:count]
        del refs[:count]
        return taken

    (packed,) = take(1)
    earlier = take(sets - 1)
    shards = take(arrays)
    heads_out, mixed_out, own_out, totals_out = take(4)
    wholes = take(arrays)
    arrived, mixed_in, q_s, k_s, v_s, in_send, in_recv, out_send, out_recv = take(9)
    gather = Gather(seq, dp, shards, wholes, units, refs) if units else None

    tokens = packed.shape[1]
    length = tokens * seq
    group = 3 * HEAD_DIM
    me = lax.axis_index("seq")
    peers = seq_peers(seq)
    greet([{"seq": peer} for peer in peers] + (gather.peers() if units else []))

    own_lanes = pl.ds(pl.multiple_of(me * tokens, tokens), tokens)
    copies = {}
    for h in range(heads):
        for d, peer in enumerate(peers):
            copy = remote(
                packed.at[pl.ds(pl.multiple_of((peer * heads + h) * group, group), group)],
                arrived.at[pl.ds(h * group, group), own_lanes],
                in_send.at[h, d],
                in_recv.at[h, d],
                {"seq": peer},
            )
            copy.start()
            copies[h, d] = copy
    steps = []
    if units:
        for unit in range(len(units)):
            gather.start(unit)
        gather.keep_own()
        steps = gather.steps()
        steps.pop(0)()
    for h in range(heads):
        arrived[h * group : (h + 1) * group, own_lanes] = packed[
            pl.ds(pl.multiple_of((me * heads + h) * group, group), group), :
        ]

    mask = causal_mask(tokens)
    for s in range(sets):
        v_s[s, HEAD_DIM:] = jnp.ones((16, length), jnp.bfloat16)
    results = []
    for h in range(heads):
        c0 = h * group
        for s in range(sets):
            source = earlier[s] if s < sets - 1 else arrived
            if s == sets - 1:
                for d in range(seq - 1):
                    copies[h, d].wait_recv()
                heads_out[c0 : c0 + group, :] = arrived[c0 : c0 + group, :]
                q_s[...] = arrived[c0 : c0 + HEAD_DIM, :] * jnp.bfloat16(HEAD_DIM**-0.5)
            k_s[s] = source[c0 + HEAD_DIM : c0 + 2 * HEAD_DIM, :].T
            v_s[s, :HEAD_DIM] = source[c0 + 2 * HEAD_DIM : c0 + 3 * HEAD_DIM, :]

        for i in range(seq):
            queries = q_s[:, i * tokens : (i + 1) * tokens]
            peak = total = None
            for j in [i] + list(range(i)):
                keys = slice(j * tokens, (j + 1) * tokens)
                scores = []
                for s in range(sets):
                    block = nn(k_s[s, keys, :], queries)
                    if j == i:
                        block = jnp.where(mask, block, -1e30)
                    scores.append(block)
                peak_now = peak
                for block in scores:
                    top = jnp.max(block, axis=0, keepdims=True)
                    peak_now = top if peak_now is None else jnp.maximum(peak_now, top)
                if total is not None:
                    total = total * jnp.exp(peak - peak_now)
                for s, block in enumerate(scores):
                    weights = jnp.exp(block - peak_now).astype(jnp.bfloat16)
                    part = nn(v_s[s, :, keys], weights)
                    total = part if total is None else total + part
                peak = peak_now
            row_sum = total[HEAD_DIM : HEAD_DIM + 1]
            own_out[h * HEAD_DIM : (h + 1) * HEAD_DIM, i * tokens : (i + 1) * tokens] = (
                total[:HEAD_DIM] / row_sum
            ).astype(jnp.bfloat16)
            totals_out[h, :, i * tokens : (i + 1) * tokens] = peak + jnp.log(row_sum)
            if steps:
                steps.pop(0)()

        mine = pl.ds(pl.multiple_of((me * heads + h) * HEAD_DIM, HEAD_DIM), HEAD_DIM)
        for d, peer in enumerate(peers):
            copy = remote(
                own_out.at[
                    pl.ds(h * HEAD_DIM, HEAD_DIM),
                    pl.ds(pl.multiple_of(peer * tokens, tokens), tokens),
                ],
                mixed_in.at[mine],
                out_send.at[h, d],
                out_recv.at[h, d],
                {"seq": peer},
            )
            copy.start()
            results.append(copy)
        mixed_in[mine] = own_out[h * HEAD_DIM : (h + 1) * HEAD_DIM, own_lanes]
    for step in steps:
        step()
    if units:
        gather.finish()
    for copy in copies.values():
        copy.wait_send()
    for copy in results:
        copy.wait()
    mixed_out[...] = mixed_in[...]


def attend_forward(seq, dp, heads, packed, earlier, shards, call_id):
    width, tokens = packed.shape
    length = tokens * seq
    sets, arrays = 1 + len(earlier), len(shards)
    units = later_units(shards) if arrays else []
    rows = heads * 3 * HEAD_DIM
    vmem = pl.BlockSpec(memory_space=pltpu.VMEM)
    hbm = pl.BlockSpec(memory_space=pl.ANY)
    dma = pltpu.SemaphoreType.DMA
    outs = pl.pallas_call(
        functools.partial(forward_kernel, seq, dp, sets, units, arrays, heads),
        out_shape=(
            jax.ShapeDtypeStruct((rows, length), jnp.bfloat16),
            jax.ShapeDtypeStruct((width // 3, tokens), jnp.bfloat16),
            jax.ShapeDtypeStruct((heads * HEAD_DIM, length), jnp.bfloat16),
            jax.ShapeDtypeStruct((heads, 1, length), jnp.float32),
        )
        + tuple(whole_shape(shard, dp) for shard in shards),
        in_specs=[vmem] * sets + [hbm] * arrays,
        out_specs=(vmem,) * 4 + (hbm,) * arrays,
        scratch_shapes=[
            pltpu.VMEM((rows, length), jnp.bfloat16),
            pltpu.VMEM((width // 3, tokens), jnp.bfloat16),
            pltpu.VMEM((HEAD_DIM, length), jnp.bfloat16),
            pltpu.VMEM((sets, length, HEAD_DIM), jnp.bfloat16),
            pltpu.VMEM((sets, HEAD_DIM + 16, length), jnp.bfloat16),
            dma((heads, seq)),
            dma((heads, seq)),
            dma((heads, seq)),
            dma((heads, seq)),
        ]
        + (Gather.scratch(arrays, len(units), dp) if units else []),
        compiler_params=pltpu.CompilerParams(
            collective_id=call_id, has_side_effects=True, vmem_limit_bytes=40 << 20
        ),
        name=f"attend_forward_{sets}",
    )(packed, *earlier, *shards)
    return outs[:4], outs[4:]


def backward_kernel(seq, dp, sets, units, heads, *refs):
    refs = list(refs)

    def take(count):
        taken = refs[:count]
        del refs[:count]
        return taken

    (d_mixed,) = take(1)
    packs = take(sets)
    own_in, totals_in = take(2)
    if units:
        (carry_in, small) = take(2)
        pairs = [take(2) for _ in range(7)]
        (second_packed,) = take(1)
    (d_packed_out,) = take(1)
    carry_out = None if units else take(1)[0]
    grads_out = take(5) if units else []
    arrived, local_grad, d_packed_in, q_s, k_s, kt_s, v_s, delta_s, dq_s, dkv_s = take(10)
    in_send, in_recv, out_send, out_recv, out_sem = take(5)
    if units:
        carry_s, carry_sem = take(2)
        product_scratch = take(3)
        work = Scatter(seq, dp, units, grads_out, refs)
        products = Products([small] + pairs + [second_packed], product_scratch, work, d_packed_in)

    tokens = d_mixed.shape[1]
    length = tokens * seq
    group = 3 * HEAD_DIM
    me = lax.axis_index("seq")
    peers = seq_peers(seq)
    greet([{"seq": peer} for peer in peers] + (work.peers() if units else []))
    own_lanes = pl.ds(pl.multiple_of(me * tokens, tokens), tokens)
    scale = jnp.bfloat16(HEAD_DIM**-0.5)

    copies = {}
    for h in range(heads):
        for d, peer in enumerate(peers):
            copy = remote(
                d_mixed.at[pl.ds(pl.multiple_of((peer * heads + h) * HEAD_DIM, HEAD_DIM), HEAD_DIM)],
                arrived.at[pl.ds(h * HEAD_DIM, HEAD_DIM), own_lanes],
                in_send.at[h, d],
                in_recv.at[h, d],
                {"seq": peer},
            )
            copy.start()
            copies[h, d] = copy
    if units:
        products.begin()
        pipeline = Pipeline(work, products)
        early = [unit[0] for unit in units].index(4)
    for h in range(heads):
        arrived[h * HEAD_DIM : (h + 1) * HEAD_DIM, own_lanes] = d_mixed[
            pl.ds(pl.multiple_of((me * heads + h) * HEAD_DIM, HEAD_DIM), HEAD_DIM), :
        ]

    def outgoing(h, rank, send_slot):
        return remote(
            local_grad.at[
                pl.ds(h * group, group), pl.ds(pl.multiple_of(rank * tokens, tokens), tokens)
            ],
            d_packed_in.at[pl.ds(pl.multiple_of((me * heads + h) * group, group), group)],
            out_send.at[h, send_slot],
            out_recv.at[h, me],
            {"seq": rank},
        )

    if units:
        pipeline.tick(early)
        pipeline.tick(early)
    mask = causal_mask(tokens)
    hook = 0
    for h in range(heads):
        c0 = h * group
        r0 = h * HEAD_DIM
        if units:
            carried = pltpu.make_async_copy(carry_in.at[h], carry_s, carry_sem.at[h])
            carried.start()
        q_s[...] = packs[-1][c0 : c0 + HEAD_DIM, :] * scale
        for s in range(sets):
            keys = packs[s][c0 + HEAD_DIM : c0 + 2 * HEAD_DIM, :]
            k_s[s] = keys.T
            kt_s[s] = keys * scale
            v_s[s] = packs[s][c0 + 2 * HEAD_DIM : c0 + 3 * HEAD_DIM, :].T
        for d in range(seq - 1):
            copies[h, d].wait_recv()
        delta_s[...] = jnp.sum(
            arrived[r0 : r0 + HEAD_DIM, :].astype(jnp.float32)
            * own_in[r0 : r0 + HEAD_DIM, :].astype(jnp.float32),
            axis=0,
            keepdims=True,
        )
        if units:
            carried.wait()
        for j in range(seq):
            keys = slice(j * tokens, (j + 1) * tokens)
            for i in range(j, seq):
                span = slice(i * tokens, (i + 1) * tokens)
                queries = q_s[:, span]
                grads = arrived[r0 : r0 + HEAD_DIM, span]
                d_query = dq_s[:, span] if j > 0 else None
                for s in range(sets):
                    chances = jnp.exp(nn(k_s[s, keys, :], queries) - totals_in[h, :, span])
                    if i == j:
                        chances = jnp.where(mask, chances, 0.0)
                    d_chance = nn(v_s[s, keys, :], grads)
                    d_score = (chances * (d_chance - delta_s[:, span])).astype(jnp.bfloat16)
                    d_key = nt(queries, d_score)
                    d_value = nt(grads, chances.astype(jnp.bfloat16))
                    if i == j:
                        if units:
                            d_key = d_key + carry_s[:HEAD_DIM, keys]
                            d_value = d_value + carry_s[HEAD_DIM:, keys]
                        dkv_s[s, :HEAD_DIM, keys] = d_key
                        dkv_s[s, HEAD_DIM:, keys] = d_value
                    else:
                        dkv_s[s, :HEAD_DIM, keys] += d_key
                        dkv_s[s, HEAD_DIM:, keys] += d_value
                    part = nn(kt_s[s, :, keys], d_score)
                    d_query = part if d_query is None else d_query + part
                dq_s[:, span] = d_query
                hook += 1
                if units and hook % EVERY == 0:
                    pipeline.tick(early)
            local_grad[c0 : c0 + HEAD_DIM, keys] = dq_s[:, keys].astype(jnp.bfloat16)
            local_grad[c0 + HEAD_DIM : c0 + group, keys] = dkv_s[sets - 1, :, keys].astype(
                jnp.bfloat16
            )
            if h == heads - 1:

                @pl.when(me != j)
                def _():
                    outgoing(h, jnp.int32(j), j).start()

        if not units:
            carry_out[h] = dkv_s[0]
        if h < heads - 1:
            for d, peer in enumerate(peers):
                outgoing(h, peer, d).start()
        d_packed_in[pl.ds(pl.multiple_of((me * heads + h) * group, group), group)] = local_grad[
            c0 : c0 + group, own_lanes
        ]
    for h in range(heads):
        for peer in peers:
            remote(
                local_grad.at[pl.ds(h * group, group), own_lanes],
                d_packed_in.at[pl.ds(pl.multiple_of((peer * heads + h) * group, group), group)],
                out_send.at[h, 0],
                out_recv.at[h, peer],
                {"seq": peer},
            ).wait_recv()
    finished = pltpu.make_async_copy(d_packed_in, d_packed_out, out_sem.at[0])
    finished.start()
    if units:
        pipeline.run_out(len(units))
        work.drain()
    for copy in copies.values():
        copy.wait_send()
    for h in range(heads - 1):
        for d, peer in enumerate(peers):
            outgoing(h, peer, d).wait_send()
    for j in range(seq):

        @pl.when(me != j)
        def _():
            outgoing(heads - 1, jnp.int32(j), j).wait_send()

    finished.wait()


def attend_backward(seq, dp, heads, d_mixed, packs, own, totals, extra, units, call_id):
    width, tokens = d_mixed.shape
    length = tokens * seq
    sets = len(packs)
    rows = heads * 3 * HEAD_DIM
    vmem = pl.BlockSpec(memory_space=pltpu.VMEM)
    hbm = pl.BlockSpec(memory_space=pl.ANY)
    dma = pltpu.SemaphoreType.DMA
    f32 = jnp.float32
    out_shape = [jax.ShapeDtypeStruct((3 * width, tokens), jnp.bfloat16)]
    out_specs = [hbm]
    more = []
    if units:
        heights = [0] * 5
        for array, high, wide, row, column in units:
            heights[array] = max(heights[array], row + high)
        widths = [0] * 5
        for array, high, wide, row, column in units:
            widths[array] = max(widths[array], column + wide)
        out_shape += [jax.ShapeDtypeStruct(shape, f32) for shape in zip(heights, widths)]
        out_specs += [hbm] * 5
        more = [pltpu.VMEM((2 * HEAD_DIM, length), f32), dma((heads,))]
        more += Products.scratch(width, tokens) + Scatter.scratch(seq, dp, units)
    else:
        out_shape.append(jax.ShapeDtypeStruct((heads, 2 * HEAD_DIM, length), f32))
        out_specs.append(vmem)
    return pl.pallas_call(
        functools.partial(backward_kernel, seq, dp, sets, units, heads),
        out_shape=tuple(out_shape),
        in_specs=[vmem] * (3 + sets) + [hbm] * len(extra),
        out_specs=tuple(out_specs),
        scratch_shapes=[
            pltpu.VMEM((heads * HEAD_DIM, length), jnp.bfloat16),
            pltpu.VMEM((rows, length), jnp.bfloat16),
            pltpu.VMEM((3 * width, tokens), jnp.bfloat16),
            pltpu.VMEM((HEAD_DIM, length), jnp.bfloat16),
            pltpu.VMEM((sets, length, HEAD_DIM), jnp.bfloat16),
            pltpu.VMEM((sets, HEAD_DIM, length), jnp.bfloat16),
            pltpu.VMEM((sets, length, HEAD_DIM), jnp.bfloat16),
            pltpu.VMEM((1, length), f32),
            pltpu.VMEM((HEAD_DIM, length), f32),
            pltpu.VMEM((sets, 2 * HEAD_DIM, length), f32),
            dma((heads, seq)),
            dma((heads, seq)),
            dma((heads, seq)),
            dma((heads, seq)),
            dma((1,)),
        ]
        + more,
        compiler_params=pltpu.CompilerParams(
            collective_id=call_id, has_side_effects=True, vmem_limit_bytes=60 << 20
        ),
        name=f"attend_backward_{sets}",
    )(d_mixed, *packs, own, totals, *extra)


def column(row):
    return jnp.broadcast_to(row, (8, row.shape[1])).T[:, :1]


def norm_unit(rows):
    centre = rows - jnp.mean(rows, axis=0, keepdims=True)
    inverse = lax.rsqrt(jnp.mean(centre * centre, axis=0, keepdims=True) + epsilon)
    return centre * inverse, inverse


def norm_backward(unit, inverse, gain, grad):
    grad = grad * gain
    share = jnp.mean(grad * unit, axis=0, keepdims=True)
    return inverse * (grad - jnp.mean(grad, axis=0, keepdims=True) - unit * share)


def gelu_slope(hidden):
    root = (2.0 / math.pi) ** 0.5
    square = hidden * hidden
    bend = jnp.tanh(root * hidden * (1.0 + 0.044715 * square))
    inner = (0.5 * root) * hidden * (1.0 + 3 * 0.044715 * square)
    return 0.5 * (1.0 + bend) + inner * (1.0 - bend * bend)


def dense_kernel(first, mlp, chunks, *refs):
    refs = list(refs)

    def take(count):
        taken = refs[:count]
        del refs[:count]
        return taken

    both = first * mlp
    count = 5 * first + (1 - first) + 6 * mlp + both
    sources = take(count)
    results = take(1 - mlp + mlp * 5 + both * 4)
    places = take(count)
    sems, out_sems = take(2)
    fetched = [
        pltpu.make_async_copy(source, place, sems.at[index])
        for index, (source, place) in enumerate(zip(sources, places))
    ]
    for copy in fetched:
        copy.start()

    def get(index):
        fetched[index].wait()
        return places[index]

    sent = []

    def put(place, result):
        copy = pltpu.make_async_copy(place, result, out_sems.at[len(sent)])
        copy.start()
        sent.append(copy)

    if first:
        grad = nn(get(1)[...], get(0)[...])
        unit, inverse = norm_unit(get(2)[...].T)
        gain_a = column(get(4)[...])
        upstream = get(3)[...] + norm_backward(unit, inverse, gain_a, grad)
    else:
        upstream = get(0)[...].astype(jnp.float32)
    if not mlp:
        (out_s,) = refs
        out_s[...] = upstream.T
        put(out_s, results[0])
    else:
        base = 5 * first + (1 - first)
        middle, hidden, down_w, up_w, out_w, gain = range(base, base + 6)
        hidden_s, grad_s, middle_s, mixed_s, normed_s, up_s, rounded_s = refs[:7]
        up_s[...] = upstream
        rounded_s[...] = upstream.astype(jnp.bfloat16)
        if first:
            first_s, second_s = refs[7:]
            rounded_out, sum_out, first_out, second_out = results[5:]
            put(rounded_s, rounded_out)
            sum_out[...] = jnp.sum(upstream, axis=1, keepdims=True)
            second_s[...] = (unit * gain_a).astype(jnp.bfloat16)
            put(second_s, second_out)
        size = places[hidden].shape[0] // chunks
        get(down_w)
        get(hidden)
        total = None
        for chunk in range(chunks):
            span = slice(chunk * size, (chunk + 1) * size)
            d_active = nn(places[down_w][span, :], rounded_s[...])
            hidden_s[span, :] = (d_active * gelu_slope(places[hidden][span, :])).astype(jnp.bfloat16)
            put(hidden_s.at[span], results[0].at[span])
            if chunk == 0:
                get(up_w)
            part = nn(places[up_w][:, span], hidden_s[span, :])
            total = part if total is None else total + part
        unit, inverse = norm_unit(get(middle)[...].T)
        gain_b = column(get(gain)[...])
        d_middle = up_s[...] + norm_backward(unit, inverse, gain_b, total)
        grad_s[...] = d_middle
        middle_s[...] = d_middle.astype(jnp.bfloat16)
        normed_s[...] = (unit * gain_b).astype(jnp.bfloat16)
        put(grad_s, results[1])
        put(middle_s, results[2])
        put(normed_s, results[4])
        mixed_s[...] = nn(get(out_w)[...], middle_s[...]).astype(jnp.bfloat16)
        put(mixed_s, results[3])
        if first:
            first_s[...] = (norm_unit(get(base + 6)[...].T)[0] * gain_a).astype(jnp.bfloat16)
            put(first_s, first_out)
    for copy in sent:
        copy.wait()


def dense_backward(before, after):
    first, mlp = int(len(before) > 1), int(len(after) > 0)
    args = list(before) + list(after)
    width, tokens = (before[3] if first else before[0]).shape
    hbm = pl.BlockSpec(memory_space=pl.ANY)
    b, f32 = jnp.bfloat16, jnp.float32
    chunks, outs, specs, more = 1, [jax.ShapeDtypeStruct((tokens, width), f32)], [hbm], []
    flops = 6 * width * width * tokens * first
    if mlp:
        ff = after[1].shape[0]
        chunks = ff // width
        flops += 2 * tokens * width * (2 * ff + width)
        flat = (width, tokens)
        shapes = [((ff, tokens), b), (flat, f32), (flat, b), (flat, b), (flat, b)]
        more = [pltpu.VMEM(shape, kind) for shape, kind in shapes]
        more += [pltpu.VMEM(flat, f32), pltpu.VMEM(flat, b)]
        outs = [jax.ShapeDtypeStruct(shape, kind) for shape, kind in shapes]
        specs = [hbm] * 5
        if first:
            more += [pltpu.VMEM(flat, b)] * 2
            outs += [jax.ShapeDtypeStruct(flat, b), jax.ShapeDtypeStruct((width, 1), f32)]
            outs += [jax.ShapeDtypeStruct(flat, b)] * 2
            specs += [hbm, pl.BlockSpec(memory_space=pltpu.VMEM), hbm, hbm]
    else:
        more = [pltpu.VMEM((tokens, width), f32)]
    return pl.pallas_call(
        functools.partial(dense_kernel, first, mlp, chunks),
        out_shape=tuple(outs),
        in_specs=[hbm] * len(args),
        out_specs=tuple(specs),
        scratch_shapes=[pltpu.VMEM(arg.shape, arg.dtype) for arg in args]
        + [pltpu.SemaphoreType.DMA((len(args),)), pltpu.SemaphoreType.DMA((16,))]
        + more,
        compiler_params=pltpu.CompilerParams(vmem_limit_bytes=58 << 20),
        cost_estimate=pl.CostEstimate(flops=flops, bytes_accessed=24 << 20, transcendentals=0),
        name=f"dense_backward_{first}{mlp}",
    )(*args)


def dots(left, right, left_side, right_side):
    return lax.dot_general(
        left,
        right,
        (((left_side,), (right_side,)), ((), ())),
        preferred_element_type=jnp.float32,
    )


def norm_rows(rows, gain):
    centre = rows - jnp.mean(rows, axis=1, keepdims=True)
    spread = jnp.mean(centre * centre, axis=1, keepdims=True)
    return (centre * lax.rsqrt(spread + epsilon) * gain).astype(jnp.bfloat16)


def block_forward(sizes, call_id, stream, qkv_w, gains, earlier, weights, shards):
    seq, dp, heads = sizes
    normed = norm_rows(stream, gains[0])
    packed = dots(qkv_w, normed, 0, 1).astype(jnp.bfloat16)
    (head_rows, mixed, own, totals), gathered = attend_forward(
        seq, dp, heads, packed, earlier, shards, call_id
    )
    out_w, up_w, down_w = weights or gathered
    middle = stream + dots(mixed, out_w, 0, 0)
    normed_b = norm_rows(middle, gains[1])
    hidden = dots(up_w, normed_b, 0, 1)
    active = jax.nn.gelu(hidden, approximate=True).astype(jnp.bfloat16)
    result = middle + dots(active, down_w, 0, 0)
    packs = earlier + [head_rows]
    stored = (stream, packs, own, totals, mixed, middle, hidden, active)
    return result, stored, (out_w, up_w, down_w)


def block_backward(sizes, call_id, before, stored, gains, weights, second):
    seq, dp, heads = sizes
    out_w, up_w, down_w = weights
    stream, packs, own, totals, mixed, middle, hidden, active = stored
    after = (middle, hidden, down_w, up_w, out_w, gains[1])
    done = dense_backward(before, after if second is None else after + (stream,))
    d_hidden, d_middle, middle_bf, d_mixed, normed_b = done[:5]
    width, tokens = d_mixed.shape
    rows = width // dp
    active = active.reshape(dp, active.shape[0] // width, rows, tokens)
    upstream = before[0] if second is None else done[5]
    factors = [mixed, middle_bf, active, upstream, normed_b, d_hidden]
    extra, units = [], []
    if second is not None:
        passed, second_factors, second_packed = second
        embed = done[6].astype(jnp.bfloat16).reshape(dp, 1, rows)
        factors, second_factors = factors + [done[7]], second_factors + [done[8]]
        extra = [passed, jnp.pad(embed, ((0, 0), (0, 7), (0, 256 - rows)))]
        for pair in zip(factors, second_factors):
            extra += pair
        extra.append(second_packed)
        ff = d_hidden.shape[0]
        units = [(0, 8, 256, 0, 0)]
        units += [(1, rows, width, 0, 0)]
        units += [(3, rows, width, row, 0) for row in range(0, ff // dp, rows)]
        units += [(2, rows, width, 0, column) for column in range(0, ff, width)]
        units += [(4, rows, width, 0, column) for column in range(0, 3 * width, width)]
    outs = attend_backward(seq, dp, heads, d_mixed, packs, own, totals, extra, units, call_id)
    return (stream, d_middle), factors, outs


def local(
    seq,
    dp,
    tokens,
    qkv_weight,
    out_weight,
    up_weight,
    down_weight,
    norm_gain,
    mlp_gain,
    pass_embed,
    cotangent,
):
    share = norm_gain.shape[0]
    lanes = [
        jnp.pad(v.reshape(1, share), ((0, 0), (0, 128 - share)))
        for v in (norm_gain, pass_embed, mlp_gain)
    ]
    small = jnp.concatenate(
        [
            jnp.concatenate(lanes[:2], axis=1),
            jnp.pad(lanes[2], ((0, 0), (0, 128))),
            jnp.zeros((6, 256), jnp.bfloat16),
        ]
    )
    qkv_w, small = gather_now(seq, dp, [qkv_weight, small])
    small = small.reshape(dp, 8, 256)
    gains = [small[:, row, :share].reshape(1, -1).astype(jnp.float32) for row in (0, 1)]
    embedding = small[:, 0, 128 : 128 + share].reshape(1, -1).astype(jnp.float32)
    heads = qkv_weight.shape[1] // (3 * HEAD_DIM * seq)
    sizes = (seq, dp, heads)
    first_out, first_kept, weights = block_forward(
        sizes,
        1,
        tokens[0].astype(jnp.float32),
        qkv_w,
        gains,
        [],
        None,
        [out_weight, up_weight, down_weight],
    )
    second_out, second_kept, weights = block_forward(
        sizes, 2, first_out + embedding, qkv_w, gains, [first_kept[1][0]], weights, []
    )
    (stream, d_middle), factors, outs = block_backward(
        sizes, 3, (cotangent[0].T,), second_kept, gains, weights, None
    )
    second = (outs[1], factors, outs[0])
    before = (outs[0], qkv_w, stream, d_middle, gains[0])
    (stream, d_middle), factors, outs = block_backward(
        sizes, 4, before, first_kept, gains, weights, second
    )
    d_first = dense_backward((outs[0], qkv_w, stream, d_middle, gains[0]), ())[0]
    packed, small, out_grad, up_grad, down_grad, qkv_grad = outs
    f32 = jnp.float32
    gain_a = jnp.sum(qkv_weight.astype(f32) * qkv_grad, axis=1) / norm_gain.astype(f32)
    gain_b = jnp.sum(up_weight.astype(f32) * up_grad, axis=1) / mlp_gain.astype(f32)
    return (
        second_out.astype(jnp.bfloat16)[None],
        d_first[None],
        qkv_grad,
        out_grad,
        up_grad,
        down_grad,
        gain_a,
        gain_b,
        small[0, :share],
    )


def solution(mesh):
    in_specs = (
        P("dp", "seq", None),
        P("dp", None),
        P("dp", None),
        P("dp", None),
        P("dp", None),
        P("dp"),
        P("dp"),
        P("dp"),
        P("dp", "seq", None),
    )
    out_specs = (
        P("dp", "seq", None),
        P("dp", "seq", None),
        P("dp", None),
        P("dp", None),
        P("dp", None),
        P("dp", None),
        P("dp"),
        P("dp"),
        P("dp"),
    )
    return jax.shard_map(
        functools.partial(local, mesh.shape["seq"], mesh.shape["dp"]), mesh=mesh, in_specs=in_specs, out_specs=out_specs, check_vma=False)
```

```python
import functools
import math

import jax
import jax.numpy as jnp
from jax import lax
from jax.experimental import pallas as pl
from jax.experimental.pallas import tpu as pltpu
from jax.sharding import PartitionSpec as P

HEAD_DIM = 64
CHUNK = 768
EVERY = 3
SLOTS = 6
PAIRS = 2
AHEAD = 2


epsilon = 1e-05


def nt(left, right):
    return lax.dot_general(
        left, right, (((1,), (1,)), ((), ())), preferred_element_type=jnp.float32
    )


def nn(left, right):
    return lax.dot_general(
        left, right, (((1,), (0,)), ((), ())), preferred_element_type=jnp.float32
    )


def remote(src, dst, send_sem, recv_sem, device):
    return pltpu.make_async_remote_copy(
        src_ref=src,
        dst_ref=dst,
        send_sem=send_sem,
        recv_sem=recv_sem,
        device_id=device,
        device_id_type=pl.DeviceIdType.MESH,
    )


def greet(devices):
    barrier = pltpu.get_barrier_semaphore()
    for device in devices:
        pl.semaphore_signal(
            barrier, inc=1, device_id=device, device_id_type=pl.DeviceIdType.MESH
        )
    pl.semaphore_wait(barrier, len(devices))


def seq_peers(seq):
    me = lax.axis_index("seq")
    return [lax.rem(me + d, seq) for d in range(1, seq)]


class Gather:
    def __init__(self, seq, dp, shards, wholes, units, sems):
        self.line = dp // 2
        self.shards, self.wholes, self.units, self.sems = shards, wholes, units, sems
        me = lax.axis_index("seq")
        self.core, self.chip = lax.rem(me, 2), lax.div(me, 2)
        self.core_peer = {"seq": me + 1 - 2 * self.core}
        self.x_peer = {"seq": self.core + 2 - 2 * self.chip}
        self.rank = lax.axis_index("dp")
        self.a, self.b = lax.div(self.rank, 2), lax.rem(self.rank, 2)
        self.y_peer = {"dp": self.a * 2 + 1 - self.b}
        self.flying, self.sent = {}, []

    @staticmethod
    def scratch(arrays, units, dp):
        line, dma = dp // 2, pltpu.SemaphoreType.DMA
        sizes = (line, line, line, line, 2 * line, 2 * line, 2 * line, 2 * line, 2 * line, 2 * line)
        return [dma((units, size)) for size in sizes] + [dma((arrays,))]

    def z_rank(self, offset):
        return lax.rem(self.a + offset, self.line) * 2 + self.b

    def peers(self):
        z = [{"dp": self.z_rank(d)} for d in range(1, self.line)]
        return z + [self.y_peer]

    def shared(self, unit):
        return sum(self.units[unit][5:]) > 0

    def place(self, unit, first, chip):
        array, row, rows, column, columns, row_step, column_step = self.units[unit]
        half = columns // 2
        start = first + row
        side = column + self.core * half
        if row_step:
            start = start + chip * row_step
        if column_step:
            side = side + chip * column_step
        if not isinstance(start, int):
            start = pl.multiple_of(start, 8)
        return pl.ds(start, rows), pl.ds(pl.multiple_of(side, 128), half)

    def block(self, unit, rank, chip):
        array = self.units[unit][0]
        return self.wholes[array].at[self.place(unit, rank * self.shards[array].shape[0], chip)]

    def send(self, kind, unit, slot, src, dst, device):
        sems = {"z": 0, "y": 2, "core": 4, "x": 6, "core2": 8}[kind]
        copy = remote(
            src, dst, self.sems[sems].at[unit, slot], self.sems[sems + 1].at[unit, slot], device
        )
        copy.start()
        self.flying[kind, unit, slot] = copy
        self.sent.append(copy)

    def keep_own(self):
        for array, (shard, whole) in enumerate(zip(self.shards, self.wholes)):
            rows = shard.shape[0]
            copy = pltpu.make_async_copy(
                shard,
                whole.at[pl.ds(pl.multiple_of(self.rank * rows, 8), rows)],
                self.sems[10].at[array],
            )
            copy.start()
            self.flying["own", array] = copy

    def start(self, unit):
        array = self.units[unit][0]
        mine = self.shards[array].at[self.place(unit, 0, self.chip)]
        there = self.block(unit, self.rank, self.chip)
        for d in range(1, self.line):
            self.send("z", unit, d, mine, there, {"dp": self.z_rank(d)})
        self.send("y", unit, 0, mine, there, self.y_peer)

    def spread(self, unit, slot, rank):
        block = self.block(unit, rank, self.chip)
        if self.shared(unit):
            self.send("x", unit, slot, block, block, self.x_peer)
        self.send("core", unit, slot, block, block, self.core_peer)

    def forward_z(self, unit):
        for d in range(1, self.line):
            self.flying["z", unit, d].wait_recv()
            rank = self.z_rank(self.line - d)
            block = self.block(unit, rank, self.chip)
            self.send("y", unit, d, block, block, self.y_peer)
            self.spread(unit, d, rank)

    def y_rank(self, d):
        return lax.rem(self.a + self.line - d, self.line) * 2 + 1 - self.b

    def forward_y(self, unit):
        for d in range(self.line):
            self.flying["y", unit, d].wait_recv()
            self.spread(unit, self.line + d, self.y_rank(d))

    def forward_x(self, unit):
        if not self.shared(unit):
            return
        for slot in range(1, 2 * self.line):
            self.flying["x", unit, slot].wait_recv()
            d = slot % self.line
            rank = self.y_rank(d) if slot >= self.line else self.z_rank(self.line - d)
            block = self.block(unit, rank, 1 - self.chip)
            self.send("core2", unit, slot, block, block, self.core_peer)

    def finish(self):
        for unit in range(len(self.units)):
            for slot in range(1, 2 * self.line):
                self.flying["core", unit, slot].wait_recv()
                if self.shared(unit):
                    self.flying["core2", unit, slot].wait_recv()
        for array in range(len(self.shards)):
            self.flying["own", array].wait()
        for copy in self.sent:
            copy.wait_send()

    def steps(self):
        count, calls = len(self.units), []
        for step in range(count + 2):
            for call, unit in (
                (self.forward_z, step),
                (self.forward_y, step - 1),
                (self.forward_x, step - 2),
            ):
                if 0 <= unit < count:
                    calls.append(functools.partial(call, unit))
        return calls


def first_units(shards):
    (rows, wide), small = shards[0].shape, shards[1].shape
    units = [(0, 0, rows, 0, CHUNK, 0, CHUNK)]
    units += [(0, 0, rows, column, CHUNK, 0, 0) for column in range(2 * CHUNK, wide, CHUNK)]
    return units + [(1, 0, small[0], 0, small[1], 0, 0)]


def later_units(shards):
    (rows, width), (_, up_wide), (down_rows, _) = [shard.shape for shard in shards]
    ups = [(1, 0, rows, column, CHUNK, 0, 0) for column in range(0, up_wide, CHUNK)]
    shared = 2 * PAIRS * rows
    pairs = [(2, row, rows, 0, width, rows, 0) for row in range(0, shared, 2 * rows)]
    downs = [(2, row, rows, 0, width, 0, 0) for row in range(shared, down_rows, rows)]
    return [(0, 0, rows, 0, width, 0, 0)] + ups[:1] + pairs[:1] + ups[1:3] + pairs[1:] + ups[3:] + downs


def gather_kernel(seq, dp, units, arrays, *refs):
    shards, wholes, sems = refs[:arrays], refs[arrays : 2 * arrays], refs[2 * arrays :]
    gather = Gather(seq, dp, shards, wholes, units, sems)
    greet(gather.peers() + [gather.core_peer, gather.x_peer])
    for unit in range(len(units)):
        gather.start(unit)
    gather.keep_own()
    for call in gather.steps():
        call()
    gather.finish()


def whole_shape(shard, dp):
    return jax.ShapeDtypeStruct((shard.shape[0] * dp, shard.shape[1]), shard.dtype)


def gather_now(seq, dp, shards):
    arrays = len(shards)
    units = first_units(shards)
    hbm = pl.BlockSpec(memory_space=pl.ANY)
    return pl.pallas_call(
        functools.partial(gather_kernel, seq, dp, units, arrays),
        out_shape=tuple(whole_shape(shard, dp) for shard in shards),
        in_specs=[hbm] * arrays,
        out_specs=(hbm,) * arrays,
        scratch_shapes=Gather.scratch(arrays, len(units), dp),
        compiler_params=pltpu.CompilerParams(
            collective_id=0, has_side_effects=True, vmem_limit_bytes=4 << 20
        ),
        name="gather_first",
    )(*shards)


class Scatter:
    def __init__(self, seq, dp, units, outs, scratch):
        self.seq, self.dp, self.line, self.chips = seq, dp, dp // 2, seq // 2
        self.units, self.outs = units, outs
        me = lax.axis_index("seq")
        self.core, self.chip = lax.rem(me, 2), lax.div(me, 2)
        self.core_peer = {"seq": me + 1 - 2 * self.core}
        self.rank = lax.axis_index("dp")
        self.a, self.b = lax.div(self.rank, 2), lax.rem(self.rank, 2)
        self.y_peer = {"dp": self.a * 2 + 1 - self.b}
        count = len(units)
        self.small, self.terms = scratch[0], scratch[1]
        self.buffers = [scratch[2 + 6 * u : 8 + 6 * u] for u in range(count)]
        self.sems = scratch[2 + 6 * count :]
        self.flying, self.sent = {}, {}

    @staticmethod
    def scratch(seq, dp, units):
        line, chips, b = dp // 2, seq // 2, jnp.bfloat16
        rows, columns = units[1][1:3]
        shapes = [
            pltpu.VMEM((dp,) + units[0][1:3], b),
            pltpu.VMEM((SLOTS, dp, rows, columns), b),
        ]
        for unit in units:
            rows, half = unit[1], unit[2] // 2
            for lead in ((dp,), (line,), (line,), (), (chips,)):
                shapes.append(pltpu.VMEM(lead + (rows, half), b))
            shapes.append(pltpu.VMEM((rows, 2 * half), jnp.float32))
        count, dma = len(units), pltpu.SemaphoreType.DMA
        sizes = (1, 1, 1, line, line, line, line, chips, chips, 1, 1)
        return shapes + [dma((count, size)) for size in sizes]

    def peers(self):
        z = [{"dp": self.other(d) * 2 + self.b} for d in range(1, self.line)]
        return z + [self.y_peer]

    def x_peers(self):
        return [
            {"seq": lax.rem(self.chip + d, self.chips) * 2 + self.core}
            for d in range(1, self.chips)
        ]

    def other(self, offset):
        return lax.rem(self.a + offset, self.line)

    def half(self, unit, core):
        half = self.units[unit][2] // 2
        return pl.ds(pl.multiple_of(core * half, 128), half)

    def term(self, unit, row, core):
        lanes = self.half(unit, core)
        if unit == 0:
            return self.small.at[row, :, lanes]
        return self.terms.at[(unit - 1) % SLOTS, row, :, lanes]

    def all_terms(self, unit, core):
        lanes = self.half(unit, core)
        if unit == 0:
            return self.small.at[:, :, lanes]
        return self.terms.at[(unit - 1) % SLOTS, :, :, lanes]

    def send(self, key, src, dst, sems, slot, device):
        unit = key[1]
        copy = remote(
            src, dst, self.sems[sems].at[unit, slot], self.sems[sems + 1].at[unit, slot], device
        )
        copy.start()
        self.flying[key] = copy
        self.sent.setdefault((unit, key[0] in ("core", "y", "z")), []).append(copy)

    def free(self, unit):
        if unit >= 1:
            for copy in self.sent.pop((unit, True), []):
                copy.wait_send()

    def start(self, unit):
        self.send(
            ("core", unit), self.all_terms(unit, 1 - self.core), self.buffers[unit][0], 0, 0, self.core_peer
        )

    def chip_sum(self, unit):
        core_in, y_in = self.buffers[unit][:2]
        self.flying["core", unit].wait_recv()
        for place in range(self.line):
            row = place * 2 + 1 - self.b
            total = self.term(unit, row, self.core)
            total[...] = add(total[...], core_in[row]).astype(jnp.bfloat16)
            self.send(("y", unit, place), total, y_in.at[place], 3, place, self.y_peer)

    def y_sum(self, unit):
        core_in, y_in, z_in = self.buffers[unit][:3]
        for place in range(self.line):
            self.flying["y", unit, place].wait_recv()
        for d in range(1, self.line):
            place = self.other(d)
            row = place * 2 + self.b
            total = self.term(unit, row, self.core)
            total[...] = add(total[...], core_in[row], y_in[place]).astype(jnp.bfloat16)
            self.send(("z", unit, d), total, z_in.at[d], 5, d, {"dp": row})

    def z_sum(self, unit):
        core_in, y_in, z_in, x_out, x_in = self.buffers[unit][:5]
        for d in range(1, self.line):
            self.flying["z", unit, d].wait_recv()
        terms = [self.term(unit, self.rank, self.core)[...], core_in[self.rank], y_in[self.a]]
        terms += [z_in[d] for d in range(1, self.line)]
        x_out[...] = add(*terms).astype(jnp.bfloat16)
        for d, peer in enumerate(self.x_peers()):
            self.send(("x", unit, d), x_out, x_in.at[d], 7, d, peer)

    def x_sum(self, unit):
        x_out, x_in, final = self.buffers[unit][3:]
        for d in range(self.chips - 1):
            self.flying["x", unit, d].wait_recv()
        mine = self.half(unit, self.core)
        final[:, mine] = add(x_out[...], *[x_in[d] for d in range(self.chips - 1)])
        self.send(("f", unit), final.at[:, mine], final.at[:, mine], 9, 0, self.core_peer)

    def finish(self, unit):
        array, rows, columns, row, column = self.units[unit]
        self.flying["f", unit].wait_recv()
        self.sent.pop((unit, False))
        for key in (("f", unit), *[("x", unit, d) for d in range(self.chips - 1)]):
            self.flying[key].wait_send()
        copy = pltpu.make_async_copy(
            self.buffers[unit][5],
            self.outs[array].at[pl.ds(row, rows), pl.ds(column, columns)],
            self.sems[2].at[unit, 0],
        )
        copy.start()
        self.flying["out", unit] = copy

    def drain(self):
        for copies in self.sent.values():
            for copy in copies:
                copy.wait_send()
        for unit in range(len(self.units)):
            self.flying["out", unit].wait()


def add(*terms):
    total = terms[0].astype(jnp.float32)
    for term in terms[1:]:
        total = total + term.astype(jnp.float32)
    return total


class Products:
    def __init__(self, refs, scratch, work, d_packed):
        (
            self.small,
            mixed,
            middle,
            active,
            upstream,
            normed_b,
            d_hidden,
            normed,
            self.second_packed,
        ) = refs
        self.stream, self.keep, self.sems = scratch
        self.work, self.d_packed = work, d_packed
        self.width, self.both = self.stream.shape[1:]
        self.tokens = self.both // 2
        self.mixed, self.active, self.d_hidden = mixed, active, d_hidden
        self.kept = (middle, normed_b, upstream, normed)
        self.flying = {}

    @staticmethod
    def scratch(width, tokens):
        b = jnp.bfloat16
        return [
            pltpu.VMEM((2, width, 2 * tokens), b),
            pltpu.VMEM((4, width, 2 * tokens), b),
            pltpu.SemaphoreType.DMA((32, 2)),
        ]

    def copy(self, key, slot, side, src, dst):
        copy = pltpu.make_async_copy(src, dst, self.sems.at[slot, side])
        copy.start()
        self.flying.setdefault(key, []).append(copy)

    def wait(self, key):
        for copy in self.flying.pop(key, []):
            copy.wait()

    def begin(self):
        self.copy("small", 30, 0, self.small, self.work.small)
        self.fetch(1)
        for index in (0, 2, 1, 3):
            for side in range(2):
                lanes = pl.ds(side * self.tokens, self.tokens)
                self.copy(
                    ("kept", index),
                    20 + index,
                    side,
                    self.kept[index][side],
                    self.keep.at[index, :, lanes],
                )
        self.fetch(2)

    def kind(self, unit):
        array, rows, columns, row, column = self.work.units[unit]
        return array, row // rows, column // columns

    def fetch(self, unit):
        if unit >= len(self.work.units):
            return
        array, row, column = self.kind(unit)
        slot = unit % 2
        for side in range(2):
            lanes = pl.ds(side * self.tokens, self.tokens)
            if array == 1:
                self.copy(unit, unit, side, self.mixed[side], self.stream.at[slot, :, lanes])
            elif array == 3:
                rows = self.work.units[unit][1]
                for rank in range(self.work.dp):
                    pltpu.make_async_copy(
                        self.active[side].at[rank, row],
                        self.stream.at[slot, pl.ds(rank * rows, rows), lanes],
                        self.sems.at[unit, side],
                    ).start()
                all_ranks = pltpu.make_async_copy(
                    self.d_hidden[side].at[pl.ds(0, self.width)],
                    self.stream.at[slot, :, lanes],
                    self.sems.at[unit, side],
                )
                self.flying.setdefault(unit, []).append(all_ranks)
            elif array == 2:
                self.copy(
                    unit,
                    unit,
                    side,
                    self.d_hidden[side].at[pl.ds(column * self.width, self.width)],
                    self.stream.at[slot, :, lanes],
                )
            elif side == 1:
                self.copy(
                    unit,
                    unit,
                    side,
                    self.second_packed.at[pl.ds(column * self.width, self.width)],
                    self.stream.at[slot, :, lanes],
                )

    def make(self, unit):
        work = self.work
        if unit == 0:
            self.wait("small")
            work.start(0)
            return
        array, row, column = self.kind(unit)
        slot = unit % 2
        kept = array - 1
        self.wait(("kept", kept))
        self.wait(unit)
        if array == 4:
            self.stream[slot, :, : self.tokens] = self.d_packed[
                column * self.width : (column + 1) * self.width, :
            ]
        work.free(unit - SLOTS)
        rows = work.units[unit][1]
        ranks = work.dp // 2
        for part in range(2):
            span = slice(part * ranks * rows, (part + 1) * ranks * rows)
            if array in (1, 3):
                product = nt(self.stream[slot, span, :], self.keep[kept])
            else:
                product = nt(self.keep[kept, span, :], self.stream[slot])
            for rank in range(ranks):
                work.terms[(unit - 1) % SLOTS, part * ranks + rank] = product[
                    rank * rows : (rank + 1) * rows, :
                ].astype(jnp.bfloat16)
        work.start(unit)
        self.fetch(unit + 2)


class Pipeline:
    def __init__(self, work, products):
        self.calls = (
            products.make,
            work.chip_sum,
            work.y_sum,
            work.z_sum,
            work.x_sum,
            work.finish,
        )
        self.lags = (0, 1, 2, 2, 2, 1)
        self.done = [0] * len(self.calls)
        self.extra = []

    def tick(self, limit):
        made = self.done[0]
        if made < limit and made - self.done[3] < SLOTS:
            self.calls[0](made)
            self.done[0] += 1
        full = self.done[0] == limit
        for stage in range(1, len(self.calls)):
            now, ahead = self.done[stage], self.done[stage - 1]
            ready = ahead - now > (0 if full else self.lags[stage])
            full = full and ahead == limit
            if ready:
                self.calls[stage](now)
                self.done[stage] += 1

    def run_out(self, limit):
        while self.done[-1] < limit:
            self.tick(limit)
            if self.done[0] == limit and self.extra:
                self.extra.pop(0)()
        for task in self.extra:
            task()


def last_tasks(sources, scratch, d_packed, result):
    weight_s, stream_s, base_s, gain_s, sems = scratch
    weight, stream, base, gain = sources
    width = weight_s.shape[1]
    flying, total = {}, {}

    def fetch(key, source, place, slot):
        flying[key] = pltpu.make_async_copy(source, place, sems.at[slot])
        flying[key].start()

    def fetch_weight(part):
        fetch(part, weight.at[:, pl.ds(part * width, width)], weight_s.at[part % 2], part)

    def begin():
        fetch_weight(0)
        fetch_weight(1)
        fetch("stream", stream, stream_s, 3)
        fetch("base", base, base_s, 4)
        fetch("gain", gain, gain_s, 5)

    def multiply(part):
        flying[part].wait()
        term = nn(weight_s[part % 2], d_packed[part * width : (part + 1) * width, :])
        if part == 0:
            fetch_weight(2)
        total["grad"] = term if part == 0 else total["grad"] + term

    def end():
        for key in ("stream", "base", "gain"):
            flying[key].wait()
        unit, inverse = norm_unit(stream_s[...].T)
        grad = base_s[...] + norm_backward(unit, inverse, column(gain_s[...]), total["grad"])
        stream_s[...] = grad.T
        copy = pltpu.make_async_copy(stream_s, result, sems.at[6])
        copy.start()
        copy.wait()

    return [begin] + [functools.partial(multiply, part) for part in range(3)] + [end]


def causal_mask(size):
    rows = lax.broadcasted_iota(jnp.int32, (size, size), 0)
    columns = lax.broadcasted_iota(jnp.int32, (size, size), 1)
    return rows <= columns


def forward_kernel(seq, dp, sets, units, arrays, heads, *refs):
    refs = list(refs)

    def take(count):
        taken = refs[:count]
        del refs[:count]
        return taken

    (packed,) = take(1)
    earlier = take(sets - 1)
    shards = take(arrays)
    heads_out, mixed_out, own_out, totals_out = take(4)
    wholes = take(arrays)
    arrived, mixed_in, q_s, k_s, v_s, in_send, in_recv, out_send, out_recv = take(9)
    gather = Gather(seq, dp, shards, wholes, units, refs) if units else None

    tokens = packed.shape[1]
    length = tokens * seq
    group = 3 * HEAD_DIM
    me = lax.axis_index("seq")
    peers = seq_peers(seq)
    greet([{"seq": peer} for peer in peers] + (gather.peers() if units else []))

    own_lanes = pl.ds(pl.multiple_of(me * tokens, tokens), tokens)
    copies = {}
    for h in range(heads):
        for d, peer in enumerate(peers):
            copy = remote(
                packed.at[pl.ds(pl.multiple_of((peer * heads + h) * group, group), group)],
                arrived.at[pl.ds(h * group, group), own_lanes],
                in_send.at[h, d],
                in_recv.at[h, d],
                {"seq": peer},
            )
            copy.start()
            copies[h, d] = copy
    steps = []
    if units:
        for unit in range(len(units)):
            gather.start(unit)
        gather.keep_own()
        steps = gather.steps()
        steps.pop(0)()
    for h in range(heads):
        arrived[h * group : (h + 1) * group, own_lanes] = packed[
            pl.ds(pl.multiple_of((me * heads + h) * group, group), group), :
        ]

    mask = causal_mask(tokens)
    for s in range(sets):
        v_s[s, HEAD_DIM:] = jnp.ones((16, length), jnp.bfloat16)
    results = []
    for h in range(heads):
        c0 = h * group
        for s in range(sets):
            source = earlier[s] if s < sets - 1 else arrived
            if s == sets - 1:
                for d in range(seq - 1):
                    copies[h, d].wait_recv()
                heads_out[c0 : c0 + group, :] = arrived[c0 : c0 + group, :]
                q_s[...] = arrived[c0 : c0 + HEAD_DIM, :] * jnp.bfloat16(HEAD_DIM**-0.5)
            k_s[s] = source[c0 + HEAD_DIM : c0 + 2 * HEAD_DIM, :].T
            v_s[s, :HEAD_DIM] = source[c0 + 2 * HEAD_DIM : c0 + 3 * HEAD_DIM, :]

        for i in range(seq):
            queries = q_s[:, i * tokens : (i + 1) * tokens]
            peak = total = None
            for j in [i] + list(range(i)):
                keys = slice(j * tokens, (j + 1) * tokens)
                scores = []
                for s in range(sets):
                    block = nn(k_s[s, keys, :], queries)
                    if j == i:
                        block = jnp.where(mask, block, -1e30)
                    scores.append(block)
                peak_now = peak
                for block in scores:
                    top = jnp.max(block, axis=0, keepdims=True)
                    peak_now = top if peak_now is None else jnp.maximum(peak_now, top)
                if total is not None:
                    total = total * jnp.exp(peak - peak_now)
                for s, block in enumerate(scores):
                    weights = jnp.exp(block - peak_now).astype(jnp.bfloat16)
                    part = nn(v_s[s, :, keys], weights)
                    total = part if total is None else total + part
                peak = peak_now
            row_sum = total[HEAD_DIM : HEAD_DIM + 1]
            own_out[h * HEAD_DIM : (h + 1) * HEAD_DIM, i * tokens : (i + 1) * tokens] = (
                total[:HEAD_DIM] / row_sum
            ).astype(jnp.bfloat16)
            totals_out[h, :, i * tokens : (i + 1) * tokens] = peak + jnp.log(row_sum)
            if steps:
                steps.pop(0)()

        mine = pl.ds(pl.multiple_of((me * heads + h) * HEAD_DIM, HEAD_DIM), HEAD_DIM)
        for d, peer in enumerate(peers):
            copy = remote(
                own_out.at[
                    pl.ds(h * HEAD_DIM, HEAD_DIM),
                    pl.ds(pl.multiple_of(peer * tokens, tokens), tokens),
                ],
                mixed_in.at[mine],
                out_send.at[h, d],
                out_recv.at[h, d],
                {"seq": peer},
            )
            copy.start()
            results.append(copy)
        mixed_in[mine] = own_out[h * HEAD_DIM : (h + 1) * HEAD_DIM, own_lanes]
    for step in steps:
        step()
    if units:
        gather.finish()
    for copy in copies.values():
        copy.wait_send()
    for copy in results:
        copy.wait()
    mixed_out[...] = mixed_in[...]


def attend_forward(seq, dp, heads, packed, earlier, shards, call_id):
    width, tokens = packed.shape
    length = tokens * seq
    sets, arrays = 1 + len(earlier), len(shards)
    units = later_units(shards) if arrays else []
    rows = heads * 3 * HEAD_DIM
    vmem = pl.BlockSpec(memory_space=pltpu.VMEM)
    hbm = pl.BlockSpec(memory_space=pl.ANY)
    dma = pltpu.SemaphoreType.DMA
    outs = pl.pallas_call(
        functools.partial(forward_kernel, seq, dp, sets, units, arrays, heads),
        out_shape=(
            jax.ShapeDtypeStruct((rows, length), jnp.bfloat16),
            jax.ShapeDtypeStruct((width // 3, tokens), jnp.bfloat16),
            jax.ShapeDtypeStruct((heads * HEAD_DIM, length), jnp.bfloat16),
            jax.ShapeDtypeStruct((heads, 1, length), jnp.float32),
        )
        + tuple(whole_shape(shard, dp) for shard in shards),
        in_specs=[vmem] * sets + [hbm] * arrays,
        out_specs=(vmem,) * 4 + (hbm,) * arrays,
        scratch_shapes=[
            pltpu.VMEM((rows, length), jnp.bfloat16),
            pltpu.VMEM((width // 3, tokens), jnp.bfloat16),
            pltpu.VMEM((HEAD_DIM, length), jnp.bfloat16),
            pltpu.VMEM((sets, length, HEAD_DIM), jnp.bfloat16),
            pltpu.VMEM((sets, HEAD_DIM + 16, length), jnp.bfloat16),
            dma((heads, seq)),
            dma((heads, seq)),
            dma((heads, seq)),
            dma((heads, seq)),
        ]
        + (Gather.scratch(arrays, len(units), dp) if units else []),
        compiler_params=pltpu.CompilerParams(
            collective_id=call_id, has_side_effects=True, vmem_limit_bytes=40 << 20
        ),
        name=f"attend_forward_{sets}",
    )(packed, *earlier, *shards)
    return outs[:4], outs[4:]


def backward_kernel(seq, dp, sets, units, heads, *refs):
    refs = list(refs)

    def take(count):
        taken = refs[:count]
        del refs[:count]
        return taken

    (d_mixed,) = take(1)
    packs = take(sets)
    own_in, totals_in = take(2)
    if units:
        (carry_in, small) = take(2)
        pairs = [take(2) for _ in range(7)]
        (second_packed,) = take(1)
        last_in = take(4)
    (d_packed_out,) = take(1)
    carry_out = None if units else take(1)[0]
    grads_out = take(5) if units else []
    arrived, local_grad, d_packed_in, q_s, k_s, kt_s, v_s, delta_s, dq_s, dkv_s = take(10)
    in_send, in_recv, out_send, out_recv, out_sem = take(5)
    if units:
        carry_s, carry_sem = take(2)
        product_scratch = take(3)
        last_s = take(5)
        work = Scatter(seq, dp, units, grads_out, refs)
        products = Products([small] + pairs + [second_packed], product_scratch, work, d_packed_in)

    tokens = d_mixed.shape[1]
    length = tokens * seq
    group = 3 * HEAD_DIM
    me = lax.axis_index("seq")
    peers = seq_peers(seq)
    greet([{"seq": peer} for peer in peers] + (work.peers() if units else []))
    own_lanes = pl.ds(pl.multiple_of(me * tokens, tokens), tokens)
    scale = jnp.bfloat16(HEAD_DIM**-0.5)

    copies = {}
    for h in range(heads):
        for d, peer in enumerate(peers):
            copy = remote(
                d_mixed.at[pl.ds(pl.multiple_of((peer * heads + h) * HEAD_DIM, HEAD_DIM), HEAD_DIM)],
                arrived.at[pl.ds(h * HEAD_DIM, HEAD_DIM), own_lanes],
                in_send.at[h, d],
                in_recv.at[h, d],
                {"seq": peer},
            )
            copy.start()
            copies[h, d] = copy
    if units:
        products.begin()
        pipeline = Pipeline(work, products)
        early = [unit[0] for unit in units].index(4)
    for h in range(heads):
        arrived[h * HEAD_DIM : (h + 1) * HEAD_DIM, own_lanes] = d_mixed[
            pl.ds(pl.multiple_of((me * heads + h) * HEAD_DIM, HEAD_DIM), HEAD_DIM), :
        ]

    def outgoing(h, rank, send_slot):
        return remote(
            local_grad.at[
                pl.ds(h * group, group), pl.ds(pl.multiple_of(rank * tokens, tokens), tokens)
            ],
            d_packed_in.at[pl.ds(pl.multiple_of((me * heads + h) * group, group), group)],
            out_send.at[h, send_slot],
            out_recv.at[h, me],
            {"seq": rank},
        )

    if units:
        for _ in range(AHEAD):
            pipeline.tick(early)
    mask = causal_mask(tokens)
    hook = 0
    for h in range(heads):
        c0 = h * group
        r0 = h * HEAD_DIM
        if units:
            carried = pltpu.make_async_copy(carry_in.at[h], carry_s, carry_sem.at[h])
            carried.start()
        q_s[...] = packs[-1][c0 : c0 + HEAD_DIM, :] * scale
        for s in range(sets):
            keys = packs[s][c0 + HEAD_DIM : c0 + 2 * HEAD_DIM, :]
            k_s[s] = keys.T
            kt_s[s] = keys * scale
            v_s[s] = packs[s][c0 + 2 * HEAD_DIM : c0 + 3 * HEAD_DIM, :].T
        for d in range(seq - 1):
            copies[h, d].wait_recv()
        delta_s[...] = jnp.sum(
            arrived[r0 : r0 + HEAD_DIM, :].astype(jnp.float32)
            * own_in[r0 : r0 + HEAD_DIM, :].astype(jnp.float32),
            axis=0,
            keepdims=True,
        )
        if units:
            carried.wait()
        for j in range(seq):
            keys = slice(j * tokens, (j + 1) * tokens)
            for i in range(j, seq):
                span = slice(i * tokens, (i + 1) * tokens)
                queries = q_s[:, span]
                grads = arrived[r0 : r0 + HEAD_DIM, span]
                d_query = dq_s[:, span] if j > 0 else None
                for s in range(sets):
                    chances = jnp.exp(nn(k_s[s, keys, :], queries) - totals_in[h, :, span])
                    if i == j:
                        chances = jnp.where(mask, chances, 0.0)
                    d_chance = nn(v_s[s, keys, :], grads)
                    d_score = (chances * (d_chance - delta_s[:, span])).astype(jnp.bfloat16)
                    d_key = nt(queries, d_score)
                    d_value = nt(grads, chances.astype(jnp.bfloat16))
                    if i == j:
                        if units:
                            d_key = d_key + carry_s[:HEAD_DIM, keys]
                            d_value = d_value + carry_s[HEAD_DIM:, keys]
                        dkv_s[s, :HEAD_DIM, keys] = d_key
                        dkv_s[s, HEAD_DIM:, keys] = d_value
                    else:
                        dkv_s[s, :HEAD_DIM, keys] += d_key
                        dkv_s[s, HEAD_DIM:, keys] += d_value
                    part = nn(kt_s[s, :, keys], d_score)
                    d_query = part if d_query is None else d_query + part
                dq_s[:, span] = d_query
                hook += 1
                if units and hook % EVERY == 0:
                    pipeline.tick(early)
            local_grad[c0 : c0 + HEAD_DIM, keys] = dq_s[:, keys].astype(jnp.bfloat16)
            local_grad[c0 + HEAD_DIM : c0 + group, keys] = dkv_s[sets - 1, :, keys].astype(
                jnp.bfloat16
            )
            if h == heads - 1:

                @pl.when(me != j)
                def _():
                    outgoing(h, jnp.int32(j), j).start()

        if not units:
            carry_out[h] = dkv_s[0]
        if h < heads - 1:
            for d, peer in enumerate(peers):
                outgoing(h, peer, d).start()
        d_packed_in[pl.ds(pl.multiple_of((me * heads + h) * group, group), group)] = local_grad[
            c0 : c0 + group, own_lanes
        ]
    for h in range(heads):
        for peer in peers:
            remote(
                local_grad.at[pl.ds(h * group, group), own_lanes],
                d_packed_in.at[pl.ds(pl.multiple_of((peer * heads + h) * group, group), group)],
                out_send.at[h, 0],
                out_recv.at[h, peer],
                {"seq": peer},
            ).wait_recv()
    if units:
        pipeline.extra = last_tasks(last_in, last_s, d_packed_in, d_packed_out)
        pipeline.run_out(len(units))
        work.drain()
    else:
        finished = pltpu.make_async_copy(d_packed_in, d_packed_out, out_sem.at[0])
        finished.start()
    for copy in copies.values():
        copy.wait_send()
    for h in range(heads - 1):
        for d, peer in enumerate(peers):
            outgoing(h, peer, d).wait_send()
    for j in range(seq):

        @pl.when(me != j)
        def _():
            outgoing(heads - 1, jnp.int32(j), j).wait_send()

    if not units:
        finished.wait()


def attend_backward(seq, dp, heads, d_mixed, packs, own, totals, extra, units, call_id):
    width, tokens = d_mixed.shape
    length = tokens * seq
    sets = len(packs)
    rows = heads * 3 * HEAD_DIM
    vmem = pl.BlockSpec(memory_space=pltpu.VMEM)
    hbm = pl.BlockSpec(memory_space=pl.ANY)
    dma = pltpu.SemaphoreType.DMA
    f32 = jnp.float32
    out_shape = [jax.ShapeDtypeStruct((3 * width, tokens), jnp.bfloat16)]
    if units:
        out_shape = [jax.ShapeDtypeStruct((tokens, width), f32)]
    out_specs = [hbm]
    more = []
    if units:
        heights = [0] * 5
        for array, high, wide, row, column in units:
            heights[array] = max(heights[array], row + high)
        widths = [0] * 5
        for array, high, wide, row, column in units:
            widths[array] = max(widths[array], column + wide)
        out_shape += [jax.ShapeDtypeStruct(shape, f32) for shape in zip(heights, widths)]
        out_specs += [hbm] * 5
        more = [pltpu.VMEM((2 * HEAD_DIM, length), f32), dma((heads,))]
        more += Products.scratch(width, tokens)
        more += [
            pltpu.VMEM((2, width, width), jnp.bfloat16),
            pltpu.VMEM((tokens, width), f32),
            pltpu.VMEM((width, tokens), f32),
            pltpu.VMEM((1, width), f32),
            dma((8,)),
        ]
        more += Scatter.scratch(seq, dp, units)
    else:
        out_shape.append(jax.ShapeDtypeStruct((heads, 2 * HEAD_DIM, length), f32))
        out_specs.append(vmem)
    return pl.pallas_call(
        functools.partial(backward_kernel, seq, dp, sets, units, heads),
        out_shape=tuple(out_shape),
        in_specs=[vmem] * (3 + sets) + [hbm] * len(extra),
        out_specs=tuple(out_specs),
        scratch_shapes=[
            pltpu.VMEM((heads * HEAD_DIM, length), jnp.bfloat16),
            pltpu.VMEM((rows, length), jnp.bfloat16),
            pltpu.VMEM((3 * width, tokens), jnp.bfloat16),
            pltpu.VMEM((HEAD_DIM, length), jnp.bfloat16),
            pltpu.VMEM((sets, length, HEAD_DIM), jnp.bfloat16),
            pltpu.VMEM((sets, HEAD_DIM, length), jnp.bfloat16),
            pltpu.VMEM((sets, length, HEAD_DIM), jnp.bfloat16),
            pltpu.VMEM((1, length), f32),
            pltpu.VMEM((HEAD_DIM, length), f32),
            pltpu.VMEM((sets, 2 * HEAD_DIM, length), f32),
            dma((heads, seq)),
            dma((heads, seq)),
            dma((heads, seq)),
            dma((heads, seq)),
            dma((1,)),
        ]
        + more,
        compiler_params=pltpu.CompilerParams(
            collective_id=call_id, has_side_effects=True, vmem_limit_bytes=60 << 20
        ),
        name=f"attend_backward_{sets}",
    )(d_mixed, *packs, own, totals, *extra)


def column(row):
    return jnp.broadcast_to(row, (8, row.shape[1])).T[:, :1]


def norm_unit(rows):
    centre = rows - jnp.mean(rows, axis=0, keepdims=True)
    inverse = lax.rsqrt(jnp.mean(centre * centre, axis=0, keepdims=True) + epsilon)
    return centre * inverse, inverse


def norm_backward(unit, inverse, gain, grad):
    grad = grad * gain
    share = jnp.mean(grad * unit, axis=0, keepdims=True)
    return inverse * (grad - jnp.mean(grad, axis=0, keepdims=True) - unit * share)


def gelu_slope(hidden):
    root = (2.0 / math.pi) ** 0.5
    square = hidden * hidden
    bend = jnp.tanh(root * hidden * (1.0 + 0.044715 * square))
    inner = (0.5 * root) * hidden * (1.0 + 3 * 0.044715 * square)
    return 0.5 * (1.0 + bend) + inner * (1.0 - bend * bend)


def dense_kernel(first, chunks, *refs):
    refs = list(refs)

    def take(count):
        taken = refs[:count]
        del refs[:count]
        return taken

    count = 5 * first + (1 - first) + 6 + first
    sources = take(count)
    results = take(5 + first * 4)
    places = take(count)
    sems, out_sems = take(2)
    base = 5 * first + (1 - first)
    middle, hidden, down_w, up_w, out_w, gain = range(base, base + 6)
    width = places[middle].shape[1]

    def span(part):
        return pl.ds(part * width, width)

    order = [(0, None)]
    if first:
        order = [(index, part) for part in range(3) for index in (1, 0)] + [(2, None), (4, None), (3, None)]
    for part in range(chunks):
        order += [(down_w, part), (hidden, part), (up_w, part)]
    order += [(middle, None), (gain, None), (out_w, None)] + [(base + 6, None)] * first
    by_columns = (up_w, 1) if first else (up_w,)
    fetched = {}
    for index, part in order:
        source, place = sources[index], places[index]
        if part is not None:
            where = (slice(None), span(part)) if index in by_columns else (span(part),)
            source, place = source.at[where], place.at[where]
        copy = pltpu.make_async_copy(source, place, sems.at[index, part or 0])
        copy.start()
        fetched[index, part] = copy

    def get(index, part=None):
        fetched[index, part].wait()
        return places[index]

    sent = []

    def put(place, result):
        copy = pltpu.make_async_copy(place, result, out_sems.at[len(sent)])
        copy.start()
        sent.append(copy)

    if first:
        grad = None
        for part in range(3):
            term = nn(get(1, part)[:, span(part)], get(0, part)[span(part), :])
            grad = term if grad is None else grad + term
        unit, inverse = norm_unit(get(2)[...].T)
        gain_a = column(get(4)[...])
        upstream = get(3)[...] + norm_backward(unit, inverse, gain_a, grad)
    else:
        upstream = get(0)[...].astype(jnp.float32)
    hidden_s, grad_s, middle_s, mixed_s, normed_s, up_s, rounded_s = refs[:7]
    up_s[...] = upstream
    rounded_s[...] = upstream.astype(jnp.bfloat16)
    if first:
        first_s, second_s = refs[7:]
        rounded_out, sum_out, first_out, second_out = results[5:]
        put(rounded_s, rounded_out)
        sum_out[...] = jnp.sum(upstream, axis=1, keepdims=True)
        second_s[...] = (unit * gain_a).astype(jnp.bfloat16)
        put(second_s, second_out)
    total = None
    for part in range(chunks):
        d_active = nn(get(down_w, part)[span(part), :], rounded_s[...])
        slope = gelu_slope(get(hidden, part)[span(part), :])
        hidden_s[span(part), :] = (d_active * slope).astype(jnp.bfloat16)
        put(hidden_s.at[span(part)], results[0].at[span(part)])
        term = nn(get(up_w, part)[:, span(part)], hidden_s[span(part), :])
        total = term if total is None else total + term
    unit, inverse = norm_unit(get(middle)[...].T)
    gain_b = column(get(gain)[...])
    d_middle = up_s[...] + norm_backward(unit, inverse, gain_b, total)
    grad_s[...] = d_middle
    middle_s[...] = d_middle.astype(jnp.bfloat16)
    normed_s[...] = (unit * gain_b).astype(jnp.bfloat16)
    put(grad_s, results[1])
    put(middle_s, results[2])
    put(normed_s, results[4])
    mixed_s[...] = nn(get(out_w)[...], middle_s[...]).astype(jnp.bfloat16)
    put(mixed_s, results[3])
    if first:
        first_s[...] = (norm_unit(get(base + 6)[...].T)[0] * gain_a).astype(jnp.bfloat16)
        put(first_s, first_out)
    for copy in sent:
        copy.wait()


def dense_backward(before, after):
    first = int(len(before) > 1)
    args = list(before) + list(after)
    width, tokens = (before[3] if first else before[0]).shape
    hbm = pl.BlockSpec(memory_space=pl.ANY)
    b, f32 = jnp.bfloat16, jnp.float32
    ff = after[1].shape[0]
    flat = (width, tokens)
    shapes = [((ff, tokens), b), (flat, f32), (flat, b), (flat, b), (flat, b)]
    more = [pltpu.VMEM(shape, kind) for shape, kind in shapes]
    more += [pltpu.VMEM(flat, f32), pltpu.VMEM(flat, b)]
    outs = [jax.ShapeDtypeStruct(shape, kind) for shape, kind in shapes]
    specs = [hbm] * 5
    if first:
        more += [pltpu.VMEM(flat, b)] * 2
        outs += [jax.ShapeDtypeStruct(flat, b), jax.ShapeDtypeStruct((width, 1), f32)]
        outs += [jax.ShapeDtypeStruct(flat, b)] * 2
        specs += [hbm, pl.BlockSpec(memory_space=pltpu.VMEM), hbm, hbm]
    flops = 2 * tokens * width * (2 * ff + width + 3 * width * first)
    return pl.pallas_call(
        functools.partial(dense_kernel, first, ff // width),
        out_shape=tuple(outs),
        in_specs=[hbm] * len(args),
        out_specs=tuple(specs),
        scratch_shapes=[pltpu.VMEM(arg.shape, arg.dtype) for arg in args]
        + [
            pltpu.SemaphoreType.DMA((len(args), max(3, ff // width))),
            pltpu.SemaphoreType.DMA((16,)),
        ]
        + more,
        compiler_params=pltpu.CompilerParams(vmem_limit_bytes=58 << 20),
        cost_estimate=pl.CostEstimate(flops=flops, bytes_accessed=24 << 20, transcendentals=0),
        name=f"dense_backward_{first}",
    )(*args)


def dots(left, right, left_side, right_side):
    return lax.dot_general(
        left,
        right,
        (((left_side,), (right_side,)), ((), ())),
        preferred_element_type=jnp.float32,
    )


def norm_rows(rows, gain):
    centre = rows - jnp.mean(rows, axis=1, keepdims=True)
    spread = jnp.mean(centre * centre, axis=1, keepdims=True)
    return (centre * lax.rsqrt(spread + epsilon) * gain).astype(jnp.bfloat16)


def block_forward(sizes, call_id, stream, qkv_w, gains, earlier, weights, shards):
    seq, dp, heads = sizes
    normed = norm_rows(stream, gains[0])
    packed = dots(qkv_w, normed, 0, 1).astype(jnp.bfloat16)
    (head_rows, mixed, own, totals), gathered = attend_forward(
        seq, dp, heads, packed, earlier, shards, call_id
    )
    out_w, up_w, down_w = weights or gathered
    middle = stream + dots(mixed, out_w, 0, 0)
    normed_b = norm_rows(middle, gains[1])
    hidden = dots(up_w, normed_b, 0, 1)
    active = jax.nn.gelu(hidden, approximate=True).astype(jnp.bfloat16)
    result = middle + dots(active, down_w, 0, 0)
    packs = earlier + [head_rows]
    stored = (stream, packs, own, totals, mixed, middle, hidden, active)
    return result, stored, (out_w, up_w, down_w)


def block_backward(sizes, call_id, before, stored, gains, weights, second):
    seq, dp, heads = sizes
    out_w, up_w, down_w = weights
    stream, packs, own, totals, mixed, middle, hidden, active = stored
    after = (middle, hidden, down_w, up_w, out_w, gains[1])
    done = dense_backward(before, after if second is None else after + (stream,))
    d_hidden, d_middle, middle_bf, d_mixed, normed_b = done[:5]
    width, tokens = d_mixed.shape
    rows = width // dp
    active = active.reshape(dp, active.shape[0] // width, rows, tokens)
    upstream = before[0] if second is None else done[5]
    factors = [mixed, middle_bf, active, upstream, normed_b, d_hidden]
    extra, units = [], []
    if second is not None:
        passed, second_factors, second_packed = second
        embed = done[6].astype(jnp.bfloat16).reshape(dp, 1, rows)
        factors, second_factors = factors + [done[7]], second_factors + [done[8]]
        extra = [passed, jnp.pad(embed, ((0, 0), (0, 7), (0, 256 - rows)))]
        for pair in zip(factors, second_factors):
            extra += pair
        extra += [second_packed, before[1], stream, d_middle, before[4]]
        ff = d_hidden.shape[0]
        units = [(0, 8, 256, 0, 0)]
        units += [(1, rows, width, 0, 0)]
        units += [(3, rows, width, row, 0) for row in range(0, ff // dp, rows)]
        units += [(2, rows, width, 0, column) for column in range(0, ff, width)]
        units += [(4, rows, width, 0, column) for column in range(0, 3 * width, width)]
    outs = attend_backward(seq, dp, heads, d_mixed, packs, own, totals, extra, units, call_id)
    return (stream, d_middle), factors, outs


def local(
    seq,
    dp,
    tokens,
    qkv_weight,
    out_weight,
    up_weight,
    down_weight,
    norm_gain,
    mlp_gain,
    pass_embed,
    cotangent,
):
    share = norm_gain.shape[0]
    lanes = [
        jnp.pad(v.reshape(1, share), ((0, 0), (0, 128 - share)))
        for v in (norm_gain, pass_embed, mlp_gain)
    ]
    small = jnp.concatenate(
        [
            jnp.concatenate(lanes[:2], axis=1),
            jnp.pad(lanes[2], ((0, 0), (0, 128))),
            jnp.zeros((6, 256), jnp.bfloat16),
        ]
    )
    qkv_w, small = gather_now(seq, dp, [qkv_weight, small])
    small = small.reshape(dp, 8, 256)
    gains = [small[:, row, :share].reshape(1, -1).astype(jnp.float32) for row in (0, 1)]
    embedding = small[:, 0, 128 : 128 + share].reshape(1, -1).astype(jnp.float32)
    heads = qkv_weight.shape[1] // (3 * HEAD_DIM * seq)
    sizes = (seq, dp, heads)
    first_out, first_kept, weights = block_forward(
        sizes,
        1,
        tokens[0].astype(jnp.float32),
        qkv_w,
        gains,
        [],
        None,
        [out_weight, up_weight, down_weight],
    )
    second_out, second_kept, weights = block_forward(
        sizes, 2, first_out + embedding, qkv_w, gains, [first_kept[1][0]], weights, []
    )
    (stream, d_middle), factors, outs = block_backward(
        sizes, 3, (cotangent[0].T,), second_kept, gains, weights, None
    )
    second = (outs[1], factors, outs[0])
    before = (outs[0], qkv_w, stream, d_middle, gains[0])
    _, _, outs = block_backward(sizes, 4, before, first_kept, gains, weights, second)
    d_first, small, out_grad, up_grad, down_grad, qkv_grad = outs
    f32 = jnp.float32
    gain_a = jnp.sum(qkv_weight.astype(f32) * qkv_grad, axis=1) / norm_gain.astype(f32)
    gain_b = jnp.sum(up_weight.astype(f32) * up_grad, axis=1) / mlp_gain.astype(f32)
    return (
        second_out.astype(jnp.bfloat16)[None],
        d_first[None],
        qkv_grad,
        out_grad,
        up_grad,
        down_grad,
        gain_a,
        gain_b,
        small[0, :share],
    )


def solution(mesh):
    in_specs = (
        P("dp", "seq", None),
        P("dp", None),
        P("dp", None),
        P("dp", None),
        P("dp", None),
        P("dp"),
        P("dp"),
        P("dp"),
        P("dp", "seq", None),
    )
    out_specs = (
        P("dp", "seq", None),
        P("dp", "seq", None),
        P("dp", None),
        P("dp", None),
        P("dp", None),
        P("dp", None),
        P("dp"),
        P("dp"),
        P("dp"),
    )
    return jax.shard_map(
        functools.partial(local, mesh.shape["seq"], mesh.shape["dp"]), mesh=mesh, in_specs=in_specs, out_specs=out_specs, check_vma=False)
```

```python
import functools
import math

import jax
import jax.numpy as jnp
from jax import lax
from jax.experimental import pallas as pl
from jax.experimental.pallas import tpu as pltpu
from jax.sharding import PartitionSpec as P

HEAD_DIM = 64
CHUNK = 768
EVERY = 3
SLOTS = 6
PAIRS = 2
AHEAD = 2


epsilon = 1e-05


def nt(left, right):
    return lax.dot_general(
        left, right, (((1,), (1,)), ((), ())), preferred_element_type=jnp.float32
    )


def nn(left, right):
    return lax.dot_general(
        left, right, (((1,), (0,)), ((), ())), preferred_element_type=jnp.float32
    )


def remote(src, dst, send_sem, recv_sem, device):
    return pltpu.make_async_remote_copy(
        src_ref=src,
        dst_ref=dst,
        send_sem=send_sem,
        recv_sem=recv_sem,
        device_id=device,
        device_id_type=pl.DeviceIdType.MESH,
    )


def greet(devices):
    barrier = pltpu.get_barrier_semaphore()
    for device in devices:
        pl.semaphore_signal(
            barrier, inc=1, device_id=device, device_id_type=pl.DeviceIdType.MESH
        )
    pl.semaphore_wait(barrier, len(devices))


def seq_peers(seq):
    me = lax.axis_index("seq")
    return [lax.rem(me + d, seq) for d in range(1, seq)]


class Gather:
    def __init__(self, seq, dp, shards, wholes, units, sems):
        self.line = dp // 2
        self.shards, self.wholes, self.units, self.sems = shards, wholes, units, sems
        me = lax.axis_index("seq")
        self.core, self.chip = lax.rem(me, 2), lax.div(me, 2)
        self.core_peer = {"seq": me + 1 - 2 * self.core}
        self.x_peer = {"seq": self.core + 2 - 2 * self.chip}
        self.rank = lax.axis_index("dp")
        self.a, self.b = lax.div(self.rank, 2), lax.rem(self.rank, 2)
        self.y_peer = {"dp": self.a * 2 + 1 - self.b}
        self.flying, self.sent = {}, []

    @staticmethod
    def scratch(arrays, units, dp):
        line, dma = dp // 2, pltpu.SemaphoreType.DMA
        sizes = (line, line, line, line, 2 * line, 2 * line, 2 * line, 2 * line, 2 * line, 2 * line)
        return [dma((units, size)) for size in sizes] + [dma((arrays,))]

    def z_rank(self, offset):
        return lax.rem(self.a + offset, self.line) * 2 + self.b

    def peers(self):
        z = [{"dp": self.z_rank(d)} for d in range(1, self.line)]
        return z + [self.y_peer]

    def shared(self, unit):
        return sum(self.units[unit][5:]) > 0

    def place(self, unit, first, chip):
        array, row, rows, column, columns, row_step, column_step = self.units[unit]
        half = columns // 2
        start = first + row
        side = column + self.core * half
        if row_step:
            start = start + chip * row_step
        if column_step:
            side = side + chip * column_step
        if not isinstance(start, int):
            start = pl.multiple_of(start, 8)
        return pl.ds(start, rows), pl.ds(pl.multiple_of(side, 128), half)

    def block(self, unit, rank, chip):
        array = self.units[unit][0]
        return self.wholes[array].at[self.place(unit, rank * self.shards[array].shape[0], chip)]

    def send(self, kind, unit, slot, src, dst, device):
        sems = {"z": 0, "y": 2, "core": 4, "x": 6, "core2": 8}[kind]
        copy = remote(
            src, dst, self.sems[sems].at[unit, slot], self.sems[sems + 1].at[unit, slot], device
        )
        copy.start()
        self.flying[kind, unit, slot] = copy
        self.sent.append(copy)

    def keep_own(self):
        for array, (shard, whole) in enumerate(zip(self.shards, self.wholes)):
            rows = shard.shape[0]
            copy = pltpu.make_async_copy(
                shard,
                whole.at[pl.ds(pl.multiple_of(self.rank * rows, 8), rows)],
                self.sems[10].at[array],
            )
            copy.start()
            self.flying["own", array] = copy

    def start(self, unit):
        array = self.units[unit][0]
        mine = self.shards[array].at[self.place(unit, 0, self.chip)]
        there = self.block(unit, self.rank, self.chip)
        for d in range(1, self.line):
            self.send("z", unit, d, mine, there, {"dp": self.z_rank(d)})
        self.send("y", unit, 0, mine, there, self.y_peer)

    def spread(self, unit, slot, rank):
        block = self.block(unit, rank, self.chip)
        if self.shared(unit):
            self.send("x", unit, slot, block, block, self.x_peer)
        self.send("core", unit, slot, block, block, self.core_peer)

    def forward_z(self, unit):
        for d in range(1, self.line):
            self.flying["z", unit, d].wait_recv()
            rank = self.z_rank(self.line - d)
            block = self.block(unit, rank, self.chip)
            self.send("y", unit, d, block, block, self.y_peer)
            self.spread(unit, d, rank)

    def y_rank(self, d):
        return lax.rem(self.a + self.line - d, self.line) * 2 + 1 - self.b

    def forward_y(self, unit):
        for d in range(self.line):
            self.flying["y", unit, d].wait_recv()
            self.spread(unit, self.line + d, self.y_rank(d))

    def forward_x(self, unit):
        if not self.shared(unit):
            return
        for slot in range(1, 2 * self.line):
            self.flying["x", unit, slot].wait_recv()
            d = slot % self.line
            rank = self.y_rank(d) if slot >= self.line else self.z_rank(self.line - d)
            block = self.block(unit, rank, 1 - self.chip)
            self.send("core2", unit, slot, block, block, self.core_peer)

    def finish(self):
        for unit in range(len(self.units)):
            for slot in range(1, 2 * self.line):
                self.flying["core", unit, slot].wait_recv()
                if self.shared(unit):
                    self.flying["core2", unit, slot].wait_recv()
        for array in range(len(self.shards)):
            self.flying["own", array].wait()
        for copy in self.sent:
            copy.wait_send()

    def steps(self):
        count, calls = len(self.units), []
        for step in range(count + 2):
            for call, unit in (
                (self.forward_z, step),
                (self.forward_y, step - 1),
                (self.forward_x, step - 2),
            ):
                if 0 <= unit < count:
                    calls.append(functools.partial(call, unit))
        return calls


def first_units(shards):
    (rows, wide), small = shards[0].shape, shards[1].shape
    units = [(0, 0, rows, 0, CHUNK, 0, CHUNK)]
    units += [(0, 0, rows, column, CHUNK, 0, 0) for column in range(2 * CHUNK, wide, CHUNK)]
    return units + [(1, 0, small[0], 0, small[1], 0, 0)]


def later_units(shards):
    (rows, width), (_, up_wide), (down_rows, _) = [shard.shape for shard in shards]
    ups = [(1, 0, rows, column, CHUNK, 0, 0) for column in range(0, up_wide, CHUNK)]
    shared = 2 * PAIRS * rows
    pairs = [(2, row, rows, 0, width, rows, 0) for row in range(0, shared, 2 * rows)]
    downs = [(2, row, rows, 0, width, 0, 0) for row in range(shared, down_rows, rows)]
    return [(0, 0, rows, 0, width, 0, 0)] + ups[:1] + pairs[:1] + ups[1:3] + pairs[1:] + ups[3:] + downs


def gather_kernel(seq, dp, units, arrays, *refs):
    shards, wholes, sems = refs[:arrays], refs[arrays : 2 * arrays], refs[2 * arrays :]
    gather = Gather(seq, dp, shards, wholes, units, sems)
    greet(gather.peers() + [gather.core_peer, gather.x_peer])
    for unit in range(len(units)):
        gather.start(unit)
    gather.keep_own()
    for call in gather.steps():
        call()
    gather.finish()


def whole_shape(shard, dp):
    return jax.ShapeDtypeStruct((shard.shape[0] * dp, shard.shape[1]), shard.dtype)


def gather_now(seq, dp, shards):
    arrays = len(shards)
    units = first_units(shards)
    hbm = pl.BlockSpec(memory_space=pl.ANY)
    return pl.pallas_call(
        functools.partial(gather_kernel, seq, dp, units, arrays),
        out_shape=tuple(whole_shape(shard, dp) for shard in shards),
        in_specs=[hbm] * arrays,
        out_specs=(hbm,) * arrays,
        scratch_shapes=Gather.scratch(arrays, len(units), dp),
        compiler_params=pltpu.CompilerParams(
            collective_id=0, has_side_effects=True, vmem_limit_bytes=4 << 20
        ),
        name="gather_first",
    )(*shards)


class Scatter:
    def __init__(self, seq, dp, units, outs, scratch):
        self.seq, self.dp, self.line, self.chips = seq, dp, dp // 2, seq // 2
        self.units, self.outs = units, outs
        me = lax.axis_index("seq")
        self.core, self.chip = lax.rem(me, 2), lax.div(me, 2)
        self.core_peer = {"seq": me + 1 - 2 * self.core}
        self.rank = lax.axis_index("dp")
        self.a, self.b = lax.div(self.rank, 2), lax.rem(self.rank, 2)
        self.y_peer = {"dp": self.a * 2 + 1 - self.b}
        count = len(units)
        self.small, self.terms = scratch[0], scratch[1]
        self.buffers = [scratch[2 + 6 * u : 8 + 6 * u] for u in range(count)]
        self.sems = scratch[2 + 6 * count :]
        self.flying, self.sent = {}, {}

    @staticmethod
    def scratch(seq, dp, units):
        line, chips, b = dp // 2, seq // 2, jnp.bfloat16
        rows, columns = units[1][1:3]
        shapes = [
            pltpu.VMEM((dp,) + units[0][1:3], b),
            pltpu.VMEM((SLOTS, dp, rows, columns), b),
        ]
        for unit in units:
            rows, half = unit[1], unit[2] // 2
            for lead in ((dp,), (line,), (line,), (), (chips,)):
                shapes.append(pltpu.VMEM(lead + (rows, half), b))
            shapes.append(pltpu.VMEM((rows, 2 * half), jnp.float32))
        count, dma = len(units), pltpu.SemaphoreType.DMA
        sizes = (1, 1, 1, line, line, line, line, chips, chips, 1, 1)
        return shapes + [dma((count, size)) for size in sizes]

    def peers(self):
        z = [{"dp": self.other(d) * 2 + self.b} for d in range(1, self.line)]
        return z + [self.y_peer]

    def x_peers(self):
        return [
            {"seq": lax.rem(self.chip + d, self.chips) * 2 + self.core}
            for d in range(1, self.chips)
        ]

    def other(self, offset):
        return lax.rem(self.a + offset, self.line)

    def half(self, unit, core):
        half = self.units[unit][2] // 2
        return pl.ds(pl.multiple_of(core * half, 128), half)

    def term(self, unit, row, core):
        lanes = self.half(unit, core)
        if unit == 0:
            return self.small.at[row, :, lanes]
        return self.terms.at[(unit - 1) % SLOTS, row, :, lanes]

    def all_terms(self, unit, core):
        lanes = self.half(unit, core)
        if unit == 0:
            return self.small.at[:, :, lanes]
        return self.terms.at[(unit - 1) % SLOTS, :, :, lanes]

    def send(self, key, src, dst, sems, slot, device):
        unit = key[1]
        copy = remote(
            src, dst, self.sems[sems].at[unit, slot], self.sems[sems + 1].at[unit, slot], device
        )
        copy.start()
        self.flying[key] = copy
        self.sent.setdefault((unit, key[0] in ("core", "y", "z")), []).append(copy)

    def free(self, unit):
        if unit >= 1:
            for copy in self.sent.pop((unit, True), []):
                copy.wait_send()

    def start(self, unit):
        self.send(
            ("core", unit), self.all_terms(unit, 1 - self.core), self.buffers[unit][0], 0, 0, self.core_peer
        )

    def chip_sum(self, unit):
        core_in, y_in = self.buffers[unit][:2]
        self.flying["core", unit].wait_recv()
        for place in range(self.line):
            row = place * 2 + 1 - self.b
            total = self.term(unit, row, self.core)
            total[...] = add(total[...], core_in[row]).astype(jnp.bfloat16)
            self.send(("y", unit, place), total, y_in.at[place], 3, place, self.y_peer)

    def y_sum(self, unit):
        core_in, y_in, z_in = self.buffers[unit][:3]
        for place in range(self.line):
            self.flying["y", unit, place].wait_recv()
        for d in range(1, self.line):
            place = self.other(d)
            row = place * 2 + self.b
            total = self.term(unit, row, self.core)
            total[...] = add(total[...], core_in[row], y_in[place]).astype(jnp.bfloat16)
            self.send(("z", unit, d), total, z_in.at[d], 5, d, {"dp": row})

    def z_sum(self, unit):
        core_in, y_in, z_in, x_out, x_in = self.buffers[unit][:5]
        for d in range(1, self.line):
            self.flying["z", unit, d].wait_recv()
        terms = [self.term(unit, self.rank, self.core)[...], core_in[self.rank], y_in[self.a]]
        terms += [z_in[d] for d in range(1, self.line)]
        x_out[...] = add(*terms).astype(jnp.bfloat16)
        for d, peer in enumerate(self.x_peers()):
            self.send(("x", unit, d), x_out, x_in.at[d], 7, d, peer)

    def x_sum(self, unit):
        x_out, x_in, final = self.buffers[unit][3:]
        for d in range(self.chips - 1):
            self.flying["x", unit, d].wait_recv()
        mine = self.half(unit, self.core)
        final[:, mine] = add(x_out[...], *[x_in[d] for d in range(self.chips - 1)])
        self.send(("f", unit), final.at[:, mine], final.at[:, mine], 9, 0, self.core_peer)

    def finish(self, unit):
        array, rows, columns, row, column = self.units[unit]
        self.flying["f", unit].wait_recv()
        self.sent.pop((unit, False))
        for key in (("f", unit), *[("x", unit, d) for d in range(self.chips - 1)]):
            self.flying[key].wait_send()
        copy = pltpu.make_async_copy(
            self.buffers[unit][5],
            self.outs[array].at[pl.ds(row, rows), pl.ds(column, columns)],
            self.sems[2].at[unit, 0],
        )
        copy.start()
        self.flying["out", unit] = copy

    def drain(self):
        for copies in self.sent.values():
            for copy in copies:
                copy.wait_send()
        for unit in range(len(self.units)):
            self.flying["out", unit].wait()


def add(*terms):
    total = terms[0].astype(jnp.float32)
    for term in terms[1:]:
        total = total + term.astype(jnp.float32)
    return total


class Products:
    def __init__(self, refs, scratch, work, d_packed):
        (
            self.small,
            mixed,
            middle,
            active,
            upstream,
            normed_b,
            d_hidden,
            normed,
            self.second_packed,
        ) = refs
        self.stream, self.keep, self.sems = scratch
        self.work, self.d_packed = work, d_packed
        self.width, self.both = self.stream.shape[1:]
        self.tokens = self.both // 2
        self.mixed, self.active, self.d_hidden = mixed, active, d_hidden
        self.kept = (middle, normed_b, upstream, normed)
        self.flying = {}

    @staticmethod
    def scratch(width, tokens):
        b = jnp.bfloat16
        return [
            pltpu.VMEM((2, width, 2 * tokens), b),
            pltpu.VMEM((4, width, 2 * tokens), b),
            pltpu.SemaphoreType.DMA((32, 2)),
        ]

    def copy(self, key, slot, side, src, dst):
        copy = pltpu.make_async_copy(src, dst, self.sems.at[slot, side])
        copy.start()
        self.flying.setdefault(key, []).append(copy)

    def wait(self, key):
        for copy in self.flying.pop(key, []):
            copy.wait()

    def begin(self):
        self.copy("small", 30, 0, self.small, self.work.small)
        self.fetch(1)
        for index in (0, 2, 1, 3):
            for side in range(2):
                lanes = pl.ds(side * self.tokens, self.tokens)
                self.copy(
                    ("kept", index),
                    20 + index,
                    side,
                    self.kept[index][side],
                    self.keep.at[index, :, lanes],
                )
        self.fetch(2)

    def kind(self, unit):
        array, rows, columns, row, column = self.work.units[unit]
        return array, row // rows, column // columns

    def fetch(self, unit):
        if unit >= len(self.work.units):
            return
        array, row, column = self.kind(unit)
        slot = unit % 2
        for side in range(2):
            lanes = pl.ds(side * self.tokens, self.tokens)
            if array == 1:
                self.copy(unit, unit, side, self.mixed[side], self.stream.at[slot, :, lanes])
            elif array == 3:
                rows = self.work.units[unit][1]
                for rank in range(self.work.dp):
                    pltpu.make_async_copy(
                        self.active[side].at[rank, row],
                        self.stream.at[slot, pl.ds(rank * rows, rows), lanes],
                        self.sems.at[unit, side],
                    ).start()
                all_ranks = pltpu.make_async_copy(
                    self.d_hidden[side].at[pl.ds(0, self.width)],
                    self.stream.at[slot, :, lanes],
                    self.sems.at[unit, side],
                )
                self.flying.setdefault(unit, []).append(all_ranks)
            elif array == 2:
                self.copy(
                    unit,
                    unit,
                    side,
                    self.d_hidden[side].at[pl.ds(column * self.width, self.width)],
                    self.stream.at[slot, :, lanes],
                )
            elif side == 1:
                self.copy(
                    unit,
                    unit,
                    side,
                    self.second_packed.at[pl.ds(column * self.width, self.width)],
                    self.stream.at[slot, :, lanes],
                )

    def make(self, unit):
        work = self.work
        if unit == 0:
            self.wait("small")
            work.start(0)
            return
        array, row, column = self.kind(unit)
        slot = unit % 2
        kept = array - 1
        self.wait(("kept", kept))
        self.wait(unit)
        if array == 4:
            self.stream[slot, :, : self.tokens] = self.d_packed[
                column * self.width : (column + 1) * self.width, :
            ]
        work.free(unit - SLOTS)
        rows = work.units[unit][1]
        ranks = work.dp // 2
        for part in range(2):
            span = slice(part * ranks * rows, (part + 1) * ranks * rows)
            if array in (1, 3):
                product = nt(self.stream[slot, span, :], self.keep[kept])
            else:
                product = nt(self.keep[kept, span, :], self.stream[slot])
            for rank in range(ranks):
                work.terms[(unit - 1) % SLOTS, part * ranks + rank] = product[
                    rank * rows : (rank + 1) * rows, :
                ].astype(jnp.bfloat16)
        work.start(unit)
        self.fetch(unit + 2)


class Pipeline:
    def __init__(self, work, products):
        self.calls = (
            products.make,
            work.chip_sum,
            work.y_sum,
            work.z_sum,
            work.x_sum,
            work.finish,
        )
        self.lags = (0, 1, 2, 2, 2, 1)
        self.done = [0] * len(self.calls)
        self.extra = []

    def tick(self, limit):
        made = self.done[0]
        if made < limit and made - self.done[3] < SLOTS:
            self.calls[0](made)
            self.done[0] += 1
        full = self.done[0] == limit
        for stage in range(1, len(self.calls)):
            now, ahead = self.done[stage], self.done[stage - 1]
            ready = ahead - now > (0 if full else self.lags[stage])
            full = full and ahead == limit
            if ready:
                self.calls[stage](now)
                self.done[stage] += 1

    def run_out(self, limit):
        while self.done[-1] < limit:
            self.tick(limit)
            if self.done[0] == limit and self.extra:
                self.extra.pop(0)()
        for task in self.extra:
            task()


def last_tasks(sources, scratch, d_packed, result):
    weight_s, stream_s, base_s, gain_s, sems = scratch
    weight, stream, base, gain = sources
    width = weight_s.shape[1]
    flying, total = {}, {}

    def fetch(key, source, place, slot):
        flying[key] = pltpu.make_async_copy(source, place, sems.at[slot])
        flying[key].start()

    def fetch_weight(part):
        fetch(part, weight.at[:, pl.ds(part * width, width)], weight_s.at[part % 2], part)

    def begin():
        fetch_weight(0)
        fetch_weight(1)
        fetch("stream", stream, stream_s, 3)
        fetch("base", base, base_s, 4)
        fetch("gain", gain, gain_s, 5)

    def multiply(part):
        flying[part].wait()
        term = nn(weight_s[part % 2], d_packed[part * width : (part + 1) * width, :])
        if part == 0:
            fetch_weight(2)
        total["grad"] = term if part == 0 else total["grad"] + term

    def end():
        for key in ("stream", "base", "gain"):
            flying[key].wait()
        unit, inverse = norm_unit(stream_s[...].T)
        grad = base_s[...] + norm_backward(unit, inverse, column(gain_s[...]), total["grad"])
        stream_s[...] = grad.T
        copy = pltpu.make_async_copy(stream_s, result, sems.at[6])
        copy.start()
        copy.wait()

    return [begin] + [functools.partial(multiply, part) for part in range(3)] + [end]


def causal_mask(size):
    rows = lax.broadcasted_iota(jnp.int32, (size, size), 0)
    columns = lax.broadcasted_iota(jnp.int32, (size, size), 1)
    return rows <= columns


def forward_kernel(seq, dp, sets, units, arrays, heads, *refs):
    refs = list(refs)

    def take(count):
        taken = refs[:count]
        del refs[:count]
        return taken

    (packed,) = take(1)
    earlier = take(sets - 1)
    shards = take(arrays)
    heads_out, mixed_out, own_out, totals_out = take(4)
    wholes = take(arrays)
    arrived, mixed_in, q_s, k_s, v_s, in_send, in_recv, out_send, out_recv = take(9)
    gather = Gather(seq, dp, shards, wholes, units, refs) if units else None

    tokens = packed.shape[1]
    length = tokens * seq
    group = 3 * HEAD_DIM
    me = lax.axis_index("seq")
    peers = seq_peers(seq)
    greet([{"seq": peer} for peer in peers] + (gather.peers() if units else []))

    own_lanes = pl.ds(pl.multiple_of(me * tokens, tokens), tokens)
    copies = {}
    for h in range(heads):
        for d, peer in enumerate(peers):
            copy = remote(
                packed.at[pl.ds(pl.multiple_of((peer * heads + h) * group, group), group)],
                arrived.at[pl.ds(h * group, group), own_lanes],
                in_send.at[h, d],
                in_recv.at[h, d],
                {"seq": peer},
            )
            copy.start()
            copies[h, d] = copy
    steps = []
    if units:
        for unit in range(len(units)):
            gather.start(unit)
        gather.keep_own()
        steps = gather.steps()
        steps.pop(0)()
    for h in range(heads):
        arrived[h * group : (h + 1) * group, own_lanes] = packed[
            pl.ds(pl.multiple_of((me * heads + h) * group, group), group), :
        ]

    mask = causal_mask(tokens)
    for s in range(sets):
        v_s[s, HEAD_DIM:] = jnp.ones((16, length), jnp.bfloat16)
    results = []
    for h in range(heads):
        c0 = h * group
        for s in range(sets):
            source = earlier[s] if s < sets - 1 else arrived
            if s == sets - 1:
                for d in range(seq - 1):
                    copies[h, d].wait_recv()
                heads_out[c0 : c0 + group, :] = arrived[c0 : c0 + group, :]
                q_s[...] = arrived[c0 : c0 + HEAD_DIM, :] * jnp.bfloat16(HEAD_DIM**-0.5)
            k_s[s] = source[c0 + HEAD_DIM : c0 + 2 * HEAD_DIM, :].T
            v_s[s, :HEAD_DIM] = source[c0 + 2 * HEAD_DIM : c0 + 3 * HEAD_DIM, :]

        for i in range(seq):
            queries = q_s[:, i * tokens : (i + 1) * tokens]
            peak = total = None
            for j in [i] + list(range(i)):
                keys = slice(j * tokens, (j + 1) * tokens)
                scores = []
                for s in range(sets):
                    block = nn(k_s[s, keys, :], queries)
                    if j == i:
                        block = jnp.where(mask, block, -1e30)
                    scores.append(block)
                peak_now = peak
                for block in scores:
                    top = jnp.max(block, axis=0, keepdims=True)
                    peak_now = top if peak_now is None else jnp.maximum(peak_now, top)
                if total is not None:
                    total = total * jnp.exp(peak - peak_now)
                for s, block in enumerate(scores):
                    weights = jnp.exp(block - peak_now).astype(jnp.bfloat16)
                    part = nn(v_s[s, :, keys], weights)
                    total = part if total is None else total + part
                peak = peak_now
            row_sum = total[HEAD_DIM : HEAD_DIM + 1]
            own_out[h * HEAD_DIM : (h + 1) * HEAD_DIM, i * tokens : (i + 1) * tokens] = (
                total[:HEAD_DIM] / row_sum
            ).astype(jnp.bfloat16)
            totals_out[h, :, i * tokens : (i + 1) * tokens] = peak + jnp.log(row_sum)
            if steps:
                steps.pop(0)()

        mine = pl.ds(pl.multiple_of((me * heads + h) * HEAD_DIM, HEAD_DIM), HEAD_DIM)
        for d, peer in enumerate(peers):
            copy = remote(
                own_out.at[
                    pl.ds(h * HEAD_DIM, HEAD_DIM),
                    pl.ds(pl.multiple_of(peer * tokens, tokens), tokens),
                ],
                mixed_in.at[mine],
                out_send.at[h, d],
                out_recv.at[h, d],
                {"seq": peer},
            )
            copy.start()
            results.append(copy)
        mixed_in[mine] = own_out[h * HEAD_DIM : (h + 1) * HEAD_DIM, own_lanes]
    for step in steps:
        step()
    if units:
        gather.finish()
    for copy in copies.values():
        copy.wait_send()
    for copy in results:
        copy.wait()
    mixed_out[...] = mixed_in[...]


def attend_forward(seq, dp, heads, packed, earlier, shards, call_id):
    width, tokens = packed.shape
    length = tokens * seq
    sets, arrays = 1 + len(earlier), len(shards)
    units = later_units(shards) if arrays else []
    rows = heads * 3 * HEAD_DIM
    vmem = pl.BlockSpec(memory_space=pltpu.VMEM)
    hbm = pl.BlockSpec(memory_space=pl.ANY)
    dma = pltpu.SemaphoreType.DMA
    outs = pl.pallas_call(
        functools.partial(forward_kernel, seq, dp, sets, units, arrays, heads),
        out_shape=(
            jax.ShapeDtypeStruct((rows, length), jnp.bfloat16),
            jax.ShapeDtypeStruct((width // 3, tokens), jnp.bfloat16),
            jax.ShapeDtypeStruct((heads * HEAD_DIM, length), jnp.bfloat16),
            jax.ShapeDtypeStruct((heads, 1, length), jnp.float32),
        )
        + tuple(whole_shape(shard, dp) for shard in shards),
        in_specs=[vmem] * sets + [hbm] * arrays,
        out_specs=(vmem,) * 4 + (hbm,) * arrays,
        scratch_shapes=[
            pltpu.VMEM((rows, length), jnp.bfloat16),
            pltpu.VMEM((width // 3, tokens), jnp.bfloat16),
            pltpu.VMEM((HEAD_DIM, length), jnp.bfloat16),
            pltpu.VMEM((sets, length, HEAD_DIM), jnp.bfloat16),
            pltpu.VMEM((sets, HEAD_DIM + 16, length), jnp.bfloat16),
            dma((heads, seq)),
            dma((heads, seq)),
            dma((heads, seq)),
            dma((heads, seq)),
        ]
        + (Gather.scratch(arrays, len(units), dp) if units else []),
        compiler_params=pltpu.CompilerParams(
            collective_id=call_id, has_side_effects=True, vmem_limit_bytes=40 << 20
        ),
        name=f"attend_forward_{sets}",
    )(packed, *earlier, *shards)
    return outs[:4], outs[4:]


def backward_kernel(seq, dp, sets, units, heads, *refs):
    refs = list(refs)

    def take(count):
        taken = refs[:count]
        del refs[:count]
        return taken

    (d_mixed,) = take(1)
    packs = take(sets)
    own_in, totals_in = take(2)
    if units:
        (carry_in, small) = take(2)
        pairs = [take(2) for _ in range(7)]
        (second_packed,) = take(1)
        last_in = take(4)
    (d_packed_out,) = take(1)
    carry_out = None if units else take(1)[0]
    grads_out = take(5) if units else []
    arrived, local_grad, d_packed_in, q_s, k_s, kt_s, v_s, delta_s, dq_s, dkv_s = take(10)
    in_send, in_recv, out_send, out_recv, out_sem = take(5)
    if units:
        carry_s, carry_sem = take(2)
        product_scratch = take(3)
        last_s = take(5)
        work = Scatter(seq, dp, units, grads_out, refs)
        products = Products([small] + pairs + [second_packed], product_scratch, work, d_packed_in)

    tokens = d_mixed.shape[1]
    length = tokens * seq
    group = 3 * HEAD_DIM
    me = lax.axis_index("seq")
    peers = seq_peers(seq)
    greet([{"seq": peer} for peer in peers] + (work.peers() if units else []))
    own_lanes = pl.ds(pl.multiple_of(me * tokens, tokens), tokens)
    scale = jnp.bfloat16(HEAD_DIM**-0.5)

    copies = {}
    for h in range(heads):
        for d, peer in enumerate(peers):
            copy = remote(
                d_mixed.at[pl.ds(pl.multiple_of((peer * heads + h) * HEAD_DIM, HEAD_DIM), HEAD_DIM)],
                arrived.at[pl.ds(h * HEAD_DIM, HEAD_DIM), own_lanes],
                in_send.at[h, d],
                in_recv.at[h, d],
                {"seq": peer},
            )
            copy.start()
            copies[h, d] = copy
    if units:
        products.begin()
        pipeline = Pipeline(work, products)
        early = [unit[0] for unit in units].index(4)
    for h in range(heads):
        arrived[h * HEAD_DIM : (h + 1) * HEAD_DIM, own_lanes] = d_mixed[
            pl.ds(pl.multiple_of((me * heads + h) * HEAD_DIM, HEAD_DIM), HEAD_DIM), :
        ]

    def outgoing(h, rank, send_slot):
        return remote(
            local_grad.at[
                pl.ds(h * group, group), pl.ds(pl.multiple_of(rank * tokens, tokens), tokens)
            ],
            d_packed_in.at[pl.ds(pl.multiple_of((me * heads + h) * group, group), group)],
            out_send.at[h, send_slot],
            out_recv.at[h, me],
            {"seq": rank},
        )

    if units:
        for _ in range(AHEAD):
            pipeline.tick(early)
    mask = causal_mask(tokens)
    hook = 0
    for h in range(heads):
        c0 = h * group
        r0 = h * HEAD_DIM
        if units:
            carried = pltpu.make_async_copy(carry_in.at[h], carry_s, carry_sem.at[h])
            carried.start()
        q_s[...] = packs[-1][c0 : c0 + HEAD_DIM, :] * scale
        for s in range(sets):
            keys = packs[s][c0 + HEAD_DIM : c0 + 2 * HEAD_DIM, :]
            k_s[s] = keys.T
            kt_s[s] = keys * scale
            v_s[s] = packs[s][c0 + 2 * HEAD_DIM : c0 + 3 * HEAD_DIM, :].T
        for d in range(seq - 1):
            copies[h, d].wait_recv()
        delta_s[...] = jnp.sum(
            arrived[r0 : r0 + HEAD_DIM, :].astype(jnp.float32)
            * own_in[r0 : r0 + HEAD_DIM, :].astype(jnp.float32),
            axis=0,
            keepdims=True,
        )
        if units:
            carried.wait()
        for j in range(seq):
            keys = slice(j * tokens, (j + 1) * tokens)
            for i in range(j, seq):
                span = slice(i * tokens, (i + 1) * tokens)
                queries = q_s[:, span]
                grads = arrived[r0 : r0 + HEAD_DIM, span]
                d_query = dq_s[:, span] if j > 0 else None
                for s in range(sets):
                    chances = jnp.exp(nn(k_s[s, keys, :], queries) - totals_in[h, :, span])
                    if i == j:
                        chances = jnp.where(mask, chances, 0.0)
                    d_chance = nn(v_s[s, keys, :], grads)
                    d_score = (chances * (d_chance - delta_s[:, span])).astype(jnp.bfloat16)
                    d_key = nt(queries, d_score)
                    d_value = nt(grads, chances.astype(jnp.bfloat16))
                    if i == j:
                        if units:
                            d_key = d_key + carry_s[:HEAD_DIM, keys]
                            d_value = d_value + carry_s[HEAD_DIM:, keys]
                        dkv_s[s, :HEAD_DIM, keys] = d_key
                        dkv_s[s, HEAD_DIM:, keys] = d_value
                    else:
                        dkv_s[s, :HEAD_DIM, keys] += d_key
                        dkv_s[s, HEAD_DIM:, keys] += d_value
                    part = nn(kt_s[s, :, keys], d_score)
                    d_query = part if d_query is None else d_query + part
                dq_s[:, span] = d_query
                hook += 1
                if units and hook % EVERY == 0 and hook < heads * seq * (seq + 1) // 2:
                    pipeline.tick(early)
            local_grad[c0 : c0 + HEAD_DIM, keys] = dq_s[:, keys].astype(jnp.bfloat16)
            local_grad[c0 + HEAD_DIM : c0 + group, keys] = dkv_s[sets - 1, :, keys].astype(
                jnp.bfloat16
            )
            if h == heads - 1:

                @pl.when(me != j)
                def _():
                    outgoing(h, jnp.int32(j), j).start()

        if not units:
            carry_out[h] = dkv_s[0]
        if h < heads - 1:
            for d, peer in enumerate(peers):
                outgoing(h, peer, d).start()
        d_packed_in[pl.ds(pl.multiple_of((me * heads + h) * group, group), group)] = local_grad[
            c0 : c0 + group, own_lanes
        ]
    if units:
        pipeline.tick(early)
    for h in range(heads):
        for peer in peers:
            remote(
                local_grad.at[pl.ds(h * group, group), own_lanes],
                d_packed_in.at[pl.ds(pl.multiple_of((peer * heads + h) * group, group), group)],
                out_send.at[h, 0],
                out_recv.at[h, peer],
                {"seq": peer},
            ).wait_recv()
    if units:
        pipeline.extra = last_tasks(last_in, last_s, d_packed_in, d_packed_out)
        pipeline.run_out(len(units))
        work.drain()
    else:
        finished = pltpu.make_async_copy(d_packed_in, d_packed_out, out_sem.at[0])
        finished.start()
    for copy in copies.values():
        copy.wait_send()
    for h in range(heads - 1):
        for d, peer in enumerate(peers):
            outgoing(h, peer, d).wait_send()
    for j in range(seq):

        @pl.when(me != j)
        def _():
            outgoing(heads - 1, jnp.int32(j), j).wait_send()

    if not units:
        finished.wait()


def attend_backward(seq, dp, heads, d_mixed, packs, own, totals, extra, units, call_id):
    width, tokens = d_mixed.shape
    length = tokens * seq
    sets = len(packs)
    rows = heads * 3 * HEAD_DIM
    vmem = pl.BlockSpec(memory_space=pltpu.VMEM)
    hbm = pl.BlockSpec(memory_space=pl.ANY)
    dma = pltpu.SemaphoreType.DMA
    f32 = jnp.float32
    out_shape = [jax.ShapeDtypeStruct((3 * width, tokens), jnp.bfloat16)]
    if units:
        out_shape = [jax.ShapeDtypeStruct((tokens, width), f32)]
    out_specs = [hbm]
    more = []
    if units:
        heights = [0] * 5
        for array, high, wide, row, column in units:
            heights[array] = max(heights[array], row + high)
        widths = [0] * 5
        for array, high, wide, row, column in units:
            widths[array] = max(widths[array], column + wide)
        out_shape += [jax.ShapeDtypeStruct(shape, f32) for shape in zip(heights, widths)]
        out_specs += [hbm] * 5
        more = [pltpu.VMEM((2 * HEAD_DIM, length), f32), dma((heads,))]
        more += Products.scratch(width, tokens)
        more += [
            pltpu.VMEM((2, width, width), jnp.bfloat16),
            pltpu.VMEM((tokens, width), f32),
            pltpu.VMEM((width, tokens), f32),
            pltpu.VMEM((1, width), f32),
            dma((8,)),
        ]
        more += Scatter.scratch(seq, dp, units)
    else:
        out_shape.append(jax.ShapeDtypeStruct((heads, 2 * HEAD_DIM, length), f32))
        out_specs.append(vmem)
    return pl.pallas_call(
        functools.partial(backward_kernel, seq, dp, sets, units, heads),
        out_shape=tuple(out_shape),
        in_specs=[vmem] * (3 + sets) + [hbm] * len(extra),
        out_specs=tuple(out_specs),
        scratch_shapes=[
            pltpu.VMEM((heads * HEAD_DIM, length), jnp.bfloat16),
            pltpu.VMEM((rows, length), jnp.bfloat16),
            pltpu.VMEM((3 * width, tokens), jnp.bfloat16),
            pltpu.VMEM((HEAD_DIM, length), jnp.bfloat16),
            pltpu.VMEM((sets, length, HEAD_DIM), jnp.bfloat16),
            pltpu.VMEM((sets, HEAD_DIM, length), jnp.bfloat16),
            pltpu.VMEM((sets, length, HEAD_DIM), jnp.bfloat16),
            pltpu.VMEM((1, length), f32),
            pltpu.VMEM((HEAD_DIM, length), f32),
            pltpu.VMEM((sets, 2 * HEAD_DIM, length), f32),
            dma((heads, seq)),
            dma((heads, seq)),
            dma((heads, seq)),
            dma((heads, seq)),
            dma((1,)),
        ]
        + more,
        compiler_params=pltpu.CompilerParams(
            collective_id=call_id, has_side_effects=True, vmem_limit_bytes=60 << 20
        ),
        name=f"attend_backward_{sets}",
    )(d_mixed, *packs, own, totals, *extra)


def column(row):
    return jnp.broadcast_to(row, (8, row.shape[1])).T[:, :1]


def norm_unit(rows):
    centre = rows - jnp.mean(rows, axis=0, keepdims=True)
    inverse = lax.rsqrt(jnp.mean(centre * centre, axis=0, keepdims=True) + epsilon)
    return centre * inverse, inverse


def norm_backward(unit, inverse, gain, grad):
    grad = grad * gain
    share = jnp.mean(grad * unit, axis=0, keepdims=True)
    return inverse * (grad - jnp.mean(grad, axis=0, keepdims=True) - unit * share)


def gelu_slope(hidden):
    root = (2.0 / math.pi) ** 0.5
    square = hidden * hidden
    bend = jnp.tanh(root * hidden * (1.0 + 0.044715 * square))
    inner = (0.5 * root) * hidden * (1.0 + 3 * 0.044715 * square)
    return 0.5 * (1.0 + bend) + inner * (1.0 - bend * bend)


def dense_kernel(first, chunks, *refs):
    refs = list(refs)

    def take(count):
        taken = refs[:count]
        del refs[:count]
        return taken

    count = 5 * first + (1 - first) + 6 + first
    sources = take(count)
    results = take(5 + first * 4)
    places = take(count)
    sems, out_sems = take(2)
    base = 5 * first + (1 - first)
    middle, hidden, down_w, up_w, out_w, gain = range(base, base + 6)
    width = places[middle].shape[1]

    def span(part):
        return pl.ds(part * width, width)

    order = [(0, None)]
    if first:
        order = [(index, part) for part in range(3) for index in (1, 0)] + [(2, None), (4, None), (3, None)]
    for part in range(chunks):
        order += [(down_w, part), (hidden, part), (up_w, part)]
    order += [(middle, None), (gain, None), (out_w, None)] + [(base + 6, None)] * first
    by_columns = (up_w, 1) if first else (up_w,)
    fetched = {}
    for index, part in order:
        source, place = sources[index], places[index]
        if part is not None:
            where = (slice(None), span(part)) if index in by_columns else (span(part),)
            source, place = source.at[where], place.at[where]
        copy = pltpu.make_async_copy(source, place, sems.at[index, part or 0])
        copy.start()
        fetched[index, part] = copy

    def get(index, part=None):
        fetched[index, part].wait()
        return places[index]

    sent = []

    def put(place, result):
        copy = pltpu.make_async_copy(place, result, out_sems.at[len(sent)])
        copy.start()
        sent.append(copy)

    if first:
        grad = None
        for part in range(3):
            term = nn(get(1, part)[:, span(part)], get(0, part)[span(part), :])
            grad = term if grad is None else grad + term
        unit, inverse = norm_unit(get(2)[...].T)
        gain_a = column(get(4)[...])
        upstream = get(3)[...] + norm_backward(unit, inverse, gain_a, grad)
    else:
        upstream = get(0)[...].astype(jnp.float32)
    hidden_s, grad_s, middle_s, mixed_s, normed_s, up_s, rounded_s = refs[:7]
    up_s[...] = upstream
    rounded_s[...] = upstream.astype(jnp.bfloat16)
    if first:
        first_s, second_s = refs[7:]
        rounded_out, sum_out, first_out, second_out = results[5:]
        put(rounded_s, rounded_out)
        sum_out[...] = jnp.sum(upstream, axis=1, keepdims=True)
        second_s[...] = (unit * gain_a).astype(jnp.bfloat16)
        put(second_s, second_out)
    total = None
    for part in range(chunks):
        d_active = nn(get(down_w, part)[span(part), :], rounded_s[...])
        slope = gelu_slope(get(hidden, part)[span(part), :])
        hidden_s[span(part), :] = (d_active * slope).astype(jnp.bfloat16)
        put(hidden_s.at[span(part)], results[0].at[span(part)])
        term = nn(get(up_w, part)[:, span(part)], hidden_s[span(part), :])
        total = term if total is None else total + term
    unit, inverse = norm_unit(get(middle)[...].T)
    gain_b = column(get(gain)[...])
    d_middle = up_s[...] + norm_backward(unit, inverse, gain_b, total)
    grad_s[...] = d_middle
    middle_s[...] = d_middle.astype(jnp.bfloat16)
    normed_s[...] = (unit * gain_b).astype(jnp.bfloat16)
    put(grad_s, results[1])
    put(middle_s, results[2])
    put(normed_s, results[4])
    mixed_s[...] = nn(get(out_w)[...], middle_s[...]).astype(jnp.bfloat16)
    put(mixed_s, results[3])
    if first:
        first_s[...] = (norm_unit(get(base + 6)[...].T)[0] * gain_a).astype(jnp.bfloat16)
        put(first_s, first_out)
    for copy in sent:
        copy.wait()


def dense_backward(before, after):
    first = int(len(before) > 1)
    args = list(before) + list(after)
    width, tokens = (before[3] if first else before[0]).shape
    hbm = pl.BlockSpec(memory_space=pl.ANY)
    b, f32 = jnp.bfloat16, jnp.float32
    ff = after[1].shape[0]
    flat = (width, tokens)
    shapes = [((ff, tokens), b), (flat, f32), (flat, b), (flat, b), (flat, b)]
    more = [pltpu.VMEM(shape, kind) for shape, kind in shapes]
    more += [pltpu.VMEM(flat, f32), pltpu.VMEM(flat, b)]
    outs = [jax.ShapeDtypeStruct(shape, kind) for shape, kind in shapes]
    specs = [hbm] * 5
    if first:
        more += [pltpu.VMEM(flat, b)] * 2
        outs += [jax.ShapeDtypeStruct(flat, b), jax.ShapeDtypeStruct((width, 1), f32)]
        outs += [jax.ShapeDtypeStruct(flat, b)] * 2
        specs += [hbm, pl.BlockSpec(memory_space=pltpu.VMEM), hbm, hbm]
    flops = 2 * tokens * width * (2 * ff + width + 3 * width * first)
    return pl.pallas_call(
        functools.partial(dense_kernel, first, ff // width),
        out_shape=tuple(outs),
        in_specs=[hbm] * len(args),
        out_specs=tuple(specs),
        scratch_shapes=[pltpu.VMEM(arg.shape, arg.dtype) for arg in args]
        + [
            pltpu.SemaphoreType.DMA((len(args), max(3, ff // width))),
            pltpu.SemaphoreType.DMA((16,)),
        ]
        + more,
        compiler_params=pltpu.CompilerParams(vmem_limit_bytes=58 << 20),
        cost_estimate=pl.CostEstimate(flops=flops, bytes_accessed=24 << 20, transcendentals=0),
        name=f"dense_backward_{first}",
    )(*args)


def dots(left, right, left_side, right_side):
    return lax.dot_general(
        left,
        right,
        (((left_side,), (right_side,)), ((), ())),
        preferred_element_type=jnp.float32,
    )


def norm_rows(rows, gain):
    centre = rows - jnp.mean(rows, axis=1, keepdims=True)
    spread = jnp.mean(centre * centre, axis=1, keepdims=True)
    return (centre * lax.rsqrt(spread + epsilon) * gain).astype(jnp.bfloat16)


def block_forward(sizes, call_id, stream, qkv_w, gains, earlier, weights, shards):
    seq, dp, heads = sizes
    normed = norm_rows(stream, gains[0])
    packed = dots(qkv_w, normed, 0, 1).astype(jnp.bfloat16)
    (head_rows, mixed, own, totals), gathered = attend_forward(
        seq, dp, heads, packed, earlier, shards, call_id
    )
    out_w, up_w, down_w = weights or gathered
    middle = stream + dots(mixed, out_w, 0, 0)
    normed_b = norm_rows(middle, gains[1])
    hidden = dots(up_w, normed_b, 0, 1)
    active = jax.nn.gelu(hidden, approximate=True).astype(jnp.bfloat16)
    result = middle + dots(active, down_w, 0, 0)
    packs = earlier + [head_rows]
    stored = (stream, packs, own, totals, mixed, middle, hidden, active)
    return result, stored, (out_w, up_w, down_w)


def block_backward(sizes, call_id, before, stored, gains, weights, second):
    seq, dp, heads = sizes
    out_w, up_w, down_w = weights
    stream, packs, own, totals, mixed, middle, hidden, active = stored
    after = (middle, hidden, down_w, up_w, out_w, gains[1])
    done = dense_backward(before, after if second is None else after + (stream,))
    d_hidden, d_middle, middle_bf, d_mixed, normed_b = done[:5]
    width, tokens = d_mixed.shape
    rows = width // dp
    active = active.reshape(dp, active.shape[0] // width, rows, tokens)
    upstream = before[0] if second is None else done[5]
    factors = [mixed, middle_bf, active, upstream, normed_b, d_hidden]
    extra, units = [], []
    if second is not None:
        passed, second_factors, second_packed = second
        embed = done[6].astype(jnp.bfloat16).reshape(dp, 1, rows)
        factors, second_factors = factors + [done[7]], second_factors + [done[8]]
        extra = [passed, jnp.pad(embed, ((0, 0), (0, 7), (0, 256 - rows)))]
        for pair in zip(factors, second_factors):
            extra += pair
        extra += [second_packed, before[1], stream, d_middle, before[4]]
        ff = d_hidden.shape[0]
        units = [(0, 8, 256, 0, 0)]
        units += [(1, rows, width, 0, 0)]
        units += [(3, rows, width, row, 0) for row in range(0, ff // dp, rows)]
        units += [(2, rows, width, 0, column) for column in range(0, ff, width)]
        units += [(4, rows, width, 0, column) for column in range(0, 3 * width, width)]
    outs = attend_backward(seq, dp, heads, d_mixed, packs, own, totals, extra, units, call_id)
    return (stream, d_middle), factors, outs


def local(
    seq,
    dp,
    tokens,
    qkv_weight,
    out_weight,
    up_weight,
    down_weight,
    norm_gain,
    mlp_gain,
    pass_embed,
    cotangent,
):
    share = norm_gain.shape[0]
    lanes = [
        jnp.pad(v.reshape(1, share), ((0, 0), (0, 128 - share)))
        for v in (norm_gain, pass_embed, mlp_gain)
    ]
    small = jnp.concatenate(
        [
            jnp.concatenate(lanes[:2], axis=1),
            jnp.pad(lanes[2], ((0, 0), (0, 128))),
            jnp.zeros((6, 256), jnp.bfloat16),
        ]
    )
    qkv_w, small = gather_now(seq, dp, [qkv_weight, small])
    small = small.reshape(dp, 8, 256)
    gains = [small[:, row, :share].reshape(1, -1).astype(jnp.float32) for row in (0, 1)]
    embedding = small[:, 0, 128 : 128 + share].reshape(1, -1).astype(jnp.float32)
    heads = qkv_weight.shape[1] // (3 * HEAD_DIM * seq)
    sizes = (seq, dp, heads)
    first_out, first_kept, weights = block_forward(
        sizes,
        1,
        tokens[0].astype(jnp.float32),
        qkv_w,
        gains,
        [],
        None,
        [out_weight, up_weight, down_weight],
    )
    second_out, second_kept, weights = block_forward(
        sizes, 2, first_out + embedding, qkv_w, gains, [first_kept[1][0]], weights, []
    )
    (stream, d_middle), factors, outs = block_backward(
        sizes, 3, (cotangent[0].T,), second_kept, gains, weights, None
    )
    second = (outs[1], factors, outs[0])
    before = (outs[0], qkv_w, stream, d_middle, gains[0])
    _, _, outs = block_backward(sizes, 4, before, first_kept, gains, weights, second)
    d_first, small, out_grad, up_grad, down_grad, qkv_grad = outs
    f32 = jnp.float32
    gain_a = jnp.sum(qkv_weight.astype(f32) * qkv_grad, axis=1) / norm_gain.astype(f32)
    gain_b = jnp.sum(up_weight.astype(f32) * up_grad, axis=1) / mlp_gain.astype(f32)
    return (
        second_out.astype(jnp.bfloat16)[None],
        d_first[None],
        qkv_grad,
        out_grad,
        up_grad,
        down_grad,
        gain_a,
        gain_b,
        small[0, :share],
    )


def solution(mesh):
    in_specs = (
        P("dp", "seq", None),
        P("dp", None),
        P("dp", None),
        P("dp", None),
        P("dp", None),
        P("dp"),
        P("dp"),
        P("dp"),
        P("dp", "seq", None),
    )
    out_specs = (
        P("dp", "seq", None),
        P("dp", "seq", None),
        P("dp", None),
        P("dp", None),
        P("dp", None),
        P("dp", None),
        P("dp"),
        P("dp"),
        P("dp"),
    )
    return jax.shard_map(
        functools.partial(local, mesh.shape["seq"], mesh.shape["dp"]), mesh=mesh, in_specs=in_specs, out_specs=out_specs, check_vma=False)
```
